32 devices in a mesh: ctx: 8 (over z, y), mp: 4 (over x, core).
Axes of the slice: x: 2, y: 2, z: 4, core: 2. Of those that a mesh axis runs over, the one named last changes fastest.
Arguments:
- query: bfloat16 [32, 8, 8, 128], P(('ctx', 'mp')), may hold values from -8 to 8
- keys: bfloat16 [32, 8, 2048, 128], P(('ctx', 'mp')), may hold values from -5 to 5
- values: bfloat16 [32, 8, 2048, 128], P(('ctx', 'mp')), may hold values from -6 to 6
- chosen: int32 [8, 32, 16], replicated, may hold values from 0 to 31, all different within a row; in each aligned block of 32 rows (0 to 31, 32 to 63, ..., all dimensions but the last counted through in order) at most 32 rows name the same one
- residual: bfloat16 [32, 8192], P('ctx', 'mp'), may hold values from -1.5 to 1.5
- output_weight: bfloat16 [8192, 8192], P('ctx', 'mp'), may hold values from -0.0625 to 0.0625
- norm_gain: float32 [8192], P('mp'), may hold values from 0.5 to 1.5
- gate_weight: bfloat16 [8192, 14336], P('mp', 'ctx'), may hold values from -0.0625 to 0.0625
- up_weight: bfloat16 [8192, 14336], P('mp', 'ctx'), may hold values from -0.0625 to 0.0625
- down_weight: bfloat16 [14336, 8192], P('ctx', 'mp'), may hold values from -0.046875 to 0.046875
Outputs:
- stream: bfloat16 [32, 8192], P('ctx', 'mp')
- update: bfloat16 [32, 8192], P('ctx', 'mp')
The draws below stay inside these ranges and needn't reach their ends.
Inputs may be any that keep to these rules, and one draw needn't show every extreme that they name: `chosen`: for each KV head, each row lists 16 different partitions; no partition is listed by more than 32 rows of one KV head, and in every draw some partition is listed by exactly 32 rows of some KV head.
All inputs are finite; a program needn't handle non-finite values.
Results may differ from the reference program's by a relative error of at most 0.025.
Values may be sent and summed in bfloat16 or wider, within the bound.
No kernel may reach another device: no remote copies, remote signals or barrier semaphores. Data moves between devices by JAX's collectives and lax.ppermute only.
A program may use at most 128 MiB of HBM per device.

```python
import math
import jax
import jax.numpy as jnp
import numpy as np
from jax import lax

MODEL_WIDTH = 8192
KEY_HEADS = 8
QUERY_PER_KEY = 8
HEAD_WIDTH = 128
FF = 14336
PARTITION_KEYS = 2048
KEPT_PARTITIONS = 16
DECODED_COUNT = 32
PARTITION_COUNT = 32
ROW_LIMIT = 32


def draw_keys(key, part):
    array_shape = (PARTITION_COUNT, KEY_HEADS, PARTITION_KEYS, HEAD_WIDTH)
    base = jnp.clip(jax.random.normal(jax.random.fold_in(key, 21), array_shape, jnp.float32), -5.0, 5.0)
    return base.astype(jnp.bfloat16)


def draw_query(key, part):
    array_shape = (DECODED_COUNT, KEY_HEADS, QUERY_PER_KEY, HEAD_WIDTH)
    base = jnp.clip(2.7 * jax.random.normal(jax.random.fold_in(key, 31), array_shape, jnp.float32), -8.0, 8.0)
    return base.astype(jnp.bfloat16)


def draw_residual(key, part):
    row_scale = 10.0 ** jax.random.uniform(jax.random.fold_in(key, 41), (DECODED_COUNT, 1), jnp.float32, -0.5, 0.5)
    column_rise = 3.0 ** (jnp.arange(MODEL_WIDTH, dtype=jnp.float32) / MODEL_WIDTH - 0.5)
    column_scale = column_rise * 10.0 ** jax.random.uniform(jax.random.fold_in(key, 42), (MODEL_WIDTH,), jnp.float32, -0.5, 0.5)
    base = jax.random.normal(jax.random.fold_in(key, 43), (DECODED_COUNT, MODEL_WIDTH), jnp.float32)
    return jnp.clip(0.15 * base * row_scale * column_scale[None, :], -1.5, 1.5).astype(jnp.bfloat16)


def block_scale(stream_key, shape, pieces, low, high):
    gain = 1.0
    for dim, blocks in pieces:
        steps = jax.random.uniform(jax.random.fold_in(jax.random.fold_in(stream_key, 6), dim), (blocks,), jnp.float32, low / len(pieces), high / len(pieces))
        gain = gain * jnp.repeat(jnp.exp(steps), shape[dim] // blocks).reshape((-1,) + (1,) * (len(shape) - 1 - dim))
    return gain


def routed_block(key, own, number, rows, number_of, top, reach, skew):
    ranking = jax.random.permutation(key, number_of)
    packed, common = load_shares(number_of, rows * top, reach, skew, True), load_shares(number_of, rows * top, reach, skew, False)
    places = jnp.arange(number_of)

    def named(lengths, turn):
        used = int((lengths > 0).sum())
        fixed = max(1, used // 4)
        shifted = fixed + (places - fixed + turn * (used - fixed)) % max(1, number_of - fixed)
        return jnp.zeros((number_of,), jnp.int32).at[ranking[jnp.where(places < fixed, places, shifted)]].set(jnp.asarray(lengths, jnp.int32))

    lengths = jnp.where(number % 4 == 0, named(packed, number // 4), named(common, number - number // 4 - 1))
    mixed = jax.random.permutation(jax.random.fold_in(own, 3), number_of)
    giver, taker = mixed[0:number_of // 2 * 2:2], mixed[1:number_of // 2 * 2:2]
    room = jnp.minimum(lengths[giver] - 1, reach - lengths[taker]) // 2
    room = jnp.where((giver == ranking[0]) | (taker == ranking[0]) | (lengths[taker] == 0), 0, jnp.maximum(room, 0))
    shifted = jax.random.randint(jax.random.fold_in(own, 4), (number_of // 2,), 0, 1 << 20) % (room + 1)
    lengths = lengths.at[giver].add(-shifted).at[taker].add(shifted)
    members = jnp.searchsorted(jnp.cumsum(lengths), jnp.arange(rows * top), side="right").astype(jnp.int32)
    grid = members.reshape(top, rows).T
    grid = grid[jax.random.permutation(jax.random.fold_in(own, 1), rows)]
    turn = jax.random.randint(jax.random.fold_in(own, 2), (rows, 1), 0, top)
    return jnp.take_along_axis(grid, (jnp.arange(top)[None, :] + turn) % top, axis=1)


def load_shares(count, total, reach, lean, full):
    portions = [(1 << 20) // math.isqrt(rank ** lean) + 1 for rank in range(1, count + 1)]
    largest = reach if full else min(reach, max(-(-total // count), total * portions[0] // sum(portions)))
    least = 1 if total - largest >= count - 1 else 0
    holding, surplus = [largest] + [least] * (count - 1), total - largest - least * (count - 1)
    while surplus > 0:
        free = [i for i in range(1, count) if holding[i] < largest] or [i for i in range(1, count) if holding[i] < reach]
        whole, budget = sum([portions[i] for i in free]), surplus
        for i in free:
            addition = min(reach - holding[i], max(1, budget * portions[i] // whole), surplus)
            holding[i] = holding[i] + addition
            surplus = surplus - addition
    return np.array(holding)


def scatter_about(stream_key, shape, width, reach, shards=(), held_as=jnp.bfloat16):
    array = width * jax.random.normal(stream_key, shape, jnp.float32)
    if shards:
        array = array * block_scale(stream_key, shape, shards, -0.22, 0.18)
    return jnp.clip(array, -reach, reach).astype(held_as)


def setup_inputs(seed: int = 0) -> dict:
    arg_keys = jax.random.split(jax.random.key(seed), 11)
    query = draw_query(jax.random.fold_in(arg_keys[10], 71), 0)
    keys = draw_keys(jax.random.fold_in(arg_keys[10], 71), 0)
    values = scatter_about(arg_keys[2], (PARTITION_COUNT, KEY_HEADS, PARTITION_KEYS, HEAD_WIDTH), 1.0, 6.0, ((0, 32),))
    chosen_keys = jax.random.split(jax.random.fold_in(arg_keys[3], 1), KEY_HEADS * DECODED_COUNT // DECODED_COUNT)
    chosen_turns = jax.random.permutation(jax.random.fold_in(arg_keys[3], 3), KEY_HEADS * DECODED_COUNT // DECODED_COUNT)
    chosen = jax.vmap(lambda own, number: routed_block(jax.random.fold_in(arg_keys[3], 2), own, number, DECODED_COUNT, PARTITION_COUNT, KEPT_PARTITIONS, ROW_LIMIT, 2))(chosen_keys, chosen_turns).reshape((KEY_HEADS, DECODED_COUNT, KEPT_PARTITIONS))
    residual = draw_residual(jax.random.fold_in(arg_keys[10], 71), 0)
    output_weight = scatter_about(arg_keys[5], (KEY_HEADS * QUERY_PER_KEY * HEAD_WIDTH, MODEL_WIDTH), (KEY_HEADS * QUERY_PER_KEY * HEAD_WIDTH) ** -0.5, 0.0625, ((0, 8), (1, 4)))
    norm_gain = jnp.clip(1.0 + 0.1 * jax.random.normal(arg_keys[6], (MODEL_WIDTH,), jnp.float32), 0.5, 1.5)
    gate_weight = scatter_about(arg_keys[7], (MODEL_WIDTH, FF), MODEL_WIDTH ** -0.5, 0.0625, ((0, 4), (1, 8)))
    up_weight = scatter_about(arg_keys[8], (MODEL_WIDTH, FF), MODEL_WIDTH ** -0.5, 0.0625, ((0, 4), (1, 8)))
    down_weight = scatter_about(arg_keys[9], (FF, MODEL_WIDTH), FF ** -0.5, 0.046875, ((0, 8), (1, 4)))
    return {"query": query, "keys": keys, "values": values, "chosen": chosen, "residual": residual, "output_weight": output_weight, "norm_gain": norm_gain, "gate_weight": gate_weight, "up_weight": up_weight, "down_weight": down_weight}


norm_eps = 1e-05

def reference(query, keys, values, chosen, residual, output_weight, norm_gain, gate_weight, up_weight, down_weight):
    head_dim = query.shape[3]
    score_scale = head_dim ** (-0.5)
    head_ids = jnp.arange(keys.shape[1], dtype=jnp.int32)

    def one_row(inputs):
        query_row, listed = inputs
        key_sel = keys[listed, head_ids[:, None]]
        value_sel = values[listed, head_ids[:, None]]
        scores = jnp.einsum('hgd,hkjd->hkgj', query_row.astype(jnp.float32), key_sel.astype(jnp.float32)) * score_scale
        block_max = lax.optimization_barrier(jnp.max(scores, axis=3))
        probs = jnp.exp(scores - block_max[..., None])
        block_sum = lax.optimization_barrier(jnp.sum(probs, axis=3))
        probs_low = lax.optimization_barrier(probs.astype(jnp.bfloat16))
        block_value = jnp.einsum('hkgj,hkjd->hkgd', probs_low.astype(jnp.float32), value_sel.astype(jnp.float32))
        row_top = lax.optimization_barrier(jnp.max(block_max, axis=1))
        factor = jnp.exp(block_max - row_top[:, None, :])
        numerator = lax.optimization_barrier(jnp.sum(factor[..., None] * block_value, axis=1))
        denominator = lax.optimization_barrier(jnp.sum(factor * block_sum, axis=1))
        return (numerator / denominator[..., None]).astype(jnp.bfloat16)
    attended = lax.map(one_row, (query, jnp.transpose(chosen, (1, 0, 2))))
    attended = attended.reshape(query.shape[0], -1)
    projected = jnp.dot(attended, output_weight, preferred_element_type=jnp.float32)
    stream = (residual.astype(jnp.float32) + projected).astype(jnp.bfloat16)
    stream_wide = stream.astype(jnp.float32)
    mean_square = lax.optimization_barrier(jnp.mean(stream_wide * stream_wide, axis=1, keepdims=True))
    normed = (stream_wide * lax.rsqrt(mean_square + norm_eps) * norm_gain).astype(jnp.bfloat16)
    gate = jnp.dot(normed, gate_weight, preferred_element_type=jnp.float32)
    up_part = jnp.dot(normed, up_weight, preferred_element_type=jnp.float32)
    hidden = (jax.nn.silu(gate) * up_part).astype(jnp.bfloat16)
    update = jnp.dot(hidden, down_weight, preferred_element_type=jnp.float32).astype(jnp.bfloat16)
    return (stream, update)
```

```python
import functools

import jax
import jax.numpy as jnp
from jax import lax
from jax.experimental import pallas as pl
from jax.experimental.pallas import tpu as pltpu
from jax.sharding import PartitionSpec as P

MODEL_WIDTH = 8192
KEPT_PARTITIONS = 16
ROW_DEV = 1


norm_eps = 1e-05
lowest_value = -1e30


def find_slots(listed, target, capacity):
    member = jnp.any(listed == target, axis=2)
    places = jnp.cumsum(member.astype(jnp.int32), axis=1) - 1
    live_count = jnp.sum(member.astype(jnp.int32), axis=1)
    slot_ranks = jnp.arange(capacity, dtype=jnp.int32)
    slot_hits = member[:, :, None] & (places[:, :, None] == slot_ranks[None, None, :])
    row_numbers = jnp.arange(listed.shape[1], dtype=jnp.int32)
    slot_rows = jnp.sum(jnp.where(slot_hits, row_numbers[None, :, None], 0), axis=1)
    slot_valid = slot_ranks[None, :] < live_count[:, None]
    return (slot_rows, slot_valid)


def global_scaling(block_max, block_sum, block_value, slot_rows, slot_valid, all_rows, head_ids):
    kv_heads, capacity, group_size = block_max.shape
    valid_wide = slot_valid[:, :, None]
    max_table = jnp.full((all_rows, kv_heads, group_size), lowest_value, jnp.float32)
    max_table = max_table.at[slot_rows, head_ids[:, None]].max(
        jnp.where(valid_wide, block_max, lowest_value)
    )
    row_top = lax.pmax(max_table.astype(jnp.bfloat16), ("ctx", "mp")).astype(max_table.dtype)
    factor = jnp.where(valid_wide, jnp.exp(block_max - row_top[slot_rows, head_ids[:, None]]), 0.0)
    return (block_value * factor[..., None], block_sum * factor)


def to_owners(array, kv_heads, capacity, per_head, ctx_count):
    shaped = array.reshape(kv_heads, capacity, per_head, -1)
    return jnp.transpose(shaped, (0, 2, 1, 3)).reshape(ctx_count, capacity, -1)


def per_device(
    query,
    keys,
    values,
    chosen,
    residual,
    output_weight,
    norm_gain,
    gate_weight,
    up_weight,
    down_weight,
):
    kv_heads = query.shape[1]
    group_size = query.shape[2]
    head_dim = query.shape[3]
    score_scale = head_dim ** (-0.5)
    ctx_count = lax.axis_size("ctx")
    mp_count = lax.axis_size("mp")
    ctx_place = lax.axis_index("ctx")
    mp_place = lax.axis_index("mp")
    own_part = ctx_place * mp_count + mp_place
    all_queries = lax.all_gather(query, ("ctx", "mp"), axis=0, tiled=True)
    all_rows = all_queries.shape[0]
    capacity = min(4 * ROW_DEV * KEPT_PARTITIONS, all_rows)
    slot_rows, slot_valid = find_slots(chosen, own_part, capacity)
    head_ids = jnp.arange(kv_heads, dtype=jnp.int32)
    picked = all_queries[slot_rows, head_ids[:, None]].reshape(
        kv_heads, capacity * group_size, head_dim
    )

    def attend(inputs):
        query_block, key_block, value_block = inputs
        scores = (
            lax.dot_general(
                query_block, key_block, (((1,), (1,)), ((), ())), preferred_element_type=jnp.float32
            )
            * score_scale
        )
        block_max = jnp.max(scores, axis=1)
        probs = jnp.exp(scores - block_max[:, None])
        block_sum = jnp.sum(probs, axis=1)
        block_value = jnp.dot(
            probs.astype(jnp.bfloat16), value_block, preferred_element_type=jnp.float32
        )
        return (block_max, block_sum, block_value)

    block_max, block_sum, block_value = lax.map(attend, (picked, keys[0], values[0]))
    block_max = block_max.reshape(kv_heads, capacity, group_size)
    block_sum = block_sum.reshape(kv_heads, capacity, group_size)
    block_value = block_value.reshape(kv_heads, capacity, group_size, head_dim)
    per_head = ctx_count // kv_heads
    feat_width = kv_heads * group_size * head_dim // ctx_count
    head_share = kv_heads * group_size // ctx_count
    own_head = ctx_place // per_head
    head_lists = lax.dynamic_index_in_dim(chosen, own_head, 0, keepdims=True)
    sources = jnp.arange(ctx_count, dtype=jnp.int32) * mp_count + mp_place
    source_rows = jax.vmap(lambda source: find_slots(head_lists, source, capacity)[0])(sources)[
        :, 0
    ]
    weighted, scaled_sum = global_scaling(
        block_max, block_sum, block_value, slot_rows, slot_valid, all_rows, head_ids
    )
    send_values = to_owners(weighted, kv_heads, capacity, per_head, ctx_count)
    send_sums = to_owners(scaled_sum, kv_heads, capacity, per_head, ctx_count)
    got_values, got_sums = (
        lax.all_to_all(
            send_values.astype(jnp.bfloat16), "ctx", split_axis=0, concat_axis=0, tiled=True
        ).astype(send_values.dtype),
        lax.all_to_all(
            send_sums.astype(jnp.bfloat16), "ctx", split_axis=0, concat_axis=0, tiled=True
        ).astype(send_sums.dtype),
    )
    numerator = jnp.zeros((all_rows, feat_width), jnp.float32).at[source_rows].add(got_values)
    denominator = jnp.zeros((all_rows, head_share), jnp.float32).at[source_rows].add(got_sums)
    numerator, denominator = (
        lax.psum(numerator.astype(jnp.bfloat16), "mp").astype(jnp.float32),
        lax.psum(denominator.astype(jnp.bfloat16), "mp").astype(jnp.float32),
    )
    attended = (
        (numerator.reshape(all_rows, -1, head_dim) / denominator[:, :, None])
        .reshape(all_rows, -1)
        .astype(jnp.bfloat16)
    )
    rows_here = attended
    projected = lax.psum_scatter(
        jnp.dot(rows_here, output_weight, preferred_element_type=jnp.float32),
        "ctx",
        scatter_dimension=0,
        tiled=True,
    )
    stream = (residual.astype(jnp.float32) + projected).astype(jnp.bfloat16)
    stream_wide = stream.astype(jnp.float32)
    squares = lax.psum(jnp.sum(stream_wide * stream_wide, axis=1), "mp")
    normed = (
        stream_wide * lax.rsqrt(squares / MODEL_WIDTH + norm_eps)[:, None] * norm_gain
    ).astype(jnp.bfloat16)
    row_piece = lax.all_gather(normed, "ctx", axis=0, tiled=True)
    gate_piece = jnp.dot(row_piece, gate_weight, preferred_element_type=jnp.float32)
    up_piece = jnp.dot(row_piece, up_weight, preferred_element_type=jnp.float32)
    gate_up = jnp.stack([gate_piece, up_piece], axis=1)
    gate_up = lax.psum(gate_up.astype(jnp.bfloat16), "mp").astype(jnp.float32)
    hidden = (jax.nn.silu(gate_up[:, 0]) * gate_up[:, 1]).astype(jnp.bfloat16)
    rows_here = hidden
    update = lax.psum_scatter(
        jnp.dot(rows_here, down_weight, preferred_element_type=jnp.float32),
        "ctx",
        scatter_dimension=0,
        tiled=True,
    ).astype(jnp.bfloat16)
    return (stream, update)


lanes = 128


def swapped(array, bit):
    count = lax.axis_size("mp")
    return lax.ppermute(array, "mp", [(i, i ^ bit) for i in range(count)])


def over_ctx(array):
    return lax.all_to_all(array, "ctx", split_axis=0, concat_axis=0, tiled=True)


def spread(array):
    return over_ctx(jnp.broadcast_to(array[None], (lax.axis_size("ctx"),) + array.shape))


def split_stat(value):
    high = value.astype(jnp.bfloat16).astype(jnp.float32)
    return high, value - high


def attend_kernel(query_a, query_b, key_ref, value_ref, bias_ref, keep_ref, send_ref, out_s, lse_s):
    rows, _, group, depth = query_a.shape
    scale = depth ** (-0.5)
    both = jnp.concatenate(
        [
            q[:, 0].astype(jnp.float32).reshape(rows * group, depth)
            for q in (query_a, query_b)
        ],
        axis=0,
    ).astype(jnp.bfloat16)
    scores = lax.dot_general(
        both, key_ref[0], (((1,), (1,)), ((), ())), preferred_element_type=jnp.float32
    )
    top = jnp.max(scores, axis=1, keepdims=True)
    probs = jnp.exp((scores - top) * scale)
    total = jnp.sum(probs, axis=1, keepdims=True)
    mixed = jnp.dot(probs.astype(jnp.bfloat16), value_ref[0], preferred_element_type=jnp.float32)
    out_s[...] = mixed / total
    lse_s[...] = jnp.broadcast_to(top * scale + jnp.log(total), lse_s.shape)
    lane = lax.broadcasted_iota(jnp.int32, (rows, lanes), 1)
    for part, ref in enumerate((keep_ref, send_ref)):
        bias = bias_ref[0, part * rows : (part + 1) * rows, :]
        stats = jnp.zeros((rows, lanes), jnp.float32)
        for g in range(group):
            window = pl.ds(part * rows * group + g, rows, stride=group)
            ref[0, :, g * depth : (g + 1) * depth] = out_s[window, :].astype(jnp.bfloat16)
            high, low = split_stat(lse_s[window, :] + bias)
            stats = jnp.where(lane == g, high, jnp.where(lane == group + g, low, stats))
        ref[0, :, group * depth :] = stats.astype(jnp.bfloat16)


def attend(query_a, query_b, keys, values, bias):
    rows, heads, group, depth = query_a.shape
    count = keys.shape[2]
    width = group * depth + lanes
    cache_spec = pl.BlockSpec((None, 1, count, depth), lambda h: (0, h, 0, 0))
    query_spec = pl.BlockSpec((rows, 1, group, depth), lambda h: (0, h, 0, 0))
    out_spec = pl.BlockSpec((1, rows, width), lambda h: (h, 0, 0))
    shape = jax.ShapeDtypeStruct((heads, rows, width), jnp.bfloat16)
    return pl.pallas_call(
        attend_kernel,
        grid=(heads,),
        in_specs=[
            query_spec,
            query_spec,
            cache_spec,
            cache_spec,
            pl.BlockSpec((1, 2 * rows, lanes), lambda h: (h, 0, 0)),
        ],
        out_specs=[out_spec, out_spec],
        out_shape=[shape, shape],
        scratch_shapes=[
            pltpu.VMEM((2 * rows * group, depth), jnp.float32),
            pltpu.VMEM((2 * rows * group, lanes), jnp.float32),
        ],
        compiler_params=pltpu.CompilerParams(vmem_limit_bytes=24 << 20),
        cost_estimate=pl.CostEstimate(
            flops=8 * heads * rows * group * depth * count,
            bytes_accessed=4 * heads * count * depth,
            transcendentals=2 * heads * rows * group * count,
        ),
    )(query_a, query_b, keys, values, bias)


def merged(parts, group, depth):
    stats = [part[:, group * depth :] for part in parts]
    lses = [s + pltpu.roll(s, lanes - group, 1) for s in stats]
    top = functools.reduce(jnp.maximum, lses)
    weights = [jnp.exp(lse - top) for lse in lses]
    total = functools.reduce(jnp.add, weights)
    inverse = 1.0 / total
    weights = [w * inverse for w in weights]
    values = []
    for g in range(group):
        values.append(
            functools.reduce(
                jnp.add,
                [
                    w[:, g : g + 1] * part[:, g * depth : (g + 1) * depth]
                    for w, part in zip(weights, parts)
                ],
            )
        )
    return values, top + jnp.log(total)


def packed_stat(lse, group):
    lane = lax.broadcasted_iota(jnp.int32, lse.shape, 1)
    high, low = split_stat(lse)
    low = pltpu.roll(low, group, 1)
    return jnp.where(lane < group, high, jnp.where(lane < 2 * group, low, 0.0))


def core_kernel(group, depth, keep_a, recv_a, keep_b, recv_b, out_ref):
    rows = keep_a.shape[1]
    for part, (keep, recv) in enumerate(((keep_a, recv_a), (keep_b, recv_b))):
        values, lse = merged(
            [keep[0].astype(jnp.float32), recv[0].astype(jnp.float32)], group, depth
        )
        where = slice(part * rows, (part + 1) * rows)
        for g in range(group):
            out_ref[0, where, g * depth : (g + 1) * depth] = values[g].astype(jnp.bfloat16)
        out_ref[0, where, group * depth :] = packed_stat(lse, group).astype(jnp.bfloat16)


def core_merge(keep_a, recv_a, keep_b, recv_b, group, depth):
    heads, rows, width = keep_a.shape
    spec = pl.BlockSpec((1, rows, width), lambda h: (h, 0, 0))
    return pl.pallas_call(
        functools.partial(core_kernel, group, depth),
        grid=(heads,),
        in_specs=[spec] * 4,
        out_specs=pl.BlockSpec((1, 2 * rows, width), lambda h: (h, 0, 0)),
        out_shape=jax.ShapeDtypeStruct((heads, 2 * rows, width), jnp.bfloat16),
        compiler_params=pltpu.CompilerParams(vmem_limit_bytes=8 << 20),
    )(keep_a, recv_a, keep_b, recv_b)


def ctx_kernel(group, depth, got_ref, out_ref):
    values, lse = merged(
        [got_ref[s].astype(jnp.float32) for s in range(got_ref.shape[0])], group, depth
    )
    for g in range(group):
        out_ref[:, g * depth : (g + 1) * depth] = values[g].astype(jnp.bfloat16)
    out_ref[:, group * depth :] = packed_stat(lse, group).astype(jnp.bfloat16)


def x_kernel(group, depth, own_ref, got_ref, out_ref):
    half = own_ref.shape[0] // 2
    own = own_ref[...].astype(jnp.float32)
    got = got_ref[...].astype(jnp.float32)
    got = jnp.concatenate([got[half:], got[:half]], axis=0)
    values, _ = merged([own, got], group, depth)
    for g in range(group):
        out_ref[:, g * depth : (g + 1) * depth] = values[g].astype(jnp.bfloat16)


def small_call(kernel, shape, *operands):
    return pl.pallas_call(
        kernel,
        out_shape=jax.ShapeDtypeStruct(shape, jnp.bfloat16),
        compiler_params=pltpu.CompilerParams(vmem_limit_bytes=8 << 20),
    )(*operands)


def per_device_dense(
    query,
    keys,
    values,
    chosen,
    residual,
    output_weight,
    norm_gain,
    gate_weight,
    up_weight,
    down_weight,
):
    _, heads, group, depth = query.shape
    ctx_count = lax.axis_size("ctx")
    mp_count = lax.axis_size("mp")
    mp_place = lax.axis_index("mp")
    own_part = lax.axis_index("ctx") * mp_count + mp_place
    all_rows = ctx_count * mp_count

    member = jnp.any(chosen == own_part, axis=2).reshape(heads, ctx_count, 1, mp_count)
    columns = mp_place ^ jnp.arange(mp_count, dtype=jnp.int32)
    picks = columns[:, None] == jnp.arange(mp_count, dtype=jnp.int32)[None, :]
    live = jnp.any(member & picks[None, None], axis=3)
    bias = jnp.where(live, 0.0, lowest_value)
    bias = jnp.transpose(bias, (0, 2, 1))[..., None]
    bias = jnp.broadcast_to(bias, (heads, mp_count, ctx_count, lanes))
    bias = bias.reshape(heads, 2, 2 * ctx_count, lanes)

    query_own = spread(query[0])
    query_core = swapped(query_own, 1)
    query_x = swapped(query_own, 2)
    query_far = swapped(query_x, 1)
    keep_a, send_a = attend(query_own, query_core, keys, values, bias[:, 0])
    recv_a = swapped(send_a, 1)
    keep_b, send_b = attend(query_x, query_far, keys, values, bias[:, 1])
    recv_b = swapped(send_b, 1)
    on_chip = core_merge(keep_a, recv_a, keep_b, recv_b, group, depth)
    got = over_ctx(on_chip)
    half_rows = 2 * ctx_count
    width = group * depth
    column = small_call(
        functools.partial(ctx_kernel, group, depth), (half_rows, width + lanes), got
    )
    attended = small_call(
        functools.partial(x_kernel, group, depth), (half_rows, width), column, swapped(column, 2)
    )
    other = swapped(attended, 1)
    pairs = jnp.stack(
        [attended.reshape(2, ctx_count, width), other.reshape(2, ctx_count, width)], axis=1
    ).reshape(all_rows, width)
    place = jnp.arange(all_rows, dtype=jnp.int32)
    target = (place % ctx_count) * mp_count + (mp_place ^ (place // ctx_count))
    order = (place[:, None] == target[None, :]).astype(jnp.bfloat16)
    attended = jnp.dot(order, pairs, preferred_element_type=jnp.float32).astype(jnp.bfloat16)

    projected = jnp.dot(attended, output_weight, preferred_element_type=jnp.float32)
    projected = over_ctx(projected.astype(jnp.bfloat16).reshape(ctx_count, mp_count, -1))
    projected = jnp.sum(projected.astype(jnp.float32), axis=0)
    stream = (residual.astype(jnp.float32) + projected).astype(jnp.bfloat16)
    rows = spread(stream).reshape(all_rows, -1).astype(jnp.float32)
    squares = jnp.sum(rows * rows, axis=1, keepdims=True)
    scaled = (rows * norm_gain).astype(jnp.bfloat16)
    gate = jnp.dot(scaled, gate_weight, preferred_element_type=jnp.float32)
    up = jnp.dot(scaled, up_weight, preferred_element_type=jnp.float32)
    units = gate.shape[1]
    lane = jnp.arange(lanes, dtype=jnp.int32)[None, :]

    def packed(wide, squares):
        high, low = split_stat(squares)
        tail = jnp.where(lane == 0, high, jnp.where(lane == 1, low, 0.0))
        return jnp.concatenate([wide.astype(jnp.bfloat16), tail.astype(jnp.bfloat16)], axis=1)

    def unpacked(array):
        wide = array.astype(jnp.float32)
        return wide[:, : 2 * units], wide[:, 2 * units : 2 * units + 1] + wide[
            :, 2 * units + 1 : 2 * units + 2
        ]

    wide = jnp.concatenate([gate, up], axis=1)
    for bit in (1, 2):
        sent = packed(wide, squares)
        other_wide, other_squares = unpacked(swapped(sent, bit))
        wide, squares = wide + other_wide, squares + other_squares
    wide = wide * lax.rsqrt(squares / MODEL_WIDTH + norm_eps)
    hidden = (jax.nn.silu(wide[:, :units]) * wide[:, units:]).astype(jnp.bfloat16)
    update = jnp.dot(hidden, down_weight, preferred_element_type=jnp.float32)
    update = over_ctx(update.astype(jnp.bfloat16).reshape(ctx_count, mp_count, -1))
    update = jnp.sum(update.astype(jnp.float32), axis=0).astype(jnp.bfloat16)
    return (stream, update)


def either(*arrays):
    query, mp_count, ctx_count = arrays[0], lax.axis_size("mp"), lax.axis_size("ctx")
    rows, heads, group, depth = query.shape
    dense = (
        rows == 1
        and mp_count == 4
        and heads == ctx_count == group == 8
        and depth == lanes
        and arrays[1].shape[0] == 1
    )
    return (per_device_dense if dense else per_device)(*arrays)


def solution(mesh):
    return jax.shard_map(
        either,
        mesh=mesh,
        in_specs=(
            P(("ctx", "mp"), None, None, None),
            P(("ctx", "mp"), None, None, None),
            P(("ctx", "mp"), None, None, None),
            P(),
            P("ctx", "mp"),
            P("ctx", "mp"),
            P("mp"),
            P("mp", "ctx"),
            P("mp", "ctx"),
            P("ctx", "mp"),
        ),
        out_specs=(P("ctx", "mp"), P("ctx", "mp")),
        check_vma=False,
    )
```

```python
import functools
import math

import jax
import jax.numpy as jnp
from jax import lax
from jax.experimental import pallas as pl
from jax.experimental.pallas import tpu as pltpu
from jax.sharding import PartitionSpec as P

MODEL_WIDTH = 8192
KEPT_PARTITIONS = 16
ROW_DEV = 1


norm_eps = 1e-05
lowest_value = -1e30


def find_slots(listed, target, capacity):
    member = jnp.any(listed == target, axis=2)
    places = jnp.cumsum(member.astype(jnp.int32), axis=1) - 1
    live_count = jnp.sum(member.astype(jnp.int32), axis=1)
    slot_ranks = jnp.arange(capacity, dtype=jnp.int32)
    slot_hits = member[:, :, None] & (places[:, :, None] == slot_ranks[None, None, :])
    row_numbers = jnp.arange(listed.shape[1], dtype=jnp.int32)
    slot_rows = jnp.sum(jnp.where(slot_hits, row_numbers[None, :, None], 0), axis=1)
    slot_valid = slot_ranks[None, :] < live_count[:, None]
    return (slot_rows, slot_valid)


def global_scaling(block_max, block_sum, block_value, slot_rows, slot_valid, all_rows, head_ids):
    kv_heads, capacity, group_size = block_max.shape
    valid_wide = slot_valid[:, :, None]
    max_table = jnp.full((all_rows, kv_heads, group_size), lowest_value, jnp.float32)
    max_table = max_table.at[slot_rows, head_ids[:, None]].max(
        jnp.where(valid_wide, block_max, lowest_value)
    )
    row_top = lax.pmax(max_table.astype(jnp.bfloat16), ("ctx", "mp")).astype(max_table.dtype)
    factor = jnp.where(valid_wide, jnp.exp(block_max - row_top[slot_rows, head_ids[:, None]]), 0.0)
    return (block_value * factor[..., None], block_sum * factor)


def to_owners(array, kv_heads, capacity, per_head, ctx_count):
    shaped = array.reshape(kv_heads, capacity, per_head, -1)
    return jnp.transpose(shaped, (0, 2, 1, 3)).reshape(ctx_count, capacity, -1)


def per_device(
    query,
    keys,
    values,
    chosen,
    residual,
    output_weight,
    norm_gain,
    gate_weight,
    up_weight,
    down_weight,
):
    kv_heads = query.shape[1]
    group_size = query.shape[2]
    head_dim = query.shape[3]
    score_scale = head_dim ** (-0.5)
    ctx_count = lax.axis_size("ctx")
    mp_count = lax.axis_size("mp")
    ctx_place = lax.axis_index("ctx")
    mp_place = lax.axis_index("mp")
    own_part = ctx_place * mp_count + mp_place
    all_queries = lax.all_gather(query, ("ctx", "mp"), axis=0, tiled=True)
    all_rows = all_queries.shape[0]
    capacity = min(4 * ROW_DEV * KEPT_PARTITIONS, all_rows)
    slot_rows, slot_valid = find_slots(chosen, own_part, capacity)
    head_ids = jnp.arange(kv_heads, dtype=jnp.int32)
    picked = all_queries[slot_rows, head_ids[:, None]].reshape(
        kv_heads, capacity * group_size, head_dim
    )

    def attend(inputs):
        query_block, key_block, value_block = inputs
        scores = (
            lax.dot_general(
                query_block, key_block, (((1,), (1,)), ((), ())), preferred_element_type=jnp.float32
            )
            * score_scale
        )
        block_max = jnp.max(scores, axis=1)
        probs = jnp.exp(scores - block_max[:, None])
        block_sum = jnp.sum(probs, axis=1)
        block_value = jnp.dot(
            probs.astype(jnp.bfloat16), value_block, preferred_element_type=jnp.float32
        )
        return (block_max, block_sum, block_value)

    block_max, block_sum, block_value = lax.map(attend, (picked, keys[0], values[0]))
    block_max = block_max.reshape(kv_heads, capacity, group_size)
    block_sum = block_sum.reshape(kv_heads, capacity, group_size)
    block_value = block_value.reshape(kv_heads, capacity, group_size, head_dim)
    per_head = ctx_count // kv_heads
    feat_width = kv_heads * group_size * head_dim // ctx_count
    head_share = kv_heads * group_size // ctx_count
    own_head = ctx_place // per_head
    head_lists = lax.dynamic_index_in_dim(chosen, own_head, 0, keepdims=True)
    sources = jnp.arange(ctx_count, dtype=jnp.int32) * mp_count + mp_place
    source_rows = jax.vmap(lambda source: find_slots(head_lists, source, capacity)[0])(sources)[
        :, 0
    ]
    weighted, scaled_sum = global_scaling(
        block_max, block_sum, block_value, slot_rows, slot_valid, all_rows, head_ids
    )
    send_values = to_owners(weighted, kv_heads, capacity, per_head, ctx_count)
    send_sums = to_owners(scaled_sum, kv_heads, capacity, per_head, ctx_count)
    got_values, got_sums = (
        lax.all_to_all(
            send_values.astype(jnp.bfloat16), "ctx", split_axis=0, concat_axis=0, tiled=True
        ).astype(send_values.dtype),
        lax.all_to_all(
            send_sums.astype(jnp.bfloat16), "ctx", split_axis=0, concat_axis=0, tiled=True
        ).astype(send_sums.dtype),
    )
    numerator = jnp.zeros((all_rows, feat_width), jnp.float32).at[source_rows].add(got_values)
    denominator = jnp.zeros((all_rows, head_share), jnp.float32).at[source_rows].add(got_sums)
    numerator, denominator = (
        lax.psum(numerator.astype(jnp.bfloat16), "mp").astype(jnp.float32),
        lax.psum(denominator.astype(jnp.bfloat16), "mp").astype(jnp.float32),
    )
    attended = (
        (numerator.reshape(all_rows, -1, head_dim) / denominator[:, :, None])
        .reshape(all_rows, -1)
        .astype(jnp.bfloat16)
    )
    rows_here = attended
    projected = lax.psum_scatter(
        jnp.dot(rows_here, output_weight, preferred_element_type=jnp.float32),
        "ctx",
        scatter_dimension=0,
        tiled=True,
    )
    stream = (residual.astype(jnp.float32) + projected).astype(jnp.bfloat16)
    stream_wide = stream.astype(jnp.float32)
    squares = lax.psum(jnp.sum(stream_wide * stream_wide, axis=1), "mp")
    normed = (
        stream_wide * lax.rsqrt(squares / MODEL_WIDTH + norm_eps)[:, None] * norm_gain
    ).astype(jnp.bfloat16)
    row_piece = lax.all_gather(normed, "ctx", axis=0, tiled=True)
    gate_piece = jnp.dot(row_piece, gate_weight, preferred_element_type=jnp.float32)
    up_piece = jnp.dot(row_piece, up_weight, preferred_element_type=jnp.float32)
    gate_up = jnp.stack([gate_piece, up_piece], axis=1)
    gate_up = lax.psum(gate_up.astype(jnp.bfloat16), "mp").astype(jnp.float32)
    hidden = (jax.nn.silu(gate_up[:, 0]) * gate_up[:, 1]).astype(jnp.bfloat16)
    rows_here = hidden
    update = lax.psum_scatter(
        jnp.dot(rows_here, down_weight, preferred_element_type=jnp.float32),
        "ctx",
        scatter_dimension=0,
        tiled=True,
    ).astype(jnp.bfloat16)
    return (stream, update)


lanes = 128
abreast = 2
log2_e = math.log2(math.e)


def swapped(array, bit):
    count = lax.axis_size("mp")
    return lax.ppermute(array, "mp", [(i, i ^ bit) for i in range(count)])


def over_ctx(array):
    return lax.all_to_all(array, "ctx", split_axis=0, concat_axis=0, tiled=True)


def copies_kernel(in_ref, out_ref):
    for i in range(out_ref.shape[0]):
        out_ref[i] = in_ref[...]


def split_stat(value):
    high = value.astype(jnp.bfloat16).astype(jnp.float32)
    return high, value - high


def attend_kernel(
    pair, part_ref, place_ref, query_a, query_b, keys, values, chosen_ref, keep_ref, send_ref,
    key_ref, value_ref, out_s, lse_s, sems,
):
    rows, heads, group, depth = query_a.shape
    scale = depth ** (-0.5)
    lane = lax.broadcasted_iota(jnp.int32, (rows, lanes), 1)
    listed = chosen_ref.shape[2]
    row_lane = lax.broadcasted_iota(jnp.int32, (rows, listed), 1)
    row_place = lax.broadcasted_iota(jnp.int32, (rows, listed), 0) * (listed // rows)

    def scored(h):
        both = jnp.concatenate(
            [
                q[:, h].astype(jnp.float32).reshape(rows * group, depth)
                for q in (query_a, query_b)
            ],
            axis=0,
        ).astype(jnp.bfloat16)
        return lax.dot_general(
            both, key_ref[h], (((1,), (1,)), ((), ())), preferred_element_type=jnp.float32
        )

    def finish(h, slot, scores):
        top = jnp.max(scores, axis=1, keepdims=True)
        probs = jnp.exp2((scores - top) * (scale * log2_e))
        total = jnp.sum(probs, axis=1, keepdims=True)
        mixed = jnp.dot(
            probs.astype(jnp.bfloat16), value_ref[h], preferred_element_type=jnp.float32
        )
        out_s[slot] = mixed * (1.0 / total)
        lse_s[slot] = jnp.broadcast_to(top * scale + jnp.log(total), lse_s.shape[1:])
        member = jnp.where(chosen_ref[h] == part_ref[0], 1.0, 0.0)
        member = jnp.max(member, axis=0, keepdims=True)
        for part, ref in enumerate((keep_ref, send_ref)):
            row = row_place + (place_ref[0] ^ (2 * pair + part))
            held = jnp.where(row_lane == row, member, 0.0)
            bias = jnp.where(jnp.max(held, axis=1, keepdims=True) > 0.5, 0.0, lowest_value)
            stats = jnp.zeros((rows, lanes), jnp.float32)
            for g in range(group):
                window = pl.ds(part * rows * group + g, rows, stride=group)
                ref[h, :, g * depth : (g + 1) * depth] = out_s[slot, window, :].astype(jnp.bfloat16)
                high, low = split_stat(lse_s[slot, window, :] + bias)
                stats = jnp.where(lane == g, high, jnp.where(lane == group + g, low, stats))
            ref[h, :, group * depth :] = stats.astype(jnp.bfloat16)

    def arrivals(h):
        return (
            pltpu.make_async_copy(keys.at[h], key_ref.at[h], sems.at[0, h]),
            pltpu.make_async_copy(values.at[h], value_ref.at[h], sems.at[1, h]),
        )

    for h in range(heads):
        for copy in arrivals(h):
            copy.start()

    @pl.loop(0, heads // abreast)
    def _(step):
        for slot in range(abreast):
            for copy in arrivals(step * abreast + slot):
                copy.wait()
        for slot in range(abreast):
            h = step * abreast + slot
            finish(h, slot, scored(h))


def attend(pair, part, place, query_a, query_b, keys, values, chosen):
    rows, heads, group, depth = query_a.shape
    count = keys.shape[1]
    width = group * depth + lanes
    shape = jax.ShapeDtypeStruct((heads, rows, width), jnp.bfloat16)
    return pl.pallas_call(
        functools.partial(attend_kernel, pair),
        in_specs=[pl.BlockSpec(memory_space=pltpu.SMEM)] * 2
        + [pl.BlockSpec(memory_space=pltpu.VMEM)] * 2
        + [pl.BlockSpec(memory_space=pltpu.HBM)] * 2
        + [pl.BlockSpec(memory_space=pltpu.VMEM)],
        out_specs=[pl.BlockSpec(memory_space=pltpu.VMEM)] * 2,
        out_shape=[shape, shape],
        scratch_shapes=[
            pltpu.VMEM(keys.shape, keys.dtype),
            pltpu.VMEM(values.shape, values.dtype),
            pltpu.VMEM((abreast, 2 * rows * group, depth), jnp.float32),
            pltpu.VMEM((abreast, 2 * rows * group, lanes), jnp.float32),
            pltpu.SemaphoreType.DMA((2, heads)),
        ],
        compiler_params=pltpu.CompilerParams(vmem_limit_bytes=24 << 20),
        cost_estimate=pl.CostEstimate(
            flops=8 * heads * rows * group * depth * count,
            bytes_accessed=4 * heads * count * depth,
            transcendentals=2 * heads * rows * group * count,
        ),
    )(
        part,
        place,
        query_a,
        query_b,
        pltpu.with_memory_space_constraint(keys, pltpu.HBM),
        pltpu.with_memory_space_constraint(values, pltpu.HBM),
        chosen,
    )


def merged(parts, group, depth):
    stats = [part[:, group * depth :] for part in parts]
    lses = [s + pltpu.roll(s, lanes - group, 1) for s in stats]
    top = functools.reduce(jnp.maximum, lses)
    weights = [jnp.exp(lse - top) for lse in lses]
    total = functools.reduce(jnp.add, weights)
    inverse = 1.0 / total
    weights = [w * inverse for w in weights]
    values = []
    for g in range(group):
        values.append(
            functools.reduce(
                jnp.add,
                [
                    w[:, g : g + 1] * part[:, g * depth : (g + 1) * depth]
                    for w, part in zip(weights, parts)
                ],
            )
        )
    return values, top + jnp.log(total)


def packed_stat(lse, group):
    lane = lax.broadcasted_iota(jnp.int32, lse.shape, 1)
    high, low = split_stat(lse)
    low = pltpu.roll(low, group, 1)
    return jnp.where(lane < group, high, jnp.where(lane < 2 * group, low, 0.0))


def core_kernel(group, depth, keep_a, recv_a, keep_b, recv_b, out_ref):
    rows = keep_a.shape[1]
    for part, (keep, recv) in enumerate(((keep_a, recv_a), (keep_b, recv_b))):
        values, lse = merged(
            [keep[0].astype(jnp.float32), recv[0].astype(jnp.float32)], group, depth
        )
        where = slice(part * rows, (part + 1) * rows)
        for g in range(group):
            out_ref[0, where, g * depth : (g + 1) * depth] = values[g].astype(jnp.bfloat16)
        out_ref[0, where, group * depth :] = packed_stat(lse, group).astype(jnp.bfloat16)


def core_merge(keep_a, recv_a, keep_b, recv_b, group, depth):
    heads, rows, width = keep_a.shape
    spec = pl.BlockSpec((1, rows, width), lambda h: (h, 0, 0))
    return pl.pallas_call(
        functools.partial(core_kernel, group, depth),
        grid=(heads,),
        in_specs=[spec] * 4,
        out_specs=pl.BlockSpec((1, 2 * rows, width), lambda h: (h, 0, 0)),
        out_shape=jax.ShapeDtypeStruct((heads, 2 * rows, width), jnp.bfloat16),
        compiler_params=pltpu.CompilerParams(vmem_limit_bytes=8 << 20),
    )(keep_a, recv_a, keep_b, recv_b)


def ctx_kernel(group, depth, got_ref, out_ref):
    values, lse = merged(
        [got_ref[s].astype(jnp.float32) for s in range(got_ref.shape[0])], group, depth
    )
    for g in range(group):
        out_ref[:, g * depth : (g + 1) * depth] = values[g].astype(jnp.bfloat16)
    out_ref[:, group * depth :] = packed_stat(lse, group).astype(jnp.bfloat16)


def x_kernel(group, depth, own_ref, got_ref, out_ref):
    half = own_ref.shape[0] // 2
    own = own_ref[...].astype(jnp.float32)
    got = got_ref[...].astype(jnp.float32)
    got = jnp.concatenate([got[half:], got[:half]], axis=0)
    values, _ = merged([own, got], group, depth)
    for g in range(group):
        out_ref[:, g * depth : (g + 1) * depth] = values[g].astype(jnp.bfloat16)


def small_call(kernel, shapes, *operands, flops=0):
    return pl.pallas_call(
        kernel,
        out_shape=jax.tree.map(
            lambda shape: jax.ShapeDtypeStruct(shape, jnp.bfloat16),
            shapes,
            is_leaf=lambda x: isinstance(x, tuple),
        ),
        compiler_params=pltpu.CompilerParams(vmem_limit_bytes=8 << 20),
        cost_estimate=pl.CostEstimate(flops=flops, bytes_accessed=1 << 19, transcendentals=0),
    )(*operands)


def scatter_rows(out_ref, value):
    step = out_ref.shape[1]
    for i in range(out_ref.shape[0]):
        out_ref[i] = value[i * step : (i + 1) * step].astype(out_ref.dtype)


def stream_kernel(got_ref, residual_ref, stream_ref, copies_ref):
    total = residual_ref[...].astype(jnp.float32)
    partial = got_ref[0].astype(jnp.float32)
    for i in range(1, got_ref.shape[0]):
        partial += got_ref[i].astype(jnp.float32)
    stream = (total + partial).astype(jnp.bfloat16)
    stream_ref[...] = stream
    for i in range(copies_ref.shape[0]):
        copies_ref[i] = stream


def project_kernel(place_ref, own_ref, got_ref, weight_ref, out_ref):
    rows = out_ref.shape[0] * out_ref.shape[1]
    half = rows // 2
    quarter = rows // 4
    place = place_ref[0]
    target = lax.broadcasted_iota(jnp.int32, (rows, half), 0)
    source = lax.broadcasted_iota(jnp.int32, (rows, half), 1)
    row = (source % quarter) * 4
    column = 2 * (source // quarter)
    own_order = jnp.where(target == row + (place ^ column), 1.0, 0.0).astype(jnp.bfloat16)
    got_order = jnp.where(target == row + (place ^ (column + 1)), 1.0, 0.0).astype(jnp.bfloat16)
    attended = jnp.dot(own_order, own_ref[...], preferred_element_type=jnp.float32) + jnp.dot(
        got_order, got_ref[...], preferred_element_type=jnp.float32
    )
    scatter_rows(
        out_ref,
        jnp.dot(
            attended.astype(jnp.bfloat16), weight_ref[...], preferred_element_type=jnp.float32
        ),
    )


def tail_of(squares):
    lane = lax.broadcasted_iota(jnp.int32, (squares.shape[0], lanes), 1)
    high, low = split_stat(squares)
    return jnp.where(lane == 0, high, jnp.where(lane == 1, low, 0.0)).astype(jnp.bfloat16)


def gate_kernel(rows_ref, gain_ref, gate_ref, up_ref, out_ref):
    units = gate_ref.shape[1]
    rows = jnp.concatenate(
        [rows_ref[i].astype(jnp.float32) for i in range(rows_ref.shape[0])], axis=0
    )
    scaled = (rows * gain_ref[...]).astype(jnp.bfloat16)
    for i, ref in enumerate((gate_ref, up_ref)):
        out_ref[:, i * units : (i + 1) * units] = jnp.dot(
            scaled, ref[...], preferred_element_type=jnp.float32
        ).astype(jnp.bfloat16)
    out_ref[:, 2 * units :] = tail_of(jnp.sum(rows * rows, axis=1, keepdims=True))


def summed(own_ref, got_ref, start, stop):
    return own_ref[:, start:stop].astype(jnp.float32) + got_ref[:, start:stop].astype(jnp.float32)


def squares_of(own_ref, got_ref):
    start = own_ref.shape[1] - lanes
    tail = summed(own_ref, got_ref, start, start + lanes)
    return tail[:, 0:1] + tail[:, 1:2]


def pair_kernel(own_ref, got_ref, out_ref):
    units = own_ref.shape[1] - lanes
    out_ref[:, :units] = summed(own_ref, got_ref, 0, units).astype(jnp.bfloat16)
    out_ref[:, units:] = tail_of(squares_of(own_ref, got_ref))


def down_kernel(own_ref, got_ref, weight_ref, out_ref):
    units = weight_ref.shape[0]
    scale = lax.rsqrt(squares_of(own_ref, got_ref) / MODEL_WIDTH + norm_eps)
    gate = summed(own_ref, got_ref, 0, units) * scale
    up = summed(own_ref, got_ref, units, 2 * units) * scale
    hidden = (jax.nn.silu(gate) * up).astype(jnp.bfloat16)
    scatter_rows(
        out_ref, jnp.dot(hidden, weight_ref[...], preferred_element_type=jnp.float32)
    )


def weighed(kernel, shape, weights, *operands, scalar=None):
    vmem = pl.BlockSpec(memory_space=pltpu.VMEM)
    specs = [vmem] * (len(operands) + len(weights))
    if scalar is not None:
        specs = [pl.BlockSpec(memory_space=pltpu.SMEM)] + specs
        operands = (scalar,) + operands
    return pl.pallas_call(
        kernel,
        in_specs=specs,
        out_specs=vmem,
        out_shape=jax.ShapeDtypeStruct(shape, jnp.bfloat16),
        compiler_params=pltpu.CompilerParams(vmem_limit_bytes=8 << 20),
        cost_estimate=pl.CostEstimate(
            flops=sum(64 * w.size for w in weights),
            bytes_accessed=sum(2 * w.size for w in weights),
            transcendentals=0,
        ),
    )(*operands, *(pltpu.with_memory_space_constraint(w, pltpu.VMEM) for w in weights))


def per_device_dense(
    query,
    keys,
    values,
    chosen,
    residual,
    output_weight,
    norm_gain,
    gate_weight,
    up_weight,
    down_weight,
):
    _, heads, group, depth = query.shape
    ctx_count = lax.axis_size("ctx")
    mp_count = lax.axis_size("mp")
    mp_place = lax.axis_index("mp")
    own_part = lax.axis_index("ctx") * mp_count + mp_place
    all_rows = ctx_count * mp_count

    part, place = jnp.reshape(own_part, (1,)), jnp.reshape(mp_place, (1,))
    chosen = jnp.transpose(chosen, (0, 2, 1))
    copies = small_call(
        copies_kernel, (ctx_count,) + query.shape[1:], query[0], flops=0
    )
    query_own = over_ctx(copies)
    keys, values = keys[0], values[0]
    query_core = swapped(query_own, 1)
    query_x = swapped(query_own, 2)
    keep_a, send_a = attend(0, part, place, query_own, query_core, keys, values, chosen)
    query_x, _ = lax.optimization_barrier((query_x, send_a))
    query_far = swapped(query_x, 1)
    recv_a = swapped(send_a, 1)
    keep_b, send_b = attend(1, part, place, query_x, query_far, keys, values, chosen)
    recv_b = swapped(send_b, 1)
    on_chip = core_merge(keep_a, recv_a, keep_b, recv_b, group, depth)
    got = over_ctx(on_chip)
    half_rows = 2 * ctx_count
    width = group * depth
    column = small_call(
        functools.partial(ctx_kernel, group, depth), (half_rows, width + lanes), got
    )
    attended = small_call(
        functools.partial(x_kernel, group, depth), (half_rows, width), column, swapped(column, 2)
    )
    other = swapped(attended, 1)
    width = output_weight.shape[1]
    block = (ctx_count, mp_count, width)
    projected = weighed(project_kernel, block, (output_weight,), attended, other, scalar=place)
    stream, copies = small_call(
        stream_kernel, [residual.shape, block], over_ctx(projected), residual
    )
    rows = over_ctx(copies)
    units = gate_weight.shape[1]
    mine = weighed(
        gate_kernel,
        (all_rows, 2 * units + lanes),
        (gate_weight, up_weight),
        rows,
        norm_gain.reshape(1, -1),
    )
    mine = small_call(pair_kernel, mine.shape, mine, swapped(mine, 1))
    update = weighed(
        down_kernel,
        block,
        (down_weight,),
        mine,
        swapped(mine, 2),
    )
    update = over_ctx(update)
    update = jnp.sum(update.astype(jnp.float32), axis=0).astype(jnp.bfloat16)
    return (stream, update)


def either(*arrays):
    query, mp_count, ctx_count = arrays[0], lax.axis_size("mp"), lax.axis_size("ctx")
    rows, heads, group, depth = query.shape
    dense = (
        rows == 1
        and mp_count == 4
        and heads == ctx_count == group == 8
        and depth == lanes
        and arrays[1].shape[0] == 1
    )
    return (per_device_dense if dense else per_device)(*arrays)


def solution(mesh):
    return jax.shard_map(
        either,
        mesh=mesh,
        in_specs=(
            P(("ctx", "mp"), None, None, None),
            P(("ctx", "mp"), None, None, None),
            P(("ctx", "mp"), None, None, None),
            P(),
            P("ctx", "mp"),
            P("ctx", "mp"),
            P("mp"),
            P("mp", "ctx"),
            P("mp", "ctx"),
            P("ctx", "mp"),
        ),
        out_specs=(P("ctx", "mp"), P("ctx", "mp")),
        check_vma=False,
    )
```

```python
import functools
import math

import jax
import jax.numpy as jnp
from jax import lax
from jax.experimental import pallas as pl
from jax.experimental.pallas import tpu as pltpu
from jax.sharding import PartitionSpec as P

MODEL_WIDTH = 8192
KEPT_PARTITIONS = 16
ROW_DEV = 1


norm_eps = 1e-05
lowest_value = -1e30


def find_slots(listed, target, capacity):
    member = jnp.any(listed == target, axis=2)
    places = jnp.cumsum(member.astype(jnp.int32), axis=1) - 1
    live_count = jnp.sum(member.astype(jnp.int32), axis=1)
    slot_ranks = jnp.arange(capacity, dtype=jnp.int32)
    slot_hits = member[:, :, None] & (places[:, :, None] == slot_ranks[None, None, :])
    row_numbers = jnp.arange(listed.shape[1], dtype=jnp.int32)
    slot_rows = jnp.sum(jnp.where(slot_hits, row_numbers[None, :, None], 0), axis=1)
    slot_valid = slot_ranks[None, :] < live_count[:, None]
    return (slot_rows, slot_valid)


def global_scaling(block_max, block_sum, block_value, slot_rows, slot_valid, all_rows, head_ids):
    kv_heads, capacity, group_size = block_max.shape
    valid_wide = slot_valid[:, :, None]
    max_table = jnp.full((all_rows, kv_heads, group_size), lowest_value, jnp.float32)
    max_table = max_table.at[slot_rows, head_ids[:, None]].max(
        jnp.where(valid_wide, block_max, lowest_value)
    )
    row_top = lax.pmax(max_table.astype(jnp.bfloat16), ("ctx", "mp")).astype(max_table.dtype)
    factor = jnp.where(valid_wide, jnp.exp(block_max - row_top[slot_rows, head_ids[:, None]]), 0.0)
    return (block_value * factor[..., None], block_sum * factor)


def to_owners(array, kv_heads, capacity, per_head, ctx_count):
    shaped = array.reshape(kv_heads, capacity, per_head, -1)
    return jnp.transpose(shaped, (0, 2, 1, 3)).reshape(ctx_count, capacity, -1)


def per_device(
    query,
    keys,
    values,
    chosen,
    residual,
    output_weight,
    norm_gain,
    gate_weight,
    up_weight,
    down_weight,
):
    kv_heads = query.shape[1]
    group_size = query.shape[2]
    head_dim = query.shape[3]
    score_scale = head_dim ** (-0.5)
    ctx_count = lax.axis_size("ctx")
    mp_count = lax.axis_size("mp")
    ctx_place = lax.axis_index("ctx")
    mp_place = lax.axis_index("mp")
    own_part = ctx_place * mp_count + mp_place
    all_queries = lax.all_gather(query, ("ctx", "mp"), axis=0, tiled=True)
    all_rows = all_queries.shape[0]
    capacity = min(4 * ROW_DEV * KEPT_PARTITIONS, all_rows)
    slot_rows, slot_valid = find_slots(chosen, own_part, capacity)
    head_ids = jnp.arange(kv_heads, dtype=jnp.int32)
    picked = all_queries[slot_rows, head_ids[:, None]].reshape(
        kv_heads, capacity * group_size, head_dim
    )

    def attend(inputs):
        query_block, key_block, value_block = inputs
        scores = (
            lax.dot_general(
                query_block, key_block, (((1,), (1,)), ((), ())), preferred_element_type=jnp.float32
            )
            * score_scale
        )
        block_max = jnp.max(scores, axis=1)
        probs = jnp.exp(scores - block_max[:, None])
        block_sum = jnp.sum(probs, axis=1)
        block_value = jnp.dot(
            probs.astype(jnp.bfloat16), value_block, preferred_element_type=jnp.float32
        )
        return (block_max, block_sum, block_value)

    block_max, block_sum, block_value = lax.map(attend, (picked, keys[0], values[0]))
    block_max = block_max.reshape(kv_heads, capacity, group_size)
    block_sum = block_sum.reshape(kv_heads, capacity, group_size)
    block_value = block_value.reshape(kv_heads, capacity, group_size, head_dim)
    per_head = ctx_count // kv_heads
    feat_width = kv_heads * group_size * head_dim // ctx_count
    head_share = kv_heads * group_size // ctx_count
    own_head = ctx_place // per_head
    head_lists = lax.dynamic_index_in_dim(chosen, own_head, 0, keepdims=True)
    sources = jnp.arange(ctx_count, dtype=jnp.int32) * mp_count + mp_place
    source_rows = jax.vmap(lambda source: find_slots(head_lists, source, capacity)[0])(sources)[
        :, 0
    ]
    weighted, scaled_sum = global_scaling(
        block_max, block_sum, block_value, slot_rows, slot_valid, all_rows, head_ids
    )
    send_values = to_owners(weighted, kv_heads, capacity, per_head, ctx_count)
    send_sums = to_owners(scaled_sum, kv_heads, capacity, per_head, ctx_count)
    got_values, got_sums = (
        lax.all_to_all(
            send_values.astype(jnp.bfloat16), "ctx", split_axis=0, concat_axis=0, tiled=True
        ).astype(send_values.dtype),
        lax.all_to_all(
            send_sums.astype(jnp.bfloat16), "ctx", split_axis=0, concat_axis=0, tiled=True
        ).astype(send_sums.dtype),
    )
    numerator = jnp.zeros((all_rows, feat_width), jnp.float32).at[source_rows].add(got_values)
    denominator = jnp.zeros((all_rows, head_share), jnp.float32).at[source_rows].add(got_sums)
    numerator, denominator = (
        lax.psum(numerator.astype(jnp.bfloat16), "mp").astype(jnp.float32),
        lax.psum(denominator.astype(jnp.bfloat16), "mp").astype(jnp.float32),
    )
    attended = (
        (numerator.reshape(all_rows, -1, head_dim) / denominator[:, :, None])
        .reshape(all_rows, -1)
        .astype(jnp.bfloat16)
    )
    rows_here = attended
    projected = lax.psum_scatter(
        jnp.dot(rows_here, output_weight, preferred_element_type=jnp.float32),
        "ctx",
        scatter_dimension=0,
        tiled=True,
    )
    stream = (residual.astype(jnp.float32) + projected).astype(jnp.bfloat16)
    stream_wide = stream.astype(jnp.float32)
    squares = lax.psum(jnp.sum(stream_wide * stream_wide, axis=1), "mp")
    normed = (
        stream_wide * lax.rsqrt(squares / MODEL_WIDTH + norm_eps)[:, None] * norm_gain
    ).astype(jnp.bfloat16)
    row_piece = lax.all_gather(normed, "ctx", axis=0, tiled=True)
    gate_piece = jnp.dot(row_piece, gate_weight, preferred_element_type=jnp.float32)
    up_piece = jnp.dot(row_piece, up_weight, preferred_element_type=jnp.float32)
    gate_up = jnp.stack([gate_piece, up_piece], axis=1)
    gate_up = lax.psum(gate_up.astype(jnp.bfloat16), "mp").astype(jnp.float32)
    hidden = (jax.nn.silu(gate_up[:, 0]) * gate_up[:, 1]).astype(jnp.bfloat16)
    rows_here = hidden
    update = lax.psum_scatter(
        jnp.dot(rows_here, down_weight, preferred_element_type=jnp.float32),
        "ctx",
        scatter_dimension=0,
        tiled=True,
    ).astype(jnp.bfloat16)
    return (stream, update)


lanes = 128
chunk = 512
ahead = 4
log2_e = math.log2(math.e)


def swapped(array, bit):
    count = lax.axis_size("mp")
    return lax.ppermute(array, "mp", [(i, i ^ bit) for i in range(count)])


def over_ctx(array):
    return lax.all_to_all(array, "ctx", split_axis=0, concat_axis=0, tiled=True)


def copies_kernel(in_ref, out_ref):
    for i in range(out_ref.shape[0]):
        out_ref[i] = in_ref[...]


def split_stat(value):
    high = value.astype(jnp.bfloat16).astype(jnp.float32)
    return high, value - high


def attend_kernel(pair, part_ref, place_ref, query_a, query_b, keys, values, chosen, *refs):
    if pair == 0:
        keep_ref, send_ref, key_ref, value_ref = refs[:4]
    else:
        keep_ref, send_ref = refs[:2]
        key_ref, value_ref = keys, values
    score_s, top_s, out_s, lse_s, chosen_ref, sems, chosen_sem = refs[-7:]
    rows, heads, group, depth = query_a.shape
    count = key_ref.shape[1]
    scale = depth ** (-0.5)
    lane = lax.broadcasted_iota(jnp.int32, (rows, lanes), 1)
    listed = chosen_ref.shape[2]
    row_lane = lax.broadcasted_iota(jnp.int32, (rows, listed), 1)
    row_place = lax.broadcasted_iota(jnp.int32, (rows, listed), 0) * (listed // rows)
    chosen_copy = pltpu.make_async_copy(chosen, chosen_ref, chosen_sem)

    def arrivals(h):
        return (
            pltpu.make_async_copy(keys.at[h], key_ref.at[h], sems.at[0, h]),
            pltpu.make_async_copy(values.at[h], value_ref.at[h], sems.at[1, h]),
        )

    def send_for(h):
        if pair == 0:
            for copy in arrivals(h):
                copy.start()

    def wait_for(h):
        if pair == 0:
            for copy in arrivals(h):
                copy.wait()

    def query_of(h):
        return jnp.concatenate(
            [
                q[:, h].astype(jnp.float32).reshape(rows * group, depth)
                for q in (query_a, query_b)
            ],
            axis=0,
        ).astype(jnp.bfloat16)

    def score(query, h, slot, i, top):
        window = slice(i * chunk, (i + 1) * chunk)
        scores = lax.dot_general(
            query, key_ref[h, window, :], (((1,), (1,)), ((), ())),
            preferred_element_type=jnp.float32,
        )
        score_s[slot, :, window] = scores
        for j in range(chunk // lanes):
            part = scores[:, j * lanes : (j + 1) * lanes]
            top = part if top is None else jnp.maximum(top, part)
        return top

    def spent(h, slot, i, top, total, mixed):
        window = slice(i * chunk, (i + 1) * chunk)
        probs = jnp.exp2((score_s[slot, :, window] - top) * (scale * log2_e))
        for j in range(chunk // lanes):
            part = probs[:, j * lanes : (j + 1) * lanes]
            total = part if total is None else total + part
        part = jnp.dot(
            probs.astype(jnp.bfloat16), value_ref[h, window, :], preferred_element_type=jnp.float32
        )
        return total, part if mixed is None else mixed + part

    def finish(h, slot, top, total, mixed):
        total = jnp.sum(total, axis=1, keepdims=True)
        out_s[slot] = mixed * (1.0 / total)
        lse_s[slot] = jnp.broadcast_to(top * scale + jnp.log(total), lse_s.shape[1:])
        member = jnp.where(chosen_ref[h] == part_ref[0], 1.0, 0.0)
        member = jnp.max(member, axis=0, keepdims=True)
        for part, ref in enumerate((keep_ref, send_ref)):
            row = row_place + (place_ref[0] ^ (2 * pair + part))
            held = jnp.where(row_lane == row, member, 0.0)
            bias = jnp.where(jnp.max(held, axis=1, keepdims=True) > 0.5, 0.0, lowest_value)
            stats = jnp.zeros((rows, lanes), jnp.float32)
            for g in range(group):
                window = pl.ds(part * rows * group + g, rows, stride=group)
                ref[h, :, g * depth : (g + 1) * depth] = out_s[slot, window, :].astype(jnp.bfloat16)
                high, low = split_stat(lse_s[slot, window, :] + bias)
                stats = jnp.where(lane == g, high, jnp.where(lane == group + g, low, stats))
            ref[h, :, group * depth :] = stats.astype(jnp.bfloat16)

    def both(h, slot, following, after):
        top = jnp.max(top_s[slot], axis=1, keepdims=True)
        query = query_of(following)
        total = mixed = later = None
        for i in range(count // chunk):
            total, mixed = spent(h, slot, i, top, total, mixed)
            later = score(query, following, after, i, later)
        top_s[after] = later
        finish(h, slot, top, total, mixed)

    for h in range(min(ahead, heads)):
        send_for(h)
    chosen_copy.start()
    wait_for(0)
    query, top = query_of(0), None
    for i in range(count // chunk):
        top = score(query, 0, 0, i, top)
    top_s[0] = top
    chosen_copy.wait()

    @pl.loop(0, heads // 2)
    def _(step):
        h = 2 * step
        wait_for(h + 1)
        both(h, 0, h + 1, 1)

        @pl.when(h + 2 < heads)
        def _():
            wait_for(h + 2)

        for i in range(2):

            @pl.when(h + ahead + i < heads)
            def _():
                send_for(h + ahead + i)

        both(h + 1, 1, jnp.minimum(h + 2, heads - 1), 0)


def attend(pair, part, place, query_a, query_b, keys, values, chosen):
    rows, heads, group, depth = query_a.shape
    count = keys.shape[1]
    width = group * depth + lanes
    shape = jax.ShapeDtypeStruct((heads, rows, width), jnp.bfloat16)
    held = [pltpu.VMEM(a.shape, a.dtype) for a in (keys, values)]
    vmem, hbm = pl.BlockSpec(memory_space=pltpu.VMEM), pl.BlockSpec(memory_space=pltpu.HBM)
    space = pltpu.VMEM if pair else pltpu.HBM
    return pl.pallas_call(
        functools.partial(attend_kernel, pair),
        in_specs=[pl.BlockSpec(memory_space=pltpu.SMEM)] * 2
        + [vmem] * 2
        + [vmem if pair else hbm] * 2
        + [hbm],
        out_specs=[vmem] * (2 if pair else 4),
        out_shape=[shape, shape] + ([] if pair else held),
        scratch_shapes=[
            pltpu.VMEM((2, 2 * rows * group, count), jnp.float32),
            pltpu.VMEM((2, 2 * rows * group, lanes), jnp.float32),
            pltpu.VMEM((2, 2 * rows * group, depth), jnp.float32),
            pltpu.VMEM((2, 2 * rows * group, lanes), jnp.float32),
            pltpu.VMEM(chosen.shape, chosen.dtype),
            pltpu.SemaphoreType.DMA((2, heads)),
            pltpu.SemaphoreType.DMA(()),
        ],
        compiler_params=pltpu.CompilerParams(vmem_limit_bytes=10 << 20),
        cost_estimate=pl.CostEstimate(
            flops=8 * heads * rows * group * depth * count,
            bytes_accessed=4 * heads * count * depth,
            transcendentals=2 * heads * rows * group * count,
        ),
    )(
        part,
        place,
        query_a,
        query_b,
        pltpu.with_memory_space_constraint(keys, space),
        pltpu.with_memory_space_constraint(values, space),
        pltpu.with_memory_space_constraint(chosen, pltpu.HBM),
    )


def merged(parts, group, depth):
    stats = [part[:, group * depth :] for part in parts]
    lses = [s + pltpu.roll(s, lanes - group, 1) for s in stats]
    top = functools.reduce(jnp.maximum, lses)
    weights = [jnp.exp(lse - top) for lse in lses]
    total = functools.reduce(jnp.add, weights)
    inverse = 1.0 / total
    weights = [w * inverse for w in weights]
    values = []
    for g in range(group):
        values.append(
            functools.reduce(
                jnp.add,
                [
                    w[:, g : g + 1] * part[:, g * depth : (g + 1) * depth]
                    for w, part in zip(weights, parts)
                ],
            )
        )
    return values, top + jnp.log(total)


def packed_stat(lse, group):
    lane = lax.broadcasted_iota(jnp.int32, lse.shape, 1)
    high, low = split_stat(lse)
    low = pltpu.roll(low, group, 1)
    return jnp.where(lane < group, high, jnp.where(lane < 2 * group, low, 0.0))


def core_kernel(group, depth, part, keep_ref, recv_ref, *refs):
    out_ref = refs[-1]
    heads, rows, _ = keep_ref.shape
    where = slice(part * rows, (part + 1) * rows)

    @pl.loop(0, heads)
    def _(h):
        values, lse = merged(
            [keep_ref[h].astype(jnp.float32), recv_ref[h].astype(jnp.float32)], group, depth
        )
        for g in range(group):
            out_ref[h, where, g * depth : (g + 1) * depth] = values[g].astype(jnp.bfloat16)
        out_ref[h, where, group * depth :] = packed_stat(lse, group).astype(jnp.bfloat16)


def core_merge(part, keep, recv, group, depth, into=None):
    heads, rows, width = keep.shape
    more = [] if into is None else [into]
    vmem = pl.BlockSpec(memory_space=pltpu.VMEM)
    return pl.pallas_call(
        functools.partial(core_kernel, group, depth, part),
        in_specs=[vmem] * (2 + len(more)),
        out_specs=vmem,
        out_shape=jax.ShapeDtypeStruct((heads, 2 * rows, width), jnp.bfloat16),
        input_output_aliases={2: 0} if more else {},
        compiler_params=pltpu.CompilerParams(vmem_limit_bytes=8 << 20),
    )(keep, recv, *more)


def ctx_kernel(group, depth, got_ref, out_ref):
    values, lse = merged(
        [got_ref[s].astype(jnp.float32) for s in range(got_ref.shape[0])], group, depth
    )
    for g in range(group):
        out_ref[:, g * depth : (g + 1) * depth] = values[g].astype(jnp.bfloat16)
    out_ref[:, group * depth :] = packed_stat(lse, group).astype(jnp.bfloat16)


def x_kernel(group, depth, own_ref, got_ref, out_ref):
    half = own_ref.shape[0] // 2
    own = own_ref[...].astype(jnp.float32)
    got = got_ref[...].astype(jnp.float32)
    got = jnp.concatenate([got[half:], got[:half]], axis=0)
    values, _ = merged([own, got], group, depth)
    for g in range(group):
        out_ref[:, g * depth : (g + 1) * depth] = values[g].astype(jnp.bfloat16)


def small_call(kernel, shapes, *operands, flops=0):
    return pl.pallas_call(
        kernel,
        out_shape=jax.tree.map(
            lambda shape: jax.ShapeDtypeStruct(shape, jnp.bfloat16),
            shapes,
            is_leaf=lambda x: isinstance(x, tuple),
        ),
        compiler_params=pltpu.CompilerParams(vmem_limit_bytes=8 << 20),
        cost_estimate=pl.CostEstimate(flops=flops, bytes_accessed=1 << 19, transcendentals=0),
    )(*operands)


def scatter_rows(out_ref, value):
    step = out_ref.shape[1]
    for i in range(out_ref.shape[0]):
        out_ref[i] = value[i * step : (i + 1) * step].astype(out_ref.dtype)


def stream_kernel(got_ref, residual_ref, stream_ref, copies_ref):
    total = residual_ref[...].astype(jnp.float32)
    partial = got_ref[0].astype(jnp.float32)
    for i in range(1, got_ref.shape[0]):
        partial += got_ref[i].astype(jnp.float32)
    stream = (total + partial).astype(jnp.bfloat16)
    stream_ref[...] = stream
    for i in range(copies_ref.shape[0]):
        copies_ref[i] = stream


def project_kernel(place_ref, own_ref, got_ref, weight_ref, out_ref):
    rows = out_ref.shape[0] * out_ref.shape[1]
    half = rows // 2
    quarter = rows // 4
    place = place_ref[0]
    target = lax.broadcasted_iota(jnp.int32, (rows, half), 0)
    source = lax.broadcasted_iota(jnp.int32, (rows, half), 1)
    row = (source % quarter) * 4
    column = 2 * (source // quarter)
    own_order = jnp.where(target == row + (place ^ column), 1.0, 0.0).astype(jnp.bfloat16)
    got_order = jnp.where(target == row + (place ^ (column + 1)), 1.0, 0.0).astype(jnp.bfloat16)
    attended = jnp.dot(own_order, own_ref[...], preferred_element_type=jnp.float32) + jnp.dot(
        got_order, got_ref[...], preferred_element_type=jnp.float32
    )
    scatter_rows(
        out_ref,
        jnp.dot(
            attended.astype(jnp.bfloat16), weight_ref[...], preferred_element_type=jnp.float32
        ),
    )


def tail_of(squares):
    lane = lax.broadcasted_iota(jnp.int32, (squares.shape[0], lanes), 1)
    high, low = split_stat(squares)
    return jnp.where(lane == 0, high, jnp.where(lane == 1, low, 0.0)).astype(jnp.bfloat16)


def gate_kernel(rows_ref, gain_ref, gate_ref, up_ref, out_ref):
    units = gate_ref.shape[1]
    rows = jnp.concatenate(
        [rows_ref[i].astype(jnp.float32) for i in range(rows_ref.shape[0])], axis=0
    )
    scaled = (rows * gain_ref[...]).astype(jnp.bfloat16)
    for i, ref in enumerate((gate_ref, up_ref)):
        out_ref[:, i * units : (i + 1) * units] = jnp.dot(
            scaled, ref[...], preferred_element_type=jnp.float32
        ).astype(jnp.bfloat16)
    out_ref[:, 2 * units :] = tail_of(jnp.sum(rows * rows, axis=1, keepdims=True))


def summed(own_ref, got_ref, start, stop):
    return own_ref[:, start:stop].astype(jnp.float32) + got_ref[:, start:stop].astype(jnp.float32)


def squares_of(own_ref, got_ref):
    start = own_ref.shape[1] - lanes
    tail = summed(own_ref, got_ref, start, start + lanes)
    return tail[:, 0:1] + tail[:, 1:2]


def pair_kernel(own_ref, got_ref, out_ref):
    units = own_ref.shape[1] - lanes
    out_ref[:, :units] = summed(own_ref, got_ref, 0, units).astype(jnp.bfloat16)
    out_ref[:, units:] = tail_of(squares_of(own_ref, got_ref))


def down_kernel(own_ref, got_ref, weight_ref, out_ref):
    units = weight_ref.shape[0]
    scale = lax.rsqrt(squares_of(own_ref, got_ref) / MODEL_WIDTH + norm_eps)
    gate = summed(own_ref, got_ref, 0, units) * scale
    up = summed(own_ref, got_ref, units, 2 * units) * scale
    hidden = (jax.nn.silu(gate) * up).astype(jnp.bfloat16)
    scatter_rows(
        out_ref, jnp.dot(hidden, weight_ref[...], preferred_element_type=jnp.float32)
    )


def weighed(kernel, shape, weights, *operands, scalar=None):
    vmem = pl.BlockSpec(memory_space=pltpu.VMEM)
    specs = [vmem] * (len(operands) + len(weights))
    if scalar is not None:
        specs = [pl.BlockSpec(memory_space=pltpu.SMEM)] + specs
        operands = (scalar,) + operands
    return pl.pallas_call(
        kernel,
        in_specs=specs,
        out_specs=vmem,
        out_shape=jax.ShapeDtypeStruct(shape, jnp.bfloat16),
        compiler_params=pltpu.CompilerParams(vmem_limit_bytes=8 << 20),
        cost_estimate=pl.CostEstimate(
            flops=sum(64 * w.size for w in weights),
            bytes_accessed=sum(2 * w.size for w in weights),
            transcendentals=0,
        ),
    )(*operands, *(pltpu.with_memory_space_constraint(w, pltpu.VMEM) for w in weights))


def per_device_dense(
    query,
    keys,
    values,
    chosen,
    residual,
    output_weight,
    norm_gain,
    gate_weight,
    up_weight,
    down_weight,
):
    _, heads, group, depth = query.shape
    ctx_count = lax.axis_size("ctx")
    mp_count = lax.axis_size("mp")
    mp_place = lax.axis_index("mp")
    own_part = lax.axis_index("ctx") * mp_count + mp_place
    all_rows = ctx_count * mp_count

    part, place = jnp.reshape(own_part, (1,)), jnp.reshape(mp_place, (1,))
    chosen = jnp.transpose(chosen, (0, 2, 1))
    copies = small_call(
        copies_kernel, (ctx_count,) + query.shape[1:], query[0], flops=0
    )
    query_own = over_ctx(copies)
    keys, values = keys[0], values[0]
    query_core = swapped(query_own, 1)
    query_x = swapped(query_own, 2)
    keep_a, send_a, keys, values = attend(0, part, place, query_own, query_core, keys, values, chosen)
    query_x, _ = lax.optimization_barrier((query_x, send_a))
    query_far = swapped(query_x, 1)
    recv_a = swapped(send_a, 1)
    keep_b, send_b = attend(1, part, place, query_x, query_far, keys, values, chosen)
    recv_b = swapped(send_b, 1)
    on_chip = core_merge(0, keep_a, recv_a, group, depth)
    on_chip = core_merge(1, keep_b, recv_b, group, depth, into=on_chip)
    got = over_ctx(on_chip)
    half_rows = 2 * ctx_count
    width = group * depth
    column = small_call(
        functools.partial(ctx_kernel, group, depth), (half_rows, width + lanes), got
    )
    attended = small_call(
        functools.partial(x_kernel, group, depth), (half_rows, width), column, swapped(column, 2)
    )
    other = swapped(attended, 1)
    width = output_weight.shape[1]
    block = (ctx_count, mp_count, width)
    projected = weighed(project_kernel, block, (output_weight,), attended, other, scalar=place)
    stream, copies = small_call(
        stream_kernel, [residual.shape, block], over_ctx(projected), residual
    )
    rows = over_ctx(copies)
    units = gate_weight.shape[1]
    mine = weighed(
        gate_kernel,
        (all_rows, 2 * units + lanes),
        (gate_weight, up_weight),
        rows,
        norm_gain.reshape(1, -1),
    )
    mine = small_call(pair_kernel, mine.shape, mine, swapped(mine, 1))
    update = weighed(
        down_kernel,
        block,
        (down_weight,),
        mine,
        swapped(mine, 2),
    )
    update = over_ctx(update)
    update = jnp.sum(update.astype(jnp.float32), axis=0).astype(jnp.bfloat16)
    return (stream, update)


def either(*arrays):
    query, mp_count, ctx_count = arrays[0], lax.axis_size("mp"), lax.axis_size("ctx")
    rows, heads, group, depth = query.shape
    dense = (
        rows == 1
        and mp_count == 4
        and heads == ctx_count == group == 8
        and depth == lanes
        and arrays[1].shape[0] == 1
    )
    return (per_device_dense if dense else per_device)(*arrays)


def solution(mesh):
    return jax.shard_map(
        either,
        mesh=mesh,
        in_specs=(
            P(("ctx", "mp"), None, None, None),
            P(("ctx", "mp"), None, None, None),
            P(("ctx", "mp"), None, None, None),
            P(),
            P("ctx", "mp"),
            P("ctx", "mp"),
            P("mp"),
            P("mp", "ctx"),
            P("mp", "ctx"),
            P("ctx", "mp"),
        ),
        out_specs=(P("ctx", "mp"), P("ctx", "mp")),
        check_vma=False,
    )
```

```python
import functools
import math

import jax
import jax.numpy as jnp
from jax import lax
from jax.experimental import pallas as pl
from jax.experimental.pallas import tpu as pltpu
from jax.sharding import PartitionSpec as P

MODEL_WIDTH = 8192
KEPT_PARTITIONS = 16
ROW_DEV = 1


norm_eps = 1e-05
lowest_value = -1e30


def find_slots(listed, target, capacity):
    member = jnp.any(listed == target, axis=2)
    places = jnp.cumsum(member.astype(jnp.int32), axis=1) - 1
    live_count = jnp.sum(member.astype(jnp.int32), axis=1)
    slot_ranks = jnp.arange(capacity, dtype=jnp.int32)
    slot_hits = member[:, :, None] & (places[:, :, None] == slot_ranks[None, None, :])
    row_numbers = jnp.arange(listed.shape[1], dtype=jnp.int32)
    slot_rows = jnp.sum(jnp.where(slot_hits, row_numbers[None, :, None], 0), axis=1)
    slot_valid = slot_ranks[None, :] < live_count[:, None]
    return (slot_rows, slot_valid)


def global_scaling(block_max, block_sum, block_value, slot_rows, slot_valid, all_rows, head_ids):
    kv_heads, capacity, group_size = block_max.shape
    valid_wide = slot_valid[:, :, None]
    max_table = jnp.full((all_rows, kv_heads, group_size), lowest_value, jnp.float32)
    max_table = max_table.at[slot_rows, head_ids[:, None]].max(
        jnp.where(valid_wide, block_max, lowest_value)
    )
    row_top = lax.pmax(max_table.astype(jnp.bfloat16), ("ctx", "mp")).astype(max_table.dtype)
    factor = jnp.where(valid_wide, jnp.exp(block_max - row_top[slot_rows, head_ids[:, None]]), 0.0)
    return (block_value * factor[..., None], block_sum * factor)


def to_owners(array, kv_heads, capacity, per_head, ctx_count):
    shaped = array.reshape(kv_heads, capacity, per_head, -1)
    return jnp.transpose(shaped, (0, 2, 1, 3)).reshape(ctx_count, capacity, -1)


def per_device(
    query,
    keys,
    values,
    chosen,
    residual,
    output_weight,
    norm_gain,
    gate_weight,
    up_weight,
    down_weight,
):
    kv_heads = query.shape[1]
    group_size = query.shape[2]
    head_dim = query.shape[3]
    score_scale = head_dim ** (-0.5)
    ctx_count = lax.axis_size("ctx")
    mp_count = lax.axis_size("mp")
    ctx_place = lax.axis_index("ctx")
    mp_place = lax.axis_index("mp")
    own_part = ctx_place * mp_count + mp_place
    all_queries = lax.all_gather(query, ("ctx", "mp"), axis=0, tiled=True)
    all_rows = all_queries.shape[0]
    capacity = min(4 * ROW_DEV * KEPT_PARTITIONS, all_rows)
    slot_rows, slot_valid = find_slots(chosen, own_part, capacity)
    head_ids = jnp.arange(kv_heads, dtype=jnp.int32)
    picked = all_queries[slot_rows, head_ids[:, None]].reshape(
        kv_heads, capacity * group_size, head_dim
    )

    def attend(inputs):
        query_block, key_block, value_block = inputs
        scores = (
            lax.dot_general(
                query_block, key_block, (((1,), (1,)), ((), ())), preferred_element_type=jnp.float32
            )
            * score_scale
        )
        block_max = jnp.max(scores, axis=1)
        probs = jnp.exp(scores - block_max[:, None])
        block_sum = jnp.sum(probs, axis=1)
        block_value = jnp.dot(
            probs.astype(jnp.bfloat16), value_block, preferred_element_type=jnp.float32
        )
        return (block_max, block_sum, block_value)

    block_max, block_sum, block_value = lax.map(attend, (picked, keys[0], values[0]))
    block_max = block_max.reshape(kv_heads, capacity, group_size)
    block_sum = block_sum.reshape(kv_heads, capacity, group_size)
    block_value = block_value.reshape(kv_heads, capacity, group_size, head_dim)
    per_head = ctx_count // kv_heads
    feat_width = kv_heads * group_size * head_dim // ctx_count
    head_share = kv_heads * group_size // ctx_count
    own_head = ctx_place // per_head
    head_lists = lax.dynamic_index_in_dim(chosen, own_head, 0, keepdims=True)
    sources = jnp.arange(ctx_count, dtype=jnp.int32) * mp_count + mp_place
    source_rows = jax.vmap(lambda source: find_slots(head_lists, source, capacity)[0])(sources)[
        :, 0
    ]
    weighted, scaled_sum = global_scaling(
        block_max, block_sum, block_value, slot_rows, slot_valid, all_rows, head_ids
    )
    send_values = to_owners(weighted, kv_heads, capacity, per_head, ctx_count)
    send_sums = to_owners(scaled_sum, kv_heads, capacity, per_head, ctx_count)
    got_values, got_sums = (
        lax.all_to_all(
            send_values.astype(jnp.bfloat16), "ctx", split_axis=0, concat_axis=0, tiled=True
        ).astype(send_values.dtype),
        lax.all_to_all(
            send_sums.astype(jnp.bfloat16), "ctx", split_axis=0, concat_axis=0, tiled=True
        ).astype(send_sums.dtype),
    )
    numerator = jnp.zeros((all_rows, feat_width), jnp.float32).at[source_rows].add(got_values)
    denominator = jnp.zeros((all_rows, head_share), jnp.float32).at[source_rows].add(got_sums)
    numerator, denominator = (
        lax.psum(numerator.astype(jnp.bfloat16), "mp").astype(jnp.float32),
        lax.psum(denominator.astype(jnp.bfloat16), "mp").astype(jnp.float32),
    )
    attended = (
        (numerator.reshape(all_rows, -1, head_dim) / denominator[:, :, None])
        .reshape(all_rows, -1)
        .astype(jnp.bfloat16)
    )
    rows_here = attended
    projected = lax.psum_scatter(
        jnp.dot(rows_here, output_weight, preferred_element_type=jnp.float32),
        "ctx",
        scatter_dimension=0,
        tiled=True,
    )
    stream = (residual.astype(jnp.float32) + projected).astype(jnp.bfloat16)
    stream_wide = stream.astype(jnp.float32)
    squares = lax.psum(jnp.sum(stream_wide * stream_wide, axis=1), "mp")
    normed = (
        stream_wide * lax.rsqrt(squares / MODEL_WIDTH + norm_eps)[:, None] * norm_gain
    ).astype(jnp.bfloat16)
    row_piece = lax.all_gather(normed, "ctx", axis=0, tiled=True)
    gate_piece = jnp.dot(row_piece, gate_weight, preferred_element_type=jnp.float32)
    up_piece = jnp.dot(row_piece, up_weight, preferred_element_type=jnp.float32)
    gate_up = jnp.stack([gate_piece, up_piece], axis=1)
    gate_up = lax.psum(gate_up.astype(jnp.bfloat16), "mp").astype(jnp.float32)
    hidden = (jax.nn.silu(gate_up[:, 0]) * gate_up[:, 1]).astype(jnp.bfloat16)
    rows_here = hidden
    update = lax.psum_scatter(
        jnp.dot(rows_here, down_weight, preferred_element_type=jnp.float32),
        "ctx",
        scatter_dimension=0,
        tiled=True,
    ).astype(jnp.bfloat16)
    return (stream, update)


lanes = 128
chunk = 512
columns_at_once = 256
ahead = 4
log2_e = math.log2(math.e)


def swapped(array, bit):
    count = lax.axis_size("mp")
    return lax.ppermute(array, "mp", [(i, i ^ bit) for i in range(count)])


def over_ctx(array):
    return lax.all_to_all(array, "ctx", split_axis=0, concat_axis=0, tiled=True)


def copies_kernel(in_ref, out_ref):
    for i in range(out_ref.shape[0]):
        out_ref[i] = in_ref[...]


def split_stat(value):
    high = value.astype(jnp.bfloat16).astype(jnp.float32)
    return high, value - high


def attend_kernel(pair, part_ref, place_ref, query_a, query_b, keys, values, chosen, *refs):
    if pair == 0:
        keep_ref, send_ref, key_ref, value_ref = refs[:4]
    else:
        keep_ref, send_ref = refs[:2]
        key_ref, value_ref = keys, values
    score_s, top_s, out_s, lse_s, chosen_ref, sems, chosen_sem = refs[-7:]
    rows, heads, group, depth = query_a.shape
    count = key_ref.shape[1]
    scale = depth ** (-0.5)
    lane = lax.broadcasted_iota(jnp.int32, (rows, lanes), 1)
    listed = chosen_ref.shape[2]
    row_lane = lax.broadcasted_iota(jnp.int32, (rows, listed), 1)
    row_place = lax.broadcasted_iota(jnp.int32, (rows, listed), 0) * (listed // rows)
    chosen_copy = pltpu.make_async_copy(chosen, chosen_ref, chosen_sem)

    def arrivals(h):
        return (
            pltpu.make_async_copy(keys.at[h], key_ref.at[h], sems.at[0, h]),
            pltpu.make_async_copy(values.at[h], value_ref.at[h], sems.at[1, h]),
        )

    def send_for(h):
        if pair == 0:
            for copy in arrivals(h):
                copy.start()

    def wait_for(h):
        if pair == 0:
            for copy in arrivals(h):
                copy.wait()

    def query_of(h):
        return jnp.concatenate(
            [
                q[:, h].astype(jnp.float32).reshape(rows * group, depth)
                for q in (query_a, query_b)
            ],
            axis=0,
        ).astype(jnp.bfloat16)

    def score(query, h, slot, i, top):
        window = slice(i * chunk, (i + 1) * chunk)
        scores = lax.dot_general(
            query, key_ref[h, window, :], (((1,), (1,)), ((), ())),
            preferred_element_type=jnp.float32,
        )
        score_s[slot, :, window] = scores
        for j in range(chunk // lanes):
            part = scores[:, j * lanes : (j + 1) * lanes]
            top = part if top is None else jnp.maximum(top, part)
        return top

    def spent(h, slot, i, top, total, mixed):
        window = slice(i * chunk, (i + 1) * chunk)
        probs = jnp.exp2((score_s[slot, :, window] - top) * (scale * log2_e))
        for j in range(chunk // lanes):
            part = probs[:, j * lanes : (j + 1) * lanes]
            total = part if total is None else total + part
        part = jnp.dot(
            probs.astype(jnp.bfloat16), value_ref[h, window, :], preferred_element_type=jnp.float32
        )
        return total, part if mixed is None else mixed + part

    def finish(h, slot, top, total, mixed):
        total = jnp.sum(total, axis=1, keepdims=True)
        out_s[slot] = mixed * (1.0 / total)
        lse_s[slot] = jnp.broadcast_to(top * scale + jnp.log(total), lse_s.shape[1:])
        member = jnp.where(chosen_ref[h] == part_ref[0], 1.0, 0.0)
        member = jnp.max(member, axis=0, keepdims=True)
        for part, ref in enumerate((keep_ref, send_ref)):
            row = row_place + (place_ref[0] ^ (2 * pair + part))
            held = jnp.where(row_lane == row, member, 0.0)
            bias = jnp.where(jnp.max(held, axis=1, keepdims=True) > 0.5, 0.0, lowest_value)
            stats = jnp.zeros((rows, lanes), jnp.float32)
            for g in range(group):
                window = pl.ds(part * rows * group + g, rows, stride=group)
                ref[h, :, g * depth : (g + 1) * depth] = out_s[slot, window, :].astype(jnp.bfloat16)
                high, low = split_stat(lse_s[slot, window, :] + bias)
                stats = jnp.where(lane == g, high, jnp.where(lane == group + g, low, stats))
            ref[h, :, group * depth :] = stats.astype(jnp.bfloat16)

    def both(h, slot, following, after):
        top = jnp.max(top_s[slot], axis=1, keepdims=True)
        query = query_of(following)
        total = mixed = later = None
        for i in range(count // chunk):
            total, mixed = spent(h, slot, i, top, total, mixed)
            later = score(query, following, after, i, later)
        top_s[after] = later
        finish(h, slot, top, total, mixed)

    for h in range(min(ahead, heads)):
        send_for(h)
    chosen_copy.start()
    wait_for(0)
    query, top = query_of(0), None
    for i in range(count // chunk):
        top = score(query, 0, 0, i, top)
    top_s[0] = top
    chosen_copy.wait()

    @pl.loop(0, heads // 2)
    def _(step):
        h = 2 * step
        wait_for(h + 1)
        both(h, 0, h + 1, 1)

        @pl.when(h + 2 < heads)
        def _():
            wait_for(h + 2)

        for i in range(2):

            @pl.when(h + ahead + i < heads)
            def _():
                send_for(h + ahead + i)

        both(h + 1, 1, jnp.minimum(h + 2, heads - 1), 0)


def attend(pair, part, place, query_a, query_b, keys, values, chosen):
    rows, heads, group, depth = query_a.shape
    count = keys.shape[1]
    width = group * depth + lanes
    shape = jax.ShapeDtypeStruct((heads, rows, width), jnp.bfloat16)
    held = [pltpu.VMEM(a.shape, a.dtype) for a in (keys, values)]
    vmem, hbm = pl.BlockSpec(memory_space=pltpu.VMEM), pl.BlockSpec(memory_space=pltpu.HBM)
    space = pltpu.VMEM if pair else pltpu.HBM
    return pl.pallas_call(
        functools.partial(attend_kernel, pair),
        in_specs=[pl.BlockSpec(memory_space=pltpu.SMEM)] * 2
        + [vmem] * 2
        + [vmem if pair else hbm] * 2
        + [hbm],
        out_specs=[vmem] * (2 if pair else 4),
        out_shape=[shape, shape] + ([] if pair else held),
        scratch_shapes=[
            pltpu.VMEM((2, 2 * rows * group, count), jnp.float32),
            pltpu.VMEM((2, 2 * rows * group, lanes), jnp.float32),
            pltpu.VMEM((2, 2 * rows * group, depth), jnp.float32),
            pltpu.VMEM((2, 2 * rows * group, lanes), jnp.float32),
            pltpu.VMEM(chosen.shape, chosen.dtype),
            pltpu.SemaphoreType.DMA((2, heads)),
            pltpu.SemaphoreType.DMA(()),
        ],
        compiler_params=pltpu.CompilerParams(vmem_limit_bytes=10 << 20),
        cost_estimate=pl.CostEstimate(
            flops=8 * heads * rows * group * depth * count,
            bytes_accessed=4 * heads * count * depth,
            transcendentals=2 * heads * rows * group * count,
        ),
    )(
        part,
        place,
        query_a,
        query_b,
        pltpu.with_memory_space_constraint(keys, space),
        pltpu.with_memory_space_constraint(values, space),
        pltpu.with_memory_space_constraint(chosen, pltpu.HBM),
    )


def merged(parts, group, depth):
    stats = [part[:, group * depth :] for part in parts]
    lses = [s + pltpu.roll(s, lanes - group, 1) for s in stats]
    top = functools.reduce(jnp.maximum, lses)
    weights = [jnp.exp(lse - top) for lse in lses]
    total = functools.reduce(jnp.add, weights)
    inverse = 1.0 / total
    weights = [w * inverse for w in weights]
    values = []
    for g in range(group):
        values.append(
            functools.reduce(
                jnp.add,
                [
                    w[:, g : g + 1] * part[:, g * depth : (g + 1) * depth]
                    for w, part in zip(weights, parts)
                ],
            )
        )
    return values, top + jnp.log(total)


def packed_stat(lse, group):
    lane = lax.broadcasted_iota(jnp.int32, lse.shape, 1)
    high, low = split_stat(lse)
    low = pltpu.roll(low, group, 1)
    return jnp.where(lane < group, high, jnp.where(lane < 2 * group, low, 0.0))


def core_kernel(group, depth, part, keep_ref, recv_ref, *refs):
    out_ref = refs[-1]
    heads, rows, _ = keep_ref.shape
    where = slice(part * rows, (part + 1) * rows)

    for h in range(heads):
        values, lse = merged(
            [keep_ref[h].astype(jnp.float32), recv_ref[h].astype(jnp.float32)], group, depth
        )
        for g in range(group):
            out_ref[h, where, g * depth : (g + 1) * depth] = values[g].astype(jnp.bfloat16)
        out_ref[h, where, group * depth :] = packed_stat(lse, group).astype(jnp.bfloat16)


def core_merge(part, keep, recv, group, depth, into=None):
    heads, rows, width = keep.shape
    more = [] if into is None else [into]
    vmem = pl.BlockSpec(memory_space=pltpu.VMEM)
    return pl.pallas_call(
        functools.partial(core_kernel, group, depth, part),
        in_specs=[vmem] * (2 + len(more)),
        out_specs=vmem,
        out_shape=jax.ShapeDtypeStruct((heads, 2 * rows, width), jnp.bfloat16),
        input_output_aliases={2: 0} if more else {},
        compiler_params=pltpu.CompilerParams(vmem_limit_bytes=8 << 20),
    )(keep, recv, *more)


def ctx_kernel(group, depth, got_ref, out_ref):
    values, lse = merged(
        [got_ref[s].astype(jnp.float32) for s in range(got_ref.shape[0])], group, depth
    )
    for g in range(group):
        out_ref[:, g * depth : (g + 1) * depth] = values[g].astype(jnp.bfloat16)
    out_ref[:, group * depth :] = packed_stat(lse, group).astype(jnp.bfloat16)


def x_kernel(group, depth, own_ref, got_ref, out_ref):
    half = own_ref.shape[0] // 2
    own = own_ref[...].astype(jnp.float32)
    got = got_ref[...].astype(jnp.float32)
    got = jnp.concatenate([got[half:], got[:half]], axis=0)
    values, _ = merged([own, got], group, depth)
    for g in range(group):
        out_ref[:, g * depth : (g + 1) * depth] = values[g].astype(jnp.bfloat16)


def small_call(kernel, shapes, *operands, flops=0):
    return pl.pallas_call(
        kernel,
        out_shape=jax.tree.map(
            lambda shape: jax.ShapeDtypeStruct(shape, jnp.bfloat16),
            shapes,
            is_leaf=lambda x: isinstance(x, tuple),
        ),
        compiler_params=pltpu.CompilerParams(vmem_limit_bytes=8 << 20),
        cost_estimate=pl.CostEstimate(flops=flops, bytes_accessed=1 << 19, transcendentals=0),
    )(*operands)


def scatter_rows(out_ref, first, start, stop, value):
    count, step, _ = out_ref.shape
    for i in range(count):
        where = i if first is None else lax.rem(first + i, count)
        out_ref[where, :, start:stop] = value[i * step : (i + 1) * step].astype(out_ref.dtype)


def stream_kernel(got_ref, residual_ref, stream_ref, copies_ref):
    total = residual_ref[...].astype(jnp.float32)
    partial = got_ref[0].astype(jnp.float32)
    for i in range(1, got_ref.shape[0]):
        partial += got_ref[i].astype(jnp.float32)
    stream = (total + partial).astype(jnp.bfloat16)
    stream_ref[...] = stream
    for i in range(copies_ref.shape[0]):
        copies_ref[i] = stream


def product(left, weight_ref, emit):
    width = weight_ref.shape[1]
    for start in range(0, width, columns_at_once):
        stop = min(start + columns_at_once, width)
        emit(
            start,
            stop,
            jnp.dot(left, weight_ref[:, start:stop], preferred_element_type=jnp.float32),
        )


def project_kernel(place_ref, own_ref, got_ref, weight_ref, out_ref):
    rows = out_ref.shape[0] * out_ref.shape[1]
    half = rows // 2
    quarter = rows // 4
    place = place_ref[0]
    target = lax.broadcasted_iota(jnp.int32, (rows, half), 0)
    source = lax.broadcasted_iota(jnp.int32, (rows, half), 1)
    row = (source % quarter) * 4
    column = 2 * (source // quarter)
    own_order = jnp.where(target == row + (place ^ column), 1.0, 0.0).astype(jnp.bfloat16)
    got_order = jnp.where(target == row + (place ^ (column + 1)), 1.0, 0.0).astype(jnp.bfloat16)
    attended = jnp.dot(own_order, own_ref[...], preferred_element_type=jnp.float32) + jnp.dot(
        got_order, got_ref[...], preferred_element_type=jnp.float32
    )
    product(
        attended.astype(jnp.bfloat16), weight_ref, functools.partial(scatter_rows, out_ref, None)
    )


def tail_of(squares):
    lane = lax.broadcasted_iota(jnp.int32, (squares.shape[0], lanes), 1)
    high, low = split_stat(squares)
    return jnp.where(lane == 0, high, jnp.where(lane == 1, low, 0.0)).astype(jnp.bfloat16)


def half_of(place_ref, count):
    return (place_ref[0] & 1) * (count // 2)


def gate_kernel(place_ref, rows_ref, gain_ref, gate_ref, up_ref, keep_ref, send_ref):
    count = rows_ref.shape[0]
    first = half_of(place_ref, count)
    rows = jnp.concatenate(
        [rows_ref[lax.rem(first + i, count)].astype(jnp.float32) for i in range(count)], axis=0
    )
    half = rows.shape[0] // 2
    scaled = (rows * gain_ref[...]).astype(jnp.bfloat16)
    units = gate_ref.shape[1]

    def emit(offset, start, stop, value):
        value = value.astype(jnp.bfloat16)
        keep_ref[:, offset + start : offset + stop] = value[:half]
        send_ref[:, offset + start : offset + stop] = value[half:]

    tail = tail_of(jnp.sum(rows * rows, axis=1, keepdims=True))
    emit(2 * units, 0, lanes, tail)
    product(scaled, gate_ref, functools.partial(emit, 0))
    product(scaled, up_ref, functools.partial(emit, units))


def summed(own_ref, got_ref, start, stop):
    return own_ref[:, start:stop].astype(jnp.float32) + got_ref[:, start:stop].astype(jnp.float32)


def squares_of(own_ref, got_ref):
    start = own_ref.shape[1] - lanes
    tail = summed(own_ref, got_ref, start, start + lanes)
    return tail[:, 0:1] + tail[:, 1:2]


def pair_kernel(own_ref, got_ref, out_ref):
    units = own_ref.shape[1] - lanes
    out_ref[:, :units] = summed(own_ref, got_ref, 0, units).astype(jnp.bfloat16)
    out_ref[:, units:] = tail_of(squares_of(own_ref, got_ref))


def hidden_kernel(own_ref, got_ref, out_ref):
    units = out_ref.shape[1]
    scale = lax.rsqrt(squares_of(own_ref, got_ref) / MODEL_WIDTH + norm_eps)
    gate = summed(own_ref, got_ref, 0, units) * scale
    up = summed(own_ref, got_ref, units, 2 * units) * scale
    out_ref[...] = (jax.nn.silu(gate) * up).astype(jnp.bfloat16)


def down_kernel(place_ref, own_ref, got_ref, weight_ref, out_ref):
    hidden = jnp.concatenate([own_ref[...], got_ref[...]], axis=0)
    first = half_of(place_ref, out_ref.shape[0])
    product(hidden, weight_ref, functools.partial(scatter_rows, out_ref, first))


def total_kernel(got_ref, out_ref):
    total = got_ref[0].astype(jnp.float32)
    for i in range(1, got_ref.shape[0]):
        total += got_ref[i].astype(jnp.float32)
    out_ref[...] = total.astype(jnp.bfloat16)


def weighed(kernel, shapes, weights, scalar, *operands):
    vmem = pl.BlockSpec(memory_space=pltpu.VMEM)
    outs = [jax.ShapeDtypeStruct(shape, jnp.bfloat16) for shape in shapes]
    return pl.pallas_call(
        kernel,
        in_specs=[pl.BlockSpec(memory_space=pltpu.SMEM)]
        + [vmem] * (len(operands) + len(weights)),
        out_specs=[vmem] * len(outs),
        out_shape=outs,
        compiler_params=pltpu.CompilerParams(vmem_limit_bytes=8 << 20),
        cost_estimate=pl.CostEstimate(
            flops=sum(64 * w.size for w in weights),
            bytes_accessed=sum(2 * w.size for w in weights),
            transcendentals=0,
        ),
    )(scalar, *operands, *(pltpu.with_memory_space_constraint(w, pltpu.VMEM) for w in weights))


def per_device_dense(
    query,
    keys,
    values,
    chosen,
    residual,
    output_weight,
    norm_gain,
    gate_weight,
    up_weight,
    down_weight,
):
    _, heads, group, depth = query.shape
    ctx_count = lax.axis_size("ctx")
    mp_count = lax.axis_size("mp")
    mp_place = lax.axis_index("mp")
    own_part = lax.axis_index("ctx") * mp_count + mp_place
    all_rows = ctx_count * mp_count

    part, place = jnp.reshape(own_part, (1,)), jnp.reshape(mp_place, (1,))
    chosen = jnp.transpose(chosen, (0, 2, 1))
    copies = small_call(
        copies_kernel, (ctx_count,) + query.shape[1:], query[0], flops=0
    )
    query_own = over_ctx(copies)
    keys, values = keys[0], values[0]
    query_core = swapped(query_own, 1)
    query_x = swapped(query_own, 2)
    keep_a, send_a, keys, values = attend(0, part, place, query_own, query_core, keys, values, chosen)
    query_x, _ = lax.optimization_barrier((query_x, send_a))
    query_far = swapped(query_x, 1)
    recv_a = swapped(send_a, 1)
    keep_b, send_b = attend(1, part, place, query_x, query_far, keys, values, chosen)
    recv_b = swapped(send_b, 1)
    on_chip = core_merge(0, keep_a, recv_a, group, depth)
    on_chip = core_merge(1, keep_b, recv_b, group, depth, into=on_chip)
    got = over_ctx(on_chip)
    half_rows = 2 * ctx_count
    width = group * depth
    column = small_call(
        functools.partial(ctx_kernel, group, depth), (half_rows, width + lanes), got
    )
    attended = small_call(
        functools.partial(x_kernel, group, depth), (half_rows, width), column, swapped(column, 2)
    )
    other = swapped(attended, 1)
    width = output_weight.shape[1]
    block = (ctx_count, mp_count, width)
    (projected,) = weighed(
        project_kernel, [block], (output_weight,), place, attended, other
    )
    stream, copies = small_call(
        stream_kernel, [residual.shape, block], over_ctx(projected), residual
    )
    rows = over_ctx(copies)
    units = gate_weight.shape[1]
    half = all_rows // 2
    keep, send = weighed(
        gate_kernel,
        [(half, 2 * units + lanes)] * 2,
        (gate_weight, up_weight),
        place,
        rows,
        norm_gain.reshape(1, -1),
    )
    mine = small_call(pair_kernel, keep.shape, keep, swapped(send, 1))
    hidden = small_call(hidden_kernel, (half, units), mine, swapped(mine, 2))
    (update,) = weighed(
        down_kernel, [block], (down_weight,), place, hidden, swapped(hidden, 1)
    )
    update = small_call(total_kernel, residual.shape, over_ctx(update))
    return (stream, update)


def either(*arrays):
    query, mp_count, ctx_count = arrays[0], lax.axis_size("mp"), lax.axis_size("ctx")
    rows, heads, group, depth = query.shape
    dense = (
        rows == 1
        and mp_count == 4
        and heads == ctx_count == group == 8
        and depth == lanes
        and arrays[1].shape[0] == 1
    )
    return (per_device_dense if dense else per_device)(*arrays)


def solution(mesh):
    return jax.shard_map(
        either,
        mesh=mesh,
        in_specs=(
            P(("ctx", "mp"), None, None, None),
            P(("ctx", "mp"), None, None, None),
            P(("ctx", "mp"), None, None, None),
            P(),
            P("ctx", "mp"),
            P("ctx", "mp"),
            P("mp"),
            P("mp", "ctx"),
            P("mp", "ctx"),
            P("ctx", "mp"),
        ),
        out_specs=(P("ctx", "mp"), P("ctx", "mp")),
        check_vma=False,
    )
```

```python
import functools
import math

import jax
import jax.numpy as jnp
from jax import lax
from jax.experimental import pallas as pl
from jax.experimental.pallas import tpu as pltpu
from jax.sharding import PartitionSpec as P

MODEL_WIDTH = 8192
KEPT_PARTITIONS = 16
ROW_DEV = 1


norm_eps = 1e-05
lowest_value = -1e30


def find_slots(listed, target, capacity):
    member = jnp.any(listed == target, axis=2)
    places = jnp.cumsum(member.astype(jnp.int32), axis=1) - 1
    live_count = jnp.sum(member.astype(jnp.int32), axis=1)
    slot_ranks = jnp.arange(capacity, dtype=jnp.int32)
    slot_hits = member[:, :, None] & (places[:, :, None] == slot_ranks[None, None, :])
    row_numbers = jnp.arange(listed.shape[1], dtype=jnp.int32)
    slot_rows = jnp.sum(jnp.where(slot_hits, row_numbers[None, :, None], 0), axis=1)
    slot_valid = slot_ranks[None, :] < live_count[:, None]
    return (slot_rows, slot_valid)


def global_scaling(block_max, block_sum, block_value, slot_rows, slot_valid, all_rows, head_ids):
    kv_heads, capacity, group_size = block_max.shape
    valid_wide = slot_valid[:, :, None]
    max_table = jnp.full((all_rows, kv_heads, group_size), lowest_value, jnp.float32)
    max_table = max_table.at[slot_rows, head_ids[:, None]].max(
        jnp.where(valid_wide, block_max, lowest_value)
    )
    row_top = lax.pmax(max_table.astype(jnp.bfloat16), ("ctx", "mp")).astype(max_table.dtype)
    factor = jnp.where(valid_wide, jnp.exp(block_max - row_top[slot_rows, head_ids[:, None]]), 0.0)
    return (block_value * factor[..., None], block_sum * factor)


def to_owners(array, kv_heads, capacity, per_head, ctx_count):
    shaped = array.reshape(kv_heads, capacity, per_head, -1)
    return jnp.transpose(shaped, (0, 2, 1, 3)).reshape(ctx_count, capacity, -1)


def per_device(
    query,
    keys,
    values,
    chosen,
    residual,
    output_weight,
    norm_gain,
    gate_weight,
    up_weight,
    down_weight,
):
    kv_heads = query.shape[1]
    group_size = query.shape[2]
    head_dim = query.shape[3]
    score_scale = head_dim ** (-0.5)
    ctx_count = lax.axis_size("ctx")
    mp_count = lax.axis_size("mp")
    ctx_place = lax.axis_index("ctx")
    mp_place = lax.axis_index("mp")
    own_part = ctx_place * mp_count + mp_place
    all_queries = lax.all_gather(query, ("ctx", "mp"), axis=0, tiled=True)
    all_rows = all_queries.shape[0]
    capacity = min(4 * ROW_DEV * KEPT_PARTITIONS, all_rows)
    slot_rows, slot_valid = find_slots(chosen, own_part, capacity)
    head_ids = jnp.arange(kv_heads, dtype=jnp.int32)
    picked = all_queries[slot_rows, head_ids[:, None]].reshape(
        kv_heads, capacity * group_size, head_dim
    )

    def attend(inputs):
        query_block, key_block, value_block = inputs
        scores = (
            lax.dot_general(
                query_block, key_block, (((1,), (1,)), ((), ())), preferred_element_type=jnp.float32
            )
            * score_scale
        )
        block_max = jnp.max(scores, axis=1)
        probs = jnp.exp(scores - block_max[:, None])
        block_sum = jnp.sum(probs, axis=1)
        block_value = jnp.dot(
            probs.astype(jnp.bfloat16), value_block, preferred_element_type=jnp.float32
        )
        return (block_max, block_sum, block_value)

    block_max, block_sum, block_value = lax.map(attend, (picked, keys[0], values[0]))
    block_max = block_max.reshape(kv_heads, capacity, group_size)
    block_sum = block_sum.reshape(kv_heads, capacity, group_size)
    block_value = block_value.reshape(kv_heads, capacity, group_size, head_dim)
    per_head = ctx_count // kv_heads
    feat_width = kv_heads * group_size * head_dim // ctx_count
    head_share = kv_heads * group_size // ctx_count
    own_head = ctx_place // per_head
    head_lists = lax.dynamic_index_in_dim(chosen, own_head, 0, keepdims=True)
    sources = jnp.arange(ctx_count, dtype=jnp.int32) * mp_count + mp_place
    source_rows = jax.vmap(lambda source: find_slots(head_lists, source, capacity)[0])(sources)[
        :, 0
    ]
    weighted, scaled_sum = global_scaling(
        block_max, block_sum, block_value, slot_rows, slot_valid, all_rows, head_ids
    )
    send_values = to_owners(weighted, kv_heads, capacity, per_head, ctx_count)
    send_sums = to_owners(scaled_sum, kv_heads, capacity, per_head, ctx_count)
    got_values, got_sums = (
        lax.all_to_all(
            send_values.astype(jnp.bfloat16), "ctx", split_axis=0, concat_axis=0, tiled=True
        ).astype(send_values.dtype),
        lax.all_to_all(
            send_sums.astype(jnp.bfloat16), "ctx", split_axis=0, concat_axis=0, tiled=True
        ).astype(send_sums.dtype),
    )
    numerator = jnp.zeros((all_rows, feat_width), jnp.float32).at[source_rows].add(got_values)
    denominator = jnp.zeros((all_rows, head_share), jnp.float32).at[source_rows].add(got_sums)
    numerator, denominator = (
        lax.psum(numerator.astype(jnp.bfloat16), "mp").astype(jnp.float32),
        lax.psum(denominator.astype(jnp.bfloat16), "mp").astype(jnp.float32),
    )
    attended = (
        (numerator.reshape(all_rows, -1, head_dim) / denominator[:, :, None])
        .reshape(all_rows, -1)
        .astype(jnp.bfloat16)
    )
    rows_here = attended
    projected = lax.psum_scatter(
        jnp.dot(rows_here, output_weight, preferred_element_type=jnp.float32),
        "ctx",
        scatter_dimension=0,
        tiled=True,
    )
    stream = (residual.astype(jnp.float32) + projected).astype(jnp.bfloat16)
    stream_wide = stream.astype(jnp.float32)
    squares = lax.psum(jnp.sum(stream_wide * stream_wide, axis=1), "mp")
    normed = (
        stream_wide * lax.rsqrt(squares / MODEL_WIDTH + norm_eps)[:, None] * norm_gain
    ).astype(jnp.bfloat16)
    row_piece = lax.all_gather(normed, "ctx", axis=0, tiled=True)
    gate_piece = jnp.dot(row_piece, gate_weight, preferred_element_type=jnp.float32)
    up_piece = jnp.dot(row_piece, up_weight, preferred_element_type=jnp.float32)
    gate_up = jnp.stack([gate_piece, up_piece], axis=1)
    gate_up = lax.psum(gate_up.astype(jnp.bfloat16), "mp").astype(jnp.float32)
    hidden = (jax.nn.silu(gate_up[:, 0]) * gate_up[:, 1]).astype(jnp.bfloat16)
    rows_here = hidden
    update = lax.psum_scatter(
        jnp.dot(rows_here, down_weight, preferred_element_type=jnp.float32),
        "ctx",
        scatter_dimension=0,
        tiled=True,
    ).astype(jnp.bfloat16)
    return (stream, update)


lanes = 128
chunk = 512
columns_at_once = 256
ahead = 4
log2_e = math.log2(math.e)


def swapped(array, bit):
    count = lax.axis_size("mp")
    return lax.ppermute(array, "mp", [(i, i ^ bit) for i in range(count)])


def over_ctx(array):
    return lax.all_to_all(array, "ctx", split_axis=0, concat_axis=0, tiled=True)


def copies_kernel(in_ref, out_ref):
    for i in range(out_ref.shape[0]):
        out_ref[i] = in_ref[...]


def split_stat(value):
    high = value.astype(jnp.bfloat16).astype(jnp.float32)
    return high, value - high


def attend_kernel(pair, part_ref, place_ref, query_a, query_b, keys, values, chosen, *refs):
    if pair == 0:
        keep_ref, send_ref, key_ref, value_ref = refs[:4]
    else:
        keep_ref, send_ref = refs[:2]
        key_ref, value_ref = keys, values
    score_s, top_s, out_s, lse_s, chosen_ref, sems, chosen_sem = refs[-7:]
    rows, heads, group, depth = query_a.shape
    count = key_ref.shape[1]
    scale = depth ** (-0.5)
    lane = lax.broadcasted_iota(jnp.int32, (rows, lanes), 1)
    listed = chosen_ref.shape[2]
    row_lane = lax.broadcasted_iota(jnp.int32, (rows, listed), 1)
    row_place = lax.broadcasted_iota(jnp.int32, (rows, listed), 0) * (listed // rows)
    chosen_copy = pltpu.make_async_copy(chosen, chosen_ref, chosen_sem)

    def arrivals(h):
        return (
            pltpu.make_async_copy(keys.at[h], key_ref.at[h], sems.at[0, h]),
            pltpu.make_async_copy(values.at[h], value_ref.at[h], sems.at[1, h]),
        )

    def send_for(h):
        if pair == 0:
            for copy in arrivals(h):
                copy.start()

    def wait_for(h):
        if pair == 0:
            for copy in arrivals(h):
                copy.wait()

    def query_of(h):
        return jnp.concatenate(
            [
                q[:, h].astype(jnp.float32).reshape(rows * group, depth)
                for q in (query_a, query_b)
            ],
            axis=0,
        ).astype(jnp.bfloat16)

    def score(query, h, slot, i, top):
        window = slice(i * chunk, (i + 1) * chunk)
        scores = lax.dot_general(
            query, key_ref[h, window, :], (((1,), (1,)), ((), ())),
            preferred_element_type=jnp.float32,
        )
        score_s[slot, :, window] = scores
        for j in range(chunk // lanes):
            part = scores[:, j * lanes : (j + 1) * lanes]
            top = part if top is None else jnp.maximum(top, part)
        return top

    def spent(h, slot, i, top, mixed):
        window = slice(i * chunk, (i + 1) * chunk)
        probs = jnp.exp2((score_s[slot, :, window] - top) * (scale * log2_e))
        ones = jnp.ones((chunk, lanes), jnp.bfloat16)
        part = jnp.dot(
            probs.astype(jnp.bfloat16),
            jnp.concatenate([value_ref[h, window, :], ones], axis=1),
            preferred_element_type=jnp.float32,
        )
        return part if mixed is None else mixed + part

    def finish(h, slot, top, mixed):
        total = mixed[:, depth:]
        out_s[slot] = mixed[:, :depth] * (1.0 / total)
        lse_s[slot] = top * scale + jnp.log(total)
        member = jnp.where(chosen_ref[h] == part_ref[0], 1.0, 0.0)
        member = jnp.max(member, axis=0, keepdims=True)
        for part, ref in enumerate((keep_ref, send_ref)):
            row = row_place + (place_ref[0] ^ (2 * pair + part))
            held = jnp.where(row_lane == row, member, 0.0)
            bias = jnp.where(jnp.max(held, axis=1, keepdims=True) > 0.5, 0.0, lowest_value)
            stats = jnp.zeros((rows, lanes), jnp.float32)
            for g in range(group):
                window = pl.ds(part * rows * group + g, rows, stride=group)
                ref[h, :, g * depth : (g + 1) * depth] = out_s[slot, window, :].astype(jnp.bfloat16)
                high, low = split_stat(lse_s[slot, window, :] + bias)
                stats = jnp.where(lane == g, high, jnp.where(lane == group + g, low, stats))
            ref[h, :, group * depth :] = stats.astype(jnp.bfloat16)

    def both(h, slot, following, after):
        top = jnp.max(top_s[slot], axis=1, keepdims=True)
        query = query_of(following)
        mixed = later = None
        for i in range(count // chunk):
            mixed = spent(h, slot, i, top, mixed)
            later = score(query, following, after, i, later)
        top_s[after] = later
        finish(h, slot, top, mixed)

    for h in range(min(ahead, heads)):
        send_for(h)
    chosen_copy.start()
    wait_for(0)
    query, top = query_of(0), None
    for i in range(count // chunk):
        top = score(query, 0, 0, i, top)
    top_s[0] = top
    chosen_copy.wait()

    @pl.loop(0, heads // 2)
    def _(step):
        h = 2 * step
        wait_for(h + 1)
        both(h, 0, h + 1, 1)

        @pl.when(h + 2 < heads)
        def _():
            wait_for(h + 2)

        for i in range(2):

            @pl.when(h + ahead + i < heads)
            def _():
                send_for(h + ahead + i)

        both(h + 1, 1, jnp.minimum(h + 2, heads - 1), 0)


def attend(pair, part, place, query_a, query_b, keys, values, chosen):
    rows, heads, group, depth = query_a.shape
    count = keys.shape[1]
    width = group * depth + lanes
    shape = jax.ShapeDtypeStruct((heads, rows, width), jnp.bfloat16)
    held = [pltpu.VMEM(a.shape, a.dtype) for a in (keys, values)]
    vmem, hbm = pl.BlockSpec(memory_space=pltpu.VMEM), pl.BlockSpec(memory_space=pltpu.HBM)
    space = pltpu.VMEM if pair else pltpu.HBM
    return pl.pallas_call(
        functools.partial(attend_kernel, pair),
        in_specs=[pl.BlockSpec(memory_space=pltpu.SMEM)] * 2
        + [vmem] * 2
        + [vmem if pair else hbm] * 2
        + [hbm],
        out_specs=[vmem] * (2 if pair else 4),
        out_shape=[shape, shape] + ([] if pair else held),
        scratch_shapes=[
            pltpu.VMEM((2, 2 * rows * group, count), jnp.float32),
            pltpu.VMEM((2, 2 * rows * group, lanes), jnp.float32),
            pltpu.VMEM((2, 2 * rows * group, depth), jnp.float32),
            pltpu.VMEM((2, 2 * rows * group, lanes), jnp.float32),
            pltpu.VMEM(chosen.shape, chosen.dtype),
            pltpu.SemaphoreType.DMA((2, heads)),
            pltpu.SemaphoreType.DMA(()),
        ],
        compiler_params=pltpu.CompilerParams(vmem_limit_bytes=10 << 20),
        cost_estimate=pl.CostEstimate(
            flops=(1 + 4 * pair) * 8 * heads * rows * group * depth * count,
            bytes_accessed=4 * heads * count * depth,
            transcendentals=2 * heads * rows * group * count,
        ),
    )(
        part,
        place,
        query_a,
        query_b,
        pltpu.with_memory_space_constraint(keys, space),
        pltpu.with_memory_space_constraint(values, space),
        pltpu.with_memory_space_constraint(chosen, pltpu.HBM),
    )


def merged(parts, group, depth):
    stats = [part[:, group * depth :] for part in parts]
    lses = [s + pltpu.roll(s, lanes - group, 1) for s in stats]
    top = functools.reduce(jnp.maximum, lses)
    weights = [jnp.exp(lse - top) for lse in lses]
    total = functools.reduce(jnp.add, weights)
    inverse = 1.0 / total
    weights = [w * inverse for w in weights]
    values = []
    for g in range(group):
        values.append(
            functools.reduce(
                jnp.add,
                [
                    w[:, g : g + 1] * part[:, g * depth : (g + 1) * depth]
                    for w, part in zip(weights, parts)
                ],
            )
        )
    return values, top + jnp.log(total)


def packed_stat(lse, group):
    lane = lax.broadcasted_iota(jnp.int32, lse.shape, 1)
    high, low = split_stat(lse)
    low = pltpu.roll(low, group, 1)
    return jnp.where(lane < group, high, jnp.where(lane < 2 * group, low, 0.0))


def core_kernel(group, depth, part, keep_ref, recv_ref, *refs):
    out_ref = refs[-1]
    heads, rows, _ = keep_ref.shape
    where = slice(part * rows, (part + 1) * rows)

    for h in range(heads):
        values, lse = merged(
            [keep_ref[h].astype(jnp.float32), recv_ref[h].astype(jnp.float32)], group, depth
        )
        for g in range(group):
            out_ref[h, where, g * depth : (g + 1) * depth] = values[g].astype(jnp.bfloat16)
        out_ref[h, where, group * depth :] = packed_stat(lse, group).astype(jnp.bfloat16)


def core_merge(part, keep, recv, group, depth, into=None):
    heads, rows, width = keep.shape
    more = [] if into is None else [into]
    vmem = pl.BlockSpec(memory_space=pltpu.VMEM)
    return pl.pallas_call(
        functools.partial(core_kernel, group, depth, part),
        in_specs=[vmem] * (2 + len(more)),
        out_specs=vmem,
        out_shape=jax.ShapeDtypeStruct((heads, 2 * rows, width), jnp.bfloat16),
        input_output_aliases={2: 0} if more else {},
        compiler_params=pltpu.CompilerParams(vmem_limit_bytes=8 << 20),
    )(keep, recv, *more)


def ctx_kernel(group, depth, got_ref, out_ref):
    values, lse = merged(
        [got_ref[s].astype(jnp.float32) for s in range(got_ref.shape[0])], group, depth
    )
    for g in range(group):
        out_ref[:, g * depth : (g + 1) * depth] = values[g].astype(jnp.bfloat16)
    out_ref[:, group * depth :] = packed_stat(lse, group).astype(jnp.bfloat16)


def x_kernel(group, depth, own_ref, got_ref, out_ref):
    half = own_ref.shape[0] // 2
    own = own_ref[...].astype(jnp.float32)
    got = got_ref[...].astype(jnp.float32)
    got = jnp.concatenate([got[half:], got[:half]], axis=0)
    values, _ = merged([own, got], group, depth)
    for g in range(group):
        out_ref[:, g * depth : (g + 1) * depth] = values[g].astype(jnp.bfloat16)


def small_call(kernel, shapes, *operands, flops=0, held=False):
    return pl.pallas_call(
        kernel,
        out_shape=jax.tree.map(
            lambda shape: (pltpu.VMEM if held else jax.ShapeDtypeStruct)(shape, jnp.bfloat16),
            shapes,
            is_leaf=lambda x: isinstance(x, tuple),
        ),
        compiler_params=pltpu.CompilerParams(vmem_limit_bytes=8 << 20),
        cost_estimate=pl.CostEstimate(flops=flops, bytes_accessed=1 << 19, transcendentals=0),
    )(*operands)


def scatter_rows(out_ref, first, start, stop, value):
    count, step, _ = out_ref.shape
    for i in range(count):
        where = i if first is None else lax.rem(first + i, count)
        out_ref[where, :, start:stop] = value[i * step : (i + 1) * step].astype(out_ref.dtype)


def stream_kernel(got_ref, residual_ref, stream_ref, copies_ref):
    total = residual_ref[...].astype(jnp.float32)
    partial = got_ref[0].astype(jnp.float32)
    for i in range(1, got_ref.shape[0]):
        partial += got_ref[i].astype(jnp.float32)
    stream = (total + partial).astype(jnp.bfloat16)
    stream_ref[...] = stream
    for i in range(copies_ref.shape[0]):
        copies_ref[i] = stream


def product(left, weight_ref, emit):
    width = weight_ref.shape[1]
    for start in range(0, width, columns_at_once):
        stop = min(start + columns_at_once, width)
        emit(
            start,
            stop,
            jnp.dot(left, weight_ref[:, start:stop], preferred_element_type=jnp.float32),
        )


def project_kernel(place_ref, own_ref, got_ref, weight_ref, out_ref):
    rows = out_ref.shape[0] * out_ref.shape[1]
    half = rows // 2
    quarter = rows // 4
    place = place_ref[0]
    target = lax.broadcasted_iota(jnp.int32, (rows, half), 0)
    source = lax.broadcasted_iota(jnp.int32, (rows, half), 1)
    row = (source % quarter) * 4
    column = 2 * (source // quarter)
    own_order = jnp.where(target == row + (place ^ column), 1.0, 0.0).astype(jnp.bfloat16)
    got_order = jnp.where(target == row + (place ^ (column + 1)), 1.0, 0.0).astype(jnp.bfloat16)
    attended = jnp.dot(own_order, own_ref[...], preferred_element_type=jnp.float32) + jnp.dot(
        got_order, got_ref[...], preferred_element_type=jnp.float32
    )
    product(
        attended.astype(jnp.bfloat16), weight_ref, functools.partial(scatter_rows, out_ref, None)
    )


def tail_of(squares):
    lane = lax.broadcasted_iota(jnp.int32, (squares.shape[0], lanes), 1)
    high, low = split_stat(squares)
    return jnp.where(lane == 0, high, jnp.where(lane == 1, low, 0.0)).astype(jnp.bfloat16)


def half_of(place_ref, count):
    return (place_ref[0] & 1) * (count // 2)


def gate_kernel(place_ref, rows_ref, gain_ref, gate_ref, up_ref, keep_ref, send_ref):
    count = rows_ref.shape[0]
    first = half_of(place_ref, count)
    rows = jnp.concatenate(
        [rows_ref[lax.rem(first + i, count)].astype(jnp.float32) for i in range(count)], axis=0
    )
    half = rows.shape[0] // 2
    scaled = (rows * gain_ref[...]).astype(jnp.bfloat16)
    units = gate_ref.shape[1]

    def emit(offset, start, stop, value):
        value = value.astype(jnp.bfloat16)
        keep_ref[:, offset + start : offset + stop] = value[:half]
        send_ref[:, offset + start : offset + stop] = value[half:]

    tail = tail_of(jnp.sum(rows * rows, axis=1, keepdims=True))
    emit(2 * units, 0, lanes, tail)
    product(scaled, gate_ref, functools.partial(emit, 0))
    product(scaled, up_ref, functools.partial(emit, units))


def summed(own_ref, got_ref, start, stop):
    return own_ref[:, start:stop].astype(jnp.float32) + got_ref[:, start:stop].astype(jnp.float32)


def squares_of(own_ref, got_ref):
    start = own_ref.shape[1] - lanes
    tail = summed(own_ref, got_ref, start, start + lanes)
    return tail[:, 0:1] + tail[:, 1:2]


def pair_kernel(own_ref, got_ref, out_ref):
    units = own_ref.shape[1] - lanes
    out_ref[:, :units] = summed(own_ref, got_ref, 0, units).astype(jnp.bfloat16)
    out_ref[:, units:] = tail_of(squares_of(own_ref, got_ref))


def hidden_kernel(own_ref, got_ref, out_ref):
    units = out_ref.shape[1]
    scale = lax.rsqrt(squares_of(own_ref, got_ref) / MODEL_WIDTH + norm_eps)
    gate = summed(own_ref, got_ref, 0, units) * scale
    up = summed(own_ref, got_ref, units, 2 * units) * scale
    out_ref[...] = (jax.nn.silu(gate) * up).astype(jnp.bfloat16)


def down_kernel(place_ref, own_ref, got_ref, weight_ref, out_ref):
    hidden = jnp.concatenate([own_ref[...], got_ref[...]], axis=0)
    first = half_of(place_ref, out_ref.shape[0])
    product(hidden, weight_ref, functools.partial(scatter_rows, out_ref, first))


def total_kernel(got_ref, out_ref):
    total = got_ref[0].astype(jnp.float32)
    for i in range(1, got_ref.shape[0]):
        total += got_ref[i].astype(jnp.float32)
    out_ref[...] = total.astype(jnp.bfloat16)


def weighed(kernel, shapes, weights, scalar, *operands):
    vmem = pl.BlockSpec(memory_space=pltpu.VMEM)
    outs = [jax.ShapeDtypeStruct(shape, jnp.bfloat16) for shape in shapes]
    return pl.pallas_call(
        kernel,
        in_specs=[pl.BlockSpec(memory_space=pltpu.SMEM)]
        + [vmem] * (len(operands) + len(weights)),
        out_specs=[vmem] * len(outs),
        out_shape=outs,
        compiler_params=pltpu.CompilerParams(vmem_limit_bytes=8 << 20),
        cost_estimate=pl.CostEstimate(
            flops=sum(64 * w.size for w in weights),
            bytes_accessed=sum(2 * w.size for w in weights),
            transcendentals=0,
        ),
    )(scalar, *operands, *(pltpu.with_memory_space_constraint(w, pltpu.VMEM) for w in weights))


def per_device_dense(
    query,
    keys,
    values,
    chosen,
    residual,
    output_weight,
    norm_gain,
    gate_weight,
    up_weight,
    down_weight,
):
    _, heads, group, depth = query.shape
    ctx_count = lax.axis_size("ctx")
    mp_count = lax.axis_size("mp")
    mp_place = lax.axis_index("mp")
    own_part = lax.axis_index("ctx") * mp_count + mp_place
    all_rows = ctx_count * mp_count

    part, place = jnp.reshape(own_part, (1,)), jnp.reshape(mp_place, (1,))
    chosen = jnp.transpose(chosen, (0, 2, 1))
    copies = small_call(
        copies_kernel, (ctx_count,) + query.shape[1:], query[0], flops=0
    )
    query_own = over_ctx(copies)
    keys, values = keys[0], values[0]
    query_core = swapped(query_own, 1)
    query_x = swapped(query_own, 2)
    keep_a, send_a, keys, values = attend(0, part, place, query_own, query_core, keys, values, chosen)
    query_x, _ = lax.optimization_barrier((query_x, send_a))
    query_far = swapped(query_x, 1)
    recv_a = swapped(send_a, 1)
    keep_b, send_b = attend(1, part, place, query_x, query_far, keys, values, chosen)
    recv_b = swapped(send_b, 1)
    on_chip = core_merge(0, keep_a, recv_a, group, depth)
    on_chip = core_merge(1, keep_b, recv_b, group, depth, into=on_chip)
    got = over_ctx(on_chip)
    half_rows = 2 * ctx_count
    width = group * depth
    column = small_call(
        functools.partial(ctx_kernel, group, depth), (half_rows, width + lanes), got
    )
    attended = small_call(
        functools.partial(x_kernel, group, depth), (half_rows, width), column, swapped(column, 2)
    )
    other = swapped(attended, 1)
    width = output_weight.shape[1]
    block = (ctx_count, mp_count, width)
    (projected,) = weighed(
        project_kernel, [block], (output_weight,), place, attended, other
    )
    stream, copies = small_call(
        stream_kernel, [residual.shape, block], over_ctx(projected), residual, held=True
    )
    rows = over_ctx(copies)
    units = gate_weight.shape[1]
    half = all_rows // 2
    keep, send = weighed(
        gate_kernel,
        [(half, 2 * units + lanes)] * 2,
        (gate_weight, up_weight),
        place,
        rows,
        norm_gain.reshape(1, -1),
    )
    mine = small_call(pair_kernel, keep.shape, keep, swapped(send, 1))
    hidden = small_call(hidden_kernel, (half, units), mine, swapped(mine, 2))
    (update,) = weighed(
        down_kernel, [block], (down_weight,), place, hidden, swapped(hidden, 1)
    )
    update = small_call(total_kernel, residual.shape, over_ctx(update))
    return (stream, update)


def either(*arrays):
    query, mp_count, ctx_count = arrays[0], lax.axis_size("mp"), lax.axis_size("ctx")
    rows, heads, group, depth = query.shape
    dense = (
        rows == 1
        and mp_count == 4
        and heads == ctx_count == group == 8
        and depth == lanes
        and arrays[1].shape[0] == 1
    )
    return (per_device_dense if dense else per_device)(*arrays)


def solution(mesh):
    return jax.shard_map(
        either,
        mesh=mesh,
        in_specs=(
            P(("ctx", "mp"), None, None, None),
            P(("ctx", "mp"), None, None, None),
            P(("ctx", "mp"), None, None, None),
            P(),
            P("ctx", "mp"),
            P("ctx", "mp"),
            P("mp"),
            P("mp", "ctx"),
            P("mp", "ctx"),
            P("ctx", "mp"),
        ),
        out_specs=(P("ctx", "mp"), P("ctx", "mp")),
        check_vma=False,
    )
```

```python
import functools
import math

import jax
import jax.numpy as jnp
from jax import lax
from jax.experimental import pallas as pl
from jax.experimental.pallas import tpu as pltpu
from jax.sharding import PartitionSpec as P

MODEL_WIDTH = 8192
KEPT_PARTITIONS = 16
ROW_DEV = 1


norm_eps = 1e-05
lowest_value = -1e30


def find_slots(listed, target, capacity):
    member = jnp.any(listed == target, axis=2)
    places = jnp.cumsum(member.astype(jnp.int32), axis=1) - 1
    live_count = jnp.sum(member.astype(jnp.int32), axis=1)
    slot_ranks = jnp.arange(capacity, dtype=jnp.int32)
    slot_hits = member[:, :, None] & (places[:, :, None] == slot_ranks[None, None, :])
    row_numbers = jnp.arange(listed.shape[1], dtype=jnp.int32)
    slot_rows = jnp.sum(jnp.where(slot_hits, row_numbers[None, :, None], 0), axis=1)
    slot_valid = slot_ranks[None, :] < live_count[:, None]
    return (slot_rows, slot_valid)


def global_scaling(block_max, block_sum, block_value, slot_rows, slot_valid, all_rows, head_ids):
    kv_heads, capacity, group_size = block_max.shape
    valid_wide = slot_valid[:, :, None]
    max_table = jnp.full((all_rows, kv_heads, group_size), lowest_value, jnp.float32)
    max_table = max_table.at[slot_rows, head_ids[:, None]].max(
        jnp.where(valid_wide, block_max, lowest_value)
    )
    row_top = lax.pmax(max_table.astype(jnp.bfloat16), ("ctx", "mp")).astype(max_table.dtype)
    factor = jnp.where(valid_wide, jnp.exp(block_max - row_top[slot_rows, head_ids[:, None]]), 0.0)
    return (block_value * factor[..., None], block_sum * factor)


def to_owners(array, kv_heads, capacity, per_head, ctx_count):
    shaped = array.reshape(kv_heads, capacity, per_head, -1)
    return jnp.transpose(shaped, (0, 2, 1, 3)).reshape(ctx_count, capacity, -1)


def per_device(
    query,
    keys,
    values,
    chosen,
    residual,
    output_weight,
    norm_gain,
    gate_weight,
    up_weight,
    down_weight,
):
    kv_heads = query.shape[1]
    group_size = query.shape[2]
    head_dim = query.shape[3]
    score_scale = head_dim ** (-0.5)
    ctx_count = lax.axis_size("ctx")
    mp_count = lax.axis_size("mp")
    ctx_place = lax.axis_index("ctx")
    mp_place = lax.axis_index("mp")
    own_part = ctx_place * mp_count + mp_place
    all_queries = lax.all_gather(query, ("ctx", "mp"), axis=0, tiled=True)
    all_rows = all_queries.shape[0]
    capacity = min(4 * ROW_DEV * KEPT_PARTITIONS, all_rows)
    slot_rows, slot_valid = find_slots(chosen, own_part, capacity)
    head_ids = jnp.arange(kv_heads, dtype=jnp.int32)
    picked = all_queries[slot_rows, head_ids[:, None]].reshape(
        kv_heads, capacity * group_size, head_dim
    )

    def attend(inputs):
        query_block, key_block, value_block = inputs
        scores = (
            lax.dot_general(
                query_block, key_block, (((1,), (1,)), ((), ())), preferred_element_type=jnp.float32
            )
            * score_scale
        )
        block_max = jnp.max(scores, axis=1)
        probs = jnp.exp(scores - block_max[:, None])
        block_sum = jnp.sum(probs, axis=1)
        block_value = jnp.dot(
            probs.astype(jnp.bfloat16), value_block, preferred_element_type=jnp.float32
        )
        return (block_max, block_sum, block_value)

    block_max, block_sum, block_value = lax.map(attend, (picked, keys[0], values[0]))
    block_max = block_max.reshape(kv_heads, capacity, group_size)
    block_sum = block_sum.reshape(kv_heads, capacity, group_size)
    block_value = block_value.reshape(kv_heads, capacity, group_size, head_dim)
    per_head = ctx_count // kv_heads
    feat_width = kv_heads * group_size * head_dim // ctx_count
    head_share = kv_heads * group_size // ctx_count
    own_head = ctx_place // per_head
    head_lists = lax.dynamic_index_in_dim(chosen, own_head, 0, keepdims=True)
    sources = jnp.arange(ctx_count, dtype=jnp.int32) * mp_count + mp_place
    source_rows = jax.vmap(lambda source: find_slots(head_lists, source, capacity)[0])(sources)[
        :, 0
    ]
    weighted, scaled_sum = global_scaling(
        block_max, block_sum, block_value, slot_rows, slot_valid, all_rows, head_ids
    )
    send_values = to_owners(weighted, kv_heads, capacity, per_head, ctx_count)
    send_sums = to_owners(scaled_sum, kv_heads, capacity, per_head, ctx_count)
    got_values, got_sums = (
        lax.all_to_all(
            send_values.astype(jnp.bfloat16), "ctx", split_axis=0, concat_axis=0, tiled=True
        ).astype(send_values.dtype),
        lax.all_to_all(
            send_sums.astype(jnp.bfloat16), "ctx", split_axis=0, concat_axis=0, tiled=True
        ).astype(send_sums.dtype),
    )
    numerator = jnp.zeros((all_rows, feat_width), jnp.float32).at[source_rows].add(got_values)
    denominator = jnp.zeros((all_rows, head_share), jnp.float32).at[source_rows].add(got_sums)
    numerator, denominator = (
        lax.psum(numerator.astype(jnp.bfloat16), "mp").astype(jnp.float32),
        lax.psum(denominator.astype(jnp.bfloat16), "mp").astype(jnp.float32),
    )
    attended = (
        (numerator.reshape(all_rows, -1, head_dim) / denominator[:, :, None])
        .reshape(all_rows, -1)
        .astype(jnp.bfloat16)
    )
    rows_here = attended
    projected = lax.psum_scatter(
        jnp.dot(rows_here, output_weight, preferred_element_type=jnp.float32),
        "ctx",
        scatter_dimension=0,
        tiled=True,
    )
    stream = (residual.astype(jnp.float32) + projected).astype(jnp.bfloat16)
    stream_wide = stream.astype(jnp.float32)
    squares = lax.psum(jnp.sum(stream_wide * stream_wide, axis=1), "mp")
    normed = (
        stream_wide * lax.rsqrt(squares / MODEL_WIDTH + norm_eps)[:, None] * norm_gain
    ).astype(jnp.bfloat16)
    row_piece = lax.all_gather(normed, "ctx", axis=0, tiled=True)
    gate_piece = jnp.dot(row_piece, gate_weight, preferred_element_type=jnp.float32)
    up_piece = jnp.dot(row_piece, up_weight, preferred_element_type=jnp.float32)
    gate_up = jnp.stack([gate_piece, up_piece], axis=1)
    gate_up = lax.psum(gate_up.astype(jnp.bfloat16), "mp").astype(jnp.float32)
    hidden = (jax.nn.silu(gate_up[:, 0]) * gate_up[:, 1]).astype(jnp.bfloat16)
    rows_here = hidden
    update = lax.psum_scatter(
        jnp.dot(rows_here, down_weight, preferred_element_type=jnp.float32),
        "ctx",
        scatter_dimension=0,
        tiled=True,
    ).astype(jnp.bfloat16)
    return (stream, update)


lanes = 128
chunk = 512
columns_at_once = 256
ahead = 4
log2_e = math.log2(math.e)


def swapped(array, bit):
    count = lax.axis_size("mp")
    return lax.ppermute(array, "mp", [(i, i ^ bit) for i in range(count)])


def over_ctx(array):
    return lax.all_to_all(array, "ctx", split_axis=0, concat_axis=0, tiled=True)


def copies_kernel(in_ref, out_ref):
    for i in range(out_ref.shape[0]):
        out_ref[i] = in_ref[...]


def split_stat(value):
    high = value.astype(jnp.bfloat16).astype(jnp.float32)
    return high, value - high


def attend_kernel(pair, part_ref, place_ref, query_a, query_b, keys, values, chosen, *refs):
    if pair == 0:
        keep_ref, send_ref, key_ref, value_ref = refs[:4]
    else:
        keep_ref, send_ref = refs[:2]
        key_ref, value_ref = keys, values
    score_s, top_s, out_s, lse_s, chosen_ref, sems, chosen_sem = refs[-7:]
    rows, heads, group, depth = query_a.shape
    count = key_ref.shape[1]
    scale = depth ** (-0.5)
    lane = lax.broadcasted_iota(jnp.int32, (rows, lanes), 1)
    listed = chosen_ref.shape[2]
    row_lane = lax.broadcasted_iota(jnp.int32, (rows, listed), 1)
    row_place = lax.broadcasted_iota(jnp.int32, (rows, listed), 0) * (listed // rows)
    chosen_copy = pltpu.make_async_copy(chosen, chosen_ref, chosen_sem)

    def arrivals(h):
        return (
            pltpu.make_async_copy(keys.at[h], key_ref.at[h], sems.at[0, h]),
            pltpu.make_async_copy(values.at[h], value_ref.at[h], sems.at[1, h]),
        )

    def send_for(h):
        if pair == 0:
            for copy in arrivals(h):
                copy.start()

    def wait_for(h):
        if pair == 0:
            for copy in arrivals(h):
                copy.wait()

    def query_of(h):
        return jnp.concatenate(
            [
                q[:, h].astype(jnp.float32).reshape(rows * group, depth)
                for q in (query_a, query_b)
            ],
            axis=0,
        ).astype(jnp.bfloat16)

    def score(query, h, slot, i, top):
        window = slice(i * chunk, (i + 1) * chunk)
        scores = lax.dot_general(
            query, key_ref[h, window, :], (((1,), (1,)), ((), ())),
            preferred_element_type=jnp.float32,
        )
        score_s[slot, :, window] = scores
        for j in range(chunk // lanes):
            part = scores[:, j * lanes : (j + 1) * lanes]
            top = part if top is None else jnp.maximum(top, part)
        return top

    def spent(h, slot, i, top, mixed):
        window = slice(i * chunk, (i + 1) * chunk)
        probs = jnp.exp2((score_s[slot, :, window] - top) * (scale * log2_e))
        ones = jnp.ones((chunk, lanes), jnp.bfloat16)
        part = jnp.dot(
            probs.astype(jnp.bfloat16),
            jnp.concatenate([value_ref[h, window, :], ones], axis=1),
            preferred_element_type=jnp.float32,
        )
        return part if mixed is None else mixed + part

    def finish(h, slot, top, mixed):
        total = mixed[:, depth:]
        out_s[slot] = mixed[:, :depth] * (1.0 / total)
        lse_s[slot] = top * scale + jnp.log(total)
        member = jnp.where(chosen_ref[h] == part_ref[0], 1.0, 0.0)
        member = jnp.max(member, axis=0, keepdims=True)
        for part, ref in enumerate((keep_ref, send_ref)):
            row = row_place + (place_ref[0] ^ (2 * pair + part))
            held = jnp.where(row_lane == row, member, 0.0)
            bias = jnp.where(jnp.max(held, axis=1, keepdims=True) > 0.5, 0.0, lowest_value)
            stats = jnp.zeros((rows, lanes), jnp.float32)
            for g in range(group):
                window = pl.ds(part * rows * group + g, rows, stride=group)
                ref[h, :, g * depth : (g + 1) * depth] = out_s[slot, window, :].astype(jnp.bfloat16)
                high, low = split_stat(lse_s[slot, window, :] + bias)
                stats = jnp.where(lane == g, high, jnp.where(lane == group + g, low, stats))
            ref[h, :, group * depth :] = stats.astype(jnp.bfloat16)

    def both(h, slot, following, after):
        top = jnp.max(top_s[slot], axis=1, keepdims=True)
        query = query_of(following)
        mixed = later = None
        for i in range(count // chunk):
            mixed = spent(h, slot, i, top, mixed)
            later = score(query, following, after, i, later)
        top_s[after] = later
        finish(h, slot, top, mixed)

    for h in range(2):
        send_for(h)
    chosen_copy.start()
    wait_for(0)
    query, top = query_of(0), None
    for i in range(count // chunk):
        top = score(query, 0, 0, i, top)
    top_s[0] = top
    chosen_copy.wait()

    @pl.loop(0, heads // 2)
    def _(step):
        h = 2 * step
        for i in range(2, 4):

            @pl.when(h + i < heads)
            def _():
                send_for(h + i)

        wait_for(h + 1)
        both(h, 0, h + 1, 1)

        @pl.when(h + 2 < heads)
        def _():
            wait_for(h + 2)

        both(h + 1, 1, jnp.minimum(h + 2, heads - 1), 0)


def attend(pair, part, place, query_a, query_b, keys, values, chosen):
    rows, heads, group, depth = query_a.shape
    count = keys.shape[1]
    width = group * depth + lanes
    shape = jax.ShapeDtypeStruct((heads, rows, width), jnp.bfloat16)
    held = [pltpu.VMEM(a.shape, a.dtype) for a in (keys, values)]
    vmem, hbm = pl.BlockSpec(memory_space=pltpu.VMEM), pl.BlockSpec(memory_space=pltpu.HBM)
    space = pltpu.VMEM if pair else pltpu.HBM
    return pl.pallas_call(
        functools.partial(attend_kernel, pair),
        in_specs=[pl.BlockSpec(memory_space=pltpu.SMEM)] * 2
        + [vmem] * 2
        + [vmem if pair else hbm] * 2
        + [hbm],
        out_specs=[vmem] * (2 if pair else 4),
        out_shape=[shape, shape] + ([] if pair else held),
        scratch_shapes=[
            pltpu.VMEM((2, 2 * rows * group, count), jnp.float32),
            pltpu.VMEM((2, 2 * rows * group, lanes), jnp.float32),
            pltpu.VMEM((2, 2 * rows * group, depth), jnp.float32),
            pltpu.VMEM((2, 2 * rows * group, lanes), jnp.float32),
            pltpu.VMEM(chosen.shape, chosen.dtype),
            pltpu.SemaphoreType.DMA((2, heads)),
            pltpu.SemaphoreType.DMA(()),
        ],
        compiler_params=pltpu.CompilerParams(vmem_limit_bytes=10 << 20),
        cost_estimate=pl.CostEstimate(
            flops=(1 + 4 * pair) * 8 * heads * rows * group * depth * count,
            bytes_accessed=4 * heads * count * depth,
            transcendentals=2 * heads * rows * group * count,
        ),
    )(
        part,
        place,
        query_a,
        query_b,
        pltpu.with_memory_space_constraint(keys, space),
        pltpu.with_memory_space_constraint(values, space),
        pltpu.with_memory_space_constraint(chosen, pltpu.HBM),
    )


def merged(parts, group, depth):
    stats = [part[:, group * depth :] for part in parts]
    lses = [s + pltpu.roll(s, lanes - group, 1) for s in stats]
    top = functools.reduce(jnp.maximum, lses)
    weights = [jnp.exp(lse - top) for lse in lses]
    total = functools.reduce(jnp.add, weights)
    inverse = 1.0 / total
    weights = [w * inverse for w in weights]
    values = []
    for g in range(group):
        values.append(
            functools.reduce(
                jnp.add,
                [
                    w[:, g : g + 1] * part[:, g * depth : (g + 1) * depth]
                    for w, part in zip(weights, parts)
                ],
            )
        )
    return values, top + jnp.log(total)


def packed_stat(lse, group):
    lane = lax.broadcasted_iota(jnp.int32, lse.shape, 1)
    high, low = split_stat(lse)
    low = pltpu.roll(low, group, 1)
    return jnp.where(lane < group, high, jnp.where(lane < 2 * group, low, 0.0))


def core_kernel(group, depth, part, keep_ref, recv_ref, *refs):
    out_ref = refs[-1]
    heads, rows, _ = keep_ref.shape
    where = slice(part * rows, (part + 1) * rows)

    for h in range(heads):
        values, lse = merged(
            [keep_ref[h].astype(jnp.float32), recv_ref[h].astype(jnp.float32)], group, depth
        )
        for g in range(group):
            out_ref[h, where, g * depth : (g + 1) * depth] = values[g].astype(jnp.bfloat16)
        out_ref[h, where, group * depth :] = packed_stat(lse, group).astype(jnp.bfloat16)


def core_merge(part, keep, recv, group, depth, into=None):
    heads, rows, width = keep.shape
    more = [] if into is None else [into]
    vmem = pl.BlockSpec(memory_space=pltpu.VMEM)
    return pl.pallas_call(
        functools.partial(core_kernel, group, depth, part),
        in_specs=[vmem] * (2 + len(more)),
        out_specs=vmem,
        out_shape=jax.ShapeDtypeStruct((heads, 2 * rows, width), jnp.bfloat16),
        input_output_aliases={2: 0} if more else {},
        compiler_params=pltpu.CompilerParams(vmem_limit_bytes=8 << 20),
    )(keep, recv, *more)


def ctx_kernel(group, depth, got_ref, out_ref):
    values, lse = merged(
        [got_ref[s].astype(jnp.float32) for s in range(got_ref.shape[0])], group, depth
    )
    for g in range(group):
        out_ref[:, g * depth : (g + 1) * depth] = values[g].astype(jnp.bfloat16)
    out_ref[:, group * depth :] = packed_stat(lse, group).astype(jnp.bfloat16)


def x_kernel(group, depth, own_ref, got_ref, out_ref):
    half = own_ref.shape[0] // 2
    own = own_ref[...].astype(jnp.float32)
    got = got_ref[...].astype(jnp.float32)
    got = jnp.concatenate([got[half:], got[:half]], axis=0)
    values, _ = merged([own, got], group, depth)
    for g in range(group):
        out_ref[:, g * depth : (g + 1) * depth] = values[g].astype(jnp.bfloat16)


def small_call(kernel, shapes, *operands, flops=0):
    return pl.pallas_call(
        kernel,
        out_shape=jax.tree.map(
            lambda shape: jax.ShapeDtypeStruct(shape, jnp.bfloat16),
            shapes,
            is_leaf=lambda x: isinstance(x, tuple),
        ),
        compiler_params=pltpu.CompilerParams(vmem_limit_bytes=8 << 20),
        cost_estimate=pl.CostEstimate(flops=flops, bytes_accessed=1 << 19, transcendentals=0),
    )(*operands)


def scatter_rows(out_ref, first, start, stop, value):
    count, step, _ = out_ref.shape
    for i in range(count):
        where = i if first is None else lax.rem(first + i, count)
        out_ref[where, :, start:stop] = value[i * step : (i + 1) * step].astype(out_ref.dtype)


def stream_kernel(got_ref, residual_ref, copies_ref):
    total = residual_ref[...].astype(jnp.float32)
    partial = got_ref[0].astype(jnp.float32)
    for i in range(1, got_ref.shape[0]):
        partial += got_ref[i].astype(jnp.float32)
    stream = (total + partial).astype(jnp.bfloat16)
    for i in range(copies_ref.shape[0]):
        copies_ref[i] = stream


def product(left, weight_ref, emit):
    width = weight_ref.shape[1]
    for start in range(0, width, columns_at_once):
        stop = min(start + columns_at_once, width)
        emit(
            start,
            stop,
            jnp.dot(left, weight_ref[:, start:stop], preferred_element_type=jnp.float32),
        )


def project_kernel(place_ref, own_ref, got_ref, weight_ref, out_ref):
    rows = out_ref.shape[0] * out_ref.shape[1]
    half = rows // 2
    quarter = rows // 4
    place = place_ref[0]
    target = lax.broadcasted_iota(jnp.int32, (rows, half), 0)
    source = lax.broadcasted_iota(jnp.int32, (rows, half), 1)
    row = (source % quarter) * 4
    column = 2 * (source // quarter)
    own_order = jnp.where(target == row + (place ^ column), 1.0, 0.0).astype(jnp.bfloat16)
    got_order = jnp.where(target == row + (place ^ (column + 1)), 1.0, 0.0).astype(jnp.bfloat16)
    attended = jnp.dot(own_order, own_ref[...], preferred_element_type=jnp.float32) + jnp.dot(
        got_order, got_ref[...], preferred_element_type=jnp.float32
    )
    product(
        attended.astype(jnp.bfloat16), weight_ref, functools.partial(scatter_rows, out_ref, None)
    )


def tail_of(squares):
    lane = lax.broadcasted_iota(jnp.int32, (squares.shape[0], lanes), 1)
    high, low = split_stat(squares)
    return jnp.where(lane == 0, high, jnp.where(lane == 1, low, 0.0)).astype(jnp.bfloat16)


def half_of(place_ref, count):
    return (place_ref[0] & 1) * (count // 2)


def rows_in_order(place_ref, rows_ref):
    count = rows_ref.shape[0]
    first = half_of(place_ref, count)
    return jnp.concatenate(
        [rows_ref[lax.rem(first + i, count)].astype(jnp.float32) for i in range(count)], axis=0
    )


def half_product(rows, gain_ref, weight_ref, keep_ref, send_ref):
    half = rows.shape[0] // 2
    scaled = (rows * gain_ref[...]).astype(jnp.bfloat16)

    def emit(start, stop, value):
        value = value.astype(jnp.bfloat16)
        keep_ref[:, start:stop] = value[:half]
        send_ref[:, start:stop] = value[half:]

    product(scaled, weight_ref, emit)


def gate_kernel(place_ref, rows_ref, gain_ref, gate_ref, keep_ref, send_ref, stream, sem):
    copy = pltpu.make_async_copy(rows_ref.at[place_ref[1]], stream, sem)
    copy.start()
    rows = rows_in_order(place_ref, rows_ref)
    half = rows.shape[0] // 2
    units = gate_ref.shape[1]
    tail = tail_of(jnp.sum(rows * rows, axis=1, keepdims=True))
    keep_ref[:, units:] = tail[:half]
    send_ref[:, units:] = tail[half:]
    half_product(rows, gain_ref, gate_ref, keep_ref, send_ref)
    copy.wait()


def up_kernel(place_ref, rows_ref, gain_ref, up_ref, keep_ref, send_ref):
    half_product(rows_in_order(place_ref, rows_ref), gain_ref, up_ref, keep_ref, send_ref)


def summed(own_ref, got_ref, start, stop):
    return own_ref[:, start:stop].astype(jnp.float32) + got_ref[:, start:stop].astype(jnp.float32)


def squares_of(own_ref, got_ref):
    start = own_ref.shape[1] - lanes
    tail = summed(own_ref, got_ref, start, start + lanes)
    return tail[:, 0:1] + tail[:, 1:2]


def gate_pair_kernel(own_ref, got_ref, out_ref):
    units = own_ref.shape[1] - lanes
    out_ref[:, :units] = summed(own_ref, got_ref, 0, units).astype(jnp.bfloat16)
    out_ref[:, units:] = tail_of(squares_of(own_ref, got_ref))


def up_pair_kernel(own_ref, got_ref, out_ref):
    out_ref[...] = summed(own_ref, got_ref, 0, own_ref.shape[1]).astype(jnp.bfloat16)


def hidden_kernel(own_gate, got_gate, own_up, got_up, out_ref):
    units = out_ref.shape[1]
    scale = lax.rsqrt(squares_of(own_gate, got_gate) / MODEL_WIDTH + norm_eps)
    gate = summed(own_gate, got_gate, 0, units) * scale
    up = summed(own_up, got_up, 0, units) * scale
    out_ref[...] = (jax.nn.silu(gate) * up).astype(jnp.bfloat16)


def down_kernel(place_ref, own_ref, got_ref, weight_ref, out_ref):
    hidden = jnp.concatenate([own_ref[...], got_ref[...]], axis=0)
    first = half_of(place_ref, out_ref.shape[0])
    product(hidden, weight_ref, functools.partial(scatter_rows, out_ref, first))


def total_kernel(got_ref, out_ref):
    total = got_ref[0].astype(jnp.float32)
    for i in range(1, got_ref.shape[0]):
        total += got_ref[i].astype(jnp.float32)
    out_ref[...] = total.astype(jnp.bfloat16)


def weighed(kernel, shapes, weights, scalar, *operands, copied=None):
    vmem = pl.BlockSpec(memory_space=pltpu.VMEM)
    outs = [jax.ShapeDtypeStruct(shape, jnp.bfloat16) for shape in shapes]
    out_specs, scratch = [vmem] * len(outs), []
    if copied is not None:
        outs.append(jax.ShapeDtypeStruct(copied, jnp.bfloat16))
        out_specs.append(pl.BlockSpec(memory_space=pltpu.HBM))
        scratch.append(pltpu.SemaphoreType.DMA(()))
    return pl.pallas_call(
        kernel,
        in_specs=[pl.BlockSpec(memory_space=pltpu.SMEM)]
        + [vmem] * (len(operands) + len(weights)),
        out_specs=out_specs,
        out_shape=outs,
        scratch_shapes=scratch,
        compiler_params=pltpu.CompilerParams(vmem_limit_bytes=8 << 20),
        cost_estimate=pl.CostEstimate(
            flops=sum(64 * w.size for w in weights),
            bytes_accessed=sum(2 * w.size for w in weights),
            transcendentals=0,
        ),
    )(scalar, *operands, *(pltpu.with_memory_space_constraint(w, pltpu.VMEM) for w in weights))


def per_device_dense(
    query,
    keys,
    values,
    chosen,
    residual,
    output_weight,
    norm_gain,
    gate_weight,
    up_weight,
    down_weight,
):
    _, heads, group, depth = query.shape
    ctx_count = lax.axis_size("ctx")
    mp_count = lax.axis_size("mp")
    mp_place = lax.axis_index("mp")
    own_part = lax.axis_index("ctx") * mp_count + mp_place
    all_rows = ctx_count * mp_count

    part = jnp.reshape(own_part, (1,))
    place = jnp.stack([mp_place, lax.axis_index("ctx")])
    chosen = jnp.transpose(chosen, (0, 2, 1))
    copies = small_call(
        copies_kernel, (ctx_count,) + query.shape[1:], query[0], flops=0
    )
    query_own = over_ctx(copies)
    keys, values = keys[0], values[0]
    query_core = swapped(query_own, 1)
    query_x = swapped(query_own, 2)
    keep_a, send_a, keys, values = attend(0, part, place, query_own, query_core, keys, values, chosen)
    query_x, _ = lax.optimization_barrier((query_x, send_a))
    query_far = swapped(query_x, 1)
    recv_a = swapped(send_a, 1)
    keep_b, send_b = attend(1, part, place, query_x, query_far, keys, values, chosen)
    recv_b = swapped(send_b, 1)
    on_chip = core_merge(0, keep_a, recv_a, group, depth)
    on_chip = core_merge(1, keep_b, recv_b, group, depth, into=on_chip)
    got = over_ctx(on_chip)
    half_rows = 2 * ctx_count
    width = group * depth
    column = small_call(
        functools.partial(ctx_kernel, group, depth), (half_rows, width + lanes), got
    )
    attended = small_call(
        functools.partial(x_kernel, group, depth), (half_rows, width), column, swapped(column, 2)
    )
    other = swapped(attended, 1)
    width = output_weight.shape[1]
    block = (ctx_count, mp_count, width)
    (projected,) = weighed(
        project_kernel, [block], (output_weight,), place, attended, other
    )
    copies = small_call(stream_kernel, block, over_ctx(projected), residual)
    rows = over_ctx(copies)
    units = gate_weight.shape[1]
    half = all_rows // 2
    gain = norm_gain.reshape(1, -1)
    keep, send, stream = weighed(
        gate_kernel, [(half, units + lanes)] * 2, (gate_weight,), place, rows, gain,
        copied=residual.shape,
    )
    recv = swapped(send, 1)
    keep_up, send_up = weighed(up_kernel, [(half, units)] * 2, (up_weight,), place, rows, gain)
    recv_up = swapped(send_up, 1)
    gate = small_call(gate_pair_kernel, keep.shape, keep, recv)
    got_gate = swapped(gate, 2)
    up = small_call(up_pair_kernel, keep_up.shape, keep_up, recv_up)
    got_up = swapped(up, 2)
    hidden = small_call(hidden_kernel, (half, units), gate, got_gate, up, got_up)
    (update,) = weighed(
        down_kernel, [block], (down_weight,), place, hidden, swapped(hidden, 1)
    )
    update = small_call(total_kernel, residual.shape, over_ctx(update))
    return (stream, update)


def either(*arrays):
    query, mp_count, ctx_count = arrays[0], lax.axis_size("mp"), lax.axis_size("ctx")
    rows, heads, group, depth = query.shape
    dense = (
        rows == 1
        and mp_count == 4
        and heads == ctx_count == group == 8
        and depth == lanes
        and arrays[1].shape[0] == 1
    )
    return (per_device_dense if dense else per_device)(*arrays)


def solution(mesh):
    return jax.shard_map(
        either,
        mesh=mesh,
        in_specs=(
            P(("ctx", "mp"), None, None, None),
            P(("ctx", "mp"), None, None, None),
            P(("ctx", "mp"), None, None, None),
            P(),
            P("ctx", "mp"),
            P("ctx", "mp"),
            P("mp"),
            P("mp", "ctx"),
            P("mp", "ctx"),
            P("ctx", "mp"),
        ),
        out_specs=(P("ctx", "mp"), P("ctx", "mp")),
        check_vma=False,
    )
```

```python
import functools
import math

import jax
import jax.numpy as jnp
from jax import lax
from jax.experimental import pallas as pl
from jax.experimental.pallas import tpu as pltpu
from jax.sharding import PartitionSpec as P

MODEL_WIDTH = 8192
KEPT_PARTITIONS = 16
ROW_DEV = 1


norm_eps = 1e-05
lowest_value = -1e30


def find_slots(listed, target, capacity):
    member = jnp.any(listed == target, axis=2)
    places = jnp.cumsum(member.astype(jnp.int32), axis=1) - 1
    live_count = jnp.sum(member.astype(jnp.int32), axis=1)
    slot_ranks = jnp.arange(capacity, dtype=jnp.int32)
    slot_hits = member[:, :, None] & (places[:, :, None] == slot_ranks[None, None, :])
    row_numbers = jnp.arange(listed.shape[1], dtype=jnp.int32)
    slot_rows = jnp.sum(jnp.where(slot_hits, row_numbers[None, :, None], 0), axis=1)
    slot_valid = slot_ranks[None, :] < live_count[:, None]
    return (slot_rows, slot_valid)


def global_scaling(block_max, block_sum, block_value, slot_rows, slot_valid, all_rows, head_ids):
    kv_heads, capacity, group_size = block_max.shape
    valid_wide = slot_valid[:, :, None]
    max_table = jnp.full((all_rows, kv_heads, group_size), lowest_value, jnp.float32)
    max_table = max_table.at[slot_rows, head_ids[:, None]].max(
        jnp.where(valid_wide, block_max, lowest_value)
    )
    row_top = lax.pmax(max_table.astype(jnp.bfloat16), ("ctx", "mp")).astype(max_table.dtype)
    factor = jnp.where(valid_wide, jnp.exp(block_max - row_top[slot_rows, head_ids[:, None]]), 0.0)
    return (block_value * factor[..., None], block_sum * factor)


def to_owners(array, kv_heads, capacity, per_head, ctx_count):
    shaped = array.reshape(kv_heads, capacity, per_head, -1)
    return jnp.transpose(shaped, (0, 2, 1, 3)).reshape(ctx_count, capacity, -1)


def per_device(
    query,
    keys,
    values,
    chosen,
    residual,
    output_weight,
    norm_gain,
    gate_weight,
    up_weight,
    down_weight,
):
    kv_heads = query.shape[1]
    group_size = query.shape[2]
    head_dim = query.shape[3]
    score_scale = head_dim ** (-0.5)
    ctx_count = lax.axis_size("ctx")
    mp_count = lax.axis_size("mp")
    ctx_place = lax.axis_index("ctx")
    mp_place = lax.axis_index("mp")
    own_part = ctx_place * mp_count + mp_place
    all_queries = lax.all_gather(query, ("ctx", "mp"), axis=0, tiled=True)
    all_rows = all_queries.shape[0]
    capacity = min(4 * ROW_DEV * KEPT_PARTITIONS, all_rows)
    slot_rows, slot_valid = find_slots(chosen, own_part, capacity)
    head_ids = jnp.arange(kv_heads, dtype=jnp.int32)
    picked = all_queries[slot_rows, head_ids[:, None]].reshape(
        kv_heads, capacity * group_size, head_dim
    )

    def attend(inputs):
        query_block, key_block, value_block = inputs
        scores = (
            lax.dot_general(
                query_block, key_block, (((1,), (1,)), ((), ())), preferred_element_type=jnp.float32
            )
            * score_scale
        )
        block_max = jnp.max(scores, axis=1)
        probs = jnp.exp(scores - block_max[:, None])
        block_sum = jnp.sum(probs, axis=1)
        block_value = jnp.dot(
            probs.astype(jnp.bfloat16), value_block, preferred_element_type=jnp.float32
        )
        return (block_max, block_sum, block_value)

    block_max, block_sum, block_value = lax.map(attend, (picked, keys[0], values[0]))
    block_max = block_max.reshape(kv_heads, capacity, group_size)
    block_sum = block_sum.reshape(kv_heads, capacity, group_size)
    block_value = block_value.reshape(kv_heads, capacity, group_size, head_dim)
    per_head = ctx_count // kv_heads
    feat_width = kv_heads * group_size * head_dim // ctx_count
    head_share = kv_heads * group_size // ctx_count
    own_head = ctx_place // per_head
    head_lists = lax.dynamic_index_in_dim(chosen, own_head, 0, keepdims=True)
    sources = jnp.arange(ctx_count, dtype=jnp.int32) * mp_count + mp_place
    source_rows = jax.vmap(lambda source: find_slots(head_lists, source, capacity)[0])(sources)[
        :, 0
    ]
    weighted, scaled_sum = global_scaling(
        block_max, block_sum, block_value, slot_rows, slot_valid, all_rows, head_ids
    )
    send_values = to_owners(weighted, kv_heads, capacity, per_head, ctx_count)
    send_sums = to_owners(scaled_sum, kv_heads, capacity, per_head, ctx_count)
    got_values, got_sums = (
        lax.all_to_all(
            send_values.astype(jnp.bfloat16), "ctx", split_axis=0, concat_axis=0, tiled=True
        ).astype(send_values.dtype),
        lax.all_to_all(
            send_sums.astype(jnp.bfloat16), "ctx", split_axis=0, concat_axis=0, tiled=True
        ).astype(send_sums.dtype),
    )
    numerator = jnp.zeros((all_rows, feat_width), jnp.float32).at[source_rows].add(got_values)
    denominator = jnp.zeros((all_rows, head_share), jnp.float32).at[source_rows].add(got_sums)
    numerator, denominator = (
        lax.psum(numerator.astype(jnp.bfloat16), "mp").astype(jnp.float32),
        lax.psum(denominator.astype(jnp.bfloat16), "mp").astype(jnp.float32),
    )
    attended = (
        (numerator.reshape(all_rows, -1, head_dim) / denominator[:, :, None])
        .reshape(all_rows, -1)
        .astype(jnp.bfloat16)
    )
    rows_here = attended
    projected = lax.psum_scatter(
        jnp.dot(rows_here, output_weight, preferred_element_type=jnp.float32),
        "ctx",
        scatter_dimension=0,
        tiled=True,
    )
    stream = (residual.astype(jnp.float32) + projected).astype(jnp.bfloat16)
    stream_wide = stream.astype(jnp.float32)
    squares = lax.psum(jnp.sum(stream_wide * stream_wide, axis=1), "mp")
    normed = (
        stream_wide * lax.rsqrt(squares / MODEL_WIDTH + norm_eps)[:, None] * norm_gain
    ).astype(jnp.bfloat16)
    row_piece = lax.all_gather(normed, "ctx", axis=0, tiled=True)
    gate_piece = jnp.dot(row_piece, gate_weight, preferred_element_type=jnp.float32)
    up_piece = jnp.dot(row_piece, up_weight, preferred_element_type=jnp.float32)
    gate_up = jnp.stack([gate_piece, up_piece], axis=1)
    gate_up = lax.psum(gate_up.astype(jnp.bfloat16), "mp").astype(jnp.float32)
    hidden = (jax.nn.silu(gate_up[:, 0]) * gate_up[:, 1]).astype(jnp.bfloat16)
    rows_here = hidden
    update = lax.psum_scatter(
        jnp.dot(rows_here, down_weight, preferred_element_type=jnp.float32),
        "ctx",
        scatter_dimension=0,
        tiled=True,
    ).astype(jnp.bfloat16)
    return (stream, update)


lanes = 128
chunk = 512
ahead = 4
columns_at_once = 256
ahead = 4
log2_e = math.log2(math.e)


def swapped(array, bit):
    count = lax.axis_size("mp")
    return lax.ppermute(array, "mp", [(i, i ^ bit) for i in range(count)])


def over_ctx(array):
    return lax.all_to_all(array, "ctx", split_axis=0, concat_axis=0, tiled=True)


def copies_kernel(in_ref, out_ref):
    for i in range(out_ref.shape[0]):
        out_ref[i] = in_ref[...]


def split_stat(value):
    high = value.astype(jnp.bfloat16).astype(jnp.float32)
    return high, value - high


def attend_kernel(pair, part_ref, query_a, query_b, keys, values, chosen, *refs):
    if pair == 0:
        keep_ref, send_ref, key_ref, value_ref = refs[:4]
    else:
        keep_ref, send_ref = refs[:2]
        key_ref, value_ref = keys, values
    score_s, top_s, out_s, lse_s, chosen_ref, sems, chosen_sem = refs[-7:]
    rows, heads, group, depth = query_a.shape
    count = key_ref.shape[1]
    scale = depth ** (-0.5)
    lane = lax.broadcasted_iota(jnp.int32, (rows, lanes), 1)
    listed = chosen_ref.shape[2]
    row_lane = lax.broadcasted_iota(jnp.int32, (rows, listed), 1)
    row_place = lax.broadcasted_iota(jnp.int32, (rows, listed), 0) * (listed // rows)
    chosen_copy = pltpu.make_async_copy(chosen, chosen_ref, chosen_sem)

    def arrivals(h):
        return (
            pltpu.make_async_copy(keys.at[h], key_ref.at[h], sems.at[0, h]),
            pltpu.make_async_copy(values.at[h], value_ref.at[h], sems.at[1, h]),
        )

    def send_for(h):
        if pair == 0:
            for copy in arrivals(h):
                copy.start()

    def wait_for(h):
        if pair == 0:
            for copy in arrivals(h):
                copy.wait()

    def query_of(h):
        return jnp.concatenate(
            [
                q[:, h].astype(jnp.float32).reshape(rows * group, depth)
                for q in (query_a, query_b)
            ],
            axis=0,
        ).astype(jnp.bfloat16)

    def score(query, h, slot, i, top):
        window = slice(i * chunk, (i + 1) * chunk)
        scores = lax.dot_general(
            query, key_ref[h, window, :], (((1,), (1,)), ((), ())),
            preferred_element_type=jnp.float32,
        )
        score_s[slot, :, window] = scores
        for j in range(chunk // lanes):
            part = scores[:, j * lanes : (j + 1) * lanes]
            top = part if top is None else jnp.maximum(top, part)
        return top

    def spent(h, slot, i, top, mixed):
        window = slice(i * chunk, (i + 1) * chunk)
        probs = jnp.exp2((score_s[slot, :, window] - top) * (scale * log2_e))
        ones = jnp.ones((chunk, lanes), jnp.bfloat16)
        part = jnp.dot(
            probs.astype(jnp.bfloat16),
            jnp.concatenate([value_ref[h, window, :], ones], axis=1),
            preferred_element_type=jnp.float32,
        )
        return part if mixed is None else mixed + part

    def finish(h, slot, top, mixed):
        total = mixed[:, depth:]
        out_s[slot] = mixed[:, :depth] * (1.0 / total)
        lse_s[slot] = top * scale + jnp.log(total)
        member = jnp.where(chosen_ref[h] == part_ref[0], 1.0, 0.0)
        member = jnp.max(member, axis=0, keepdims=True)
        for part, ref in enumerate((keep_ref, send_ref)):
            row = row_place + (lax.rem(part_ref[0], listed // rows) ^ (2 * pair + part))
            held = jnp.where(row_lane == row, member, 0.0)
            bias = jnp.where(jnp.max(held, axis=1, keepdims=True) > 0.5, 0.0, lowest_value)
            stats = jnp.zeros((rows, lanes), jnp.float32)
            for g in range(group):
                window = pl.ds(part * rows * group + g, rows, stride=group)
                ref[h, :, g * depth : (g + 1) * depth] = out_s[slot, window, :].astype(jnp.bfloat16)
                high, low = split_stat(lse_s[slot, window, :] + bias)
                stats = jnp.where(lane == g, high, jnp.where(lane == group + g, low, stats))
            ref[h, :, group * depth :] = stats.astype(jnp.bfloat16)

    def both(h, slot, following, after):
        top = jnp.max(top_s[slot], axis=1, keepdims=True)
        query = query_of(following)
        mixed = later = None
        for i in range(count // chunk):
            mixed = spent(h, slot, i, top, mixed)
            later = score(query, following, after, i, later)
        top_s[after] = later
        finish(h, slot, top, mixed)

    for h in range(min(ahead, heads)):
        send_for(h)
    chosen_copy.start()
    wait_for(0)
    query, top = query_of(0), None
    for i in range(count // chunk):
        top = score(query, 0, 0, i, top)
    top_s[0] = top
    chosen_copy.wait()

    @pl.loop(0, heads // 2)
    def _(step):
        h = 2 * step
        wait_for(h + 1)
        both(h, 0, h + 1, 1)

        @pl.when(h + 2 < heads)
        def _():
            wait_for(h + 2)

        for i in range(2):

            @pl.when(h + ahead + i < heads)
            def _():
                send_for(h + ahead + i)

        both(h + 1, 1, jnp.minimum(h + 2, heads - 1), 0)


def attend(pair, part, query_a, query_b, keys, values, chosen):
    rows, heads, group, depth = query_a.shape
    count = keys.shape[1]
    width = group * depth + lanes
    shape = jax.ShapeDtypeStruct((heads, rows, width), jnp.bfloat16)
    held = [pltpu.VMEM(a.shape, a.dtype) for a in (keys, values)]
    vmem, hbm = pl.BlockSpec(memory_space=pltpu.VMEM), pl.BlockSpec(memory_space=pltpu.HBM)
    space = pltpu.VMEM if pair else pltpu.HBM
    return pl.pallas_call(
        functools.partial(attend_kernel, pair),
        in_specs=[pl.BlockSpec(memory_space=pltpu.SMEM)]
        + [vmem] * 2
        + [vmem if pair else hbm] * 2
        + [hbm],
        out_specs=[vmem] * (2 if pair else 4),
        out_shape=[shape, shape] + ([] if pair else held),
        scratch_shapes=[
            pltpu.VMEM((2, 2 * rows * group, count), jnp.float32),
            pltpu.VMEM((2, 2 * rows * group, lanes), jnp.float32),
            pltpu.VMEM((2, 2 * rows * group, depth), jnp.float32),
            pltpu.VMEM((2, 2 * rows * group, lanes), jnp.float32),
            pltpu.VMEM(chosen.shape, chosen.dtype),
            pltpu.SemaphoreType.DMA((2, heads)),
            pltpu.SemaphoreType.DMA(()),
        ],
        compiler_params=pltpu.CompilerParams(vmem_limit_bytes=10 << 20),
        cost_estimate=pl.CostEstimate(
            flops=(1 + 4 * pair) * 8 * heads * rows * group * depth * count,
            bytes_accessed=4 * heads * count * depth,
            transcendentals=2 * heads * rows * group * count,
        ),
    )(
        part,
        query_a,
        query_b,
        pltpu.with_memory_space_constraint(keys, space),
        pltpu.with_memory_space_constraint(values, space),
        pltpu.with_memory_space_constraint(chosen, pltpu.HBM),
    )


def merged(parts, group, depth):
    stats = [part[:, group * depth :] for part in parts]
    lses = [s + pltpu.roll(s, lanes - group, 1) for s in stats]
    top = functools.reduce(jnp.maximum, lses)
    weights = [jnp.exp(lse - top) for lse in lses]
    total = functools.reduce(jnp.add, weights)
    inverse = 1.0 / total
    weights = [w * inverse for w in weights]
    values = []
    for g in range(group):
        values.append(
            functools.reduce(
                jnp.add,
                [
                    w[:, g : g + 1] * part[:, g * depth : (g + 1) * depth]
                    for w, part in zip(weights, parts)
                ],
            )
        )
    return values, top + jnp.log(total)


def packed_stat(lse, group):
    lane = lax.broadcasted_iota(jnp.int32, lse.shape, 1)
    high, low = split_stat(lse)
    low = pltpu.roll(low, group, 1)
    return jnp.where(lane < group, high, jnp.where(lane < 2 * group, low, 0.0))


def core_kernel(group, depth, part, keep_ref, recv_ref, *refs):
    out_ref = refs[-1]
    heads, rows, _ = keep_ref.shape
    where = slice(part * rows, (part + 1) * rows)

    for h in range(heads):
        values, lse = merged(
            [keep_ref[h].astype(jnp.float32), recv_ref[h].astype(jnp.float32)], group, depth
        )
        for g in range(group):
            out_ref[h, where, g * depth : (g + 1) * depth] = values[g].astype(jnp.bfloat16)
        out_ref[h, where, group * depth :] = packed_stat(lse, group).astype(jnp.bfloat16)


def core_merge(part, keep, recv, group, depth, into=None):
    heads, rows, width = keep.shape
    more = [] if into is None else [into]
    vmem = pl.BlockSpec(memory_space=pltpu.VMEM)
    return pl.pallas_call(
        functools.partial(core_kernel, group, depth, part),
        in_specs=[vmem] * (2 + len(more)),
        out_specs=vmem,
        out_shape=jax.ShapeDtypeStruct((heads, 2 * rows, width), jnp.bfloat16),
        input_output_aliases={2: 0} if more else {},
        compiler_params=pltpu.CompilerParams(vmem_limit_bytes=8 << 20),
    )(keep, recv, *more)


def ctx_kernel(group, depth, got_ref, out_ref):
    values, lse = merged(
        [got_ref[s].astype(jnp.float32) for s in range(got_ref.shape[0])], group, depth
    )
    for g in range(group):
        out_ref[:, g * depth : (g + 1) * depth] = values[g].astype(jnp.bfloat16)
    out_ref[:, group * depth :] = packed_stat(lse, group).astype(jnp.bfloat16)


def x_kernel(group, depth, own_ref, got_ref, out_ref):
    half = own_ref.shape[0] // 2
    own = own_ref[...].astype(jnp.float32)
    got = got_ref[...].astype(jnp.float32)
    got = jnp.concatenate([got[half:], got[:half]], axis=0)
    values, _ = merged([own, got], group, depth)
    for g in range(group):
        out_ref[:, g * depth : (g + 1) * depth] = values[g].astype(jnp.bfloat16)


def small_call(kernel, shapes, *operands, flops=0):
    return pl.pallas_call(
        kernel,
        out_shape=jax.tree.map(
            lambda shape: jax.ShapeDtypeStruct(shape, jnp.bfloat16),
            shapes,
            is_leaf=lambda x: isinstance(x, tuple),
        ),
        compiler_params=pltpu.CompilerParams(vmem_limit_bytes=8 << 20),
        cost_estimate=pl.CostEstimate(flops=flops, bytes_accessed=1 << 19, transcendentals=0),
    )(*operands)


def scatter_rows(out_ref, first, start, stop, value):
    count, step, _ = out_ref.shape
    for i in range(count):
        where = i if first is None else lax.rem(first + i, count)
        out_ref[where, :, start:stop] = value[i * step : (i + 1) * step].astype(out_ref.dtype)


def stream_kernel(got_ref, residual_ref, copies_ref):
    total = residual_ref[...].astype(jnp.float32)
    partial = got_ref[0].astype(jnp.float32)
    for i in range(1, got_ref.shape[0]):
        partial += got_ref[i].astype(jnp.float32)
    stream = (total + partial).astype(jnp.bfloat16)
    for i in range(copies_ref.shape[0]):
        copies_ref[i] = stream


def product(left, weight_ref, emit):
    width = weight_ref.shape[1]
    for start in range(0, width, columns_at_once):
        stop = min(start + columns_at_once, width)
        emit(
            start,
            stop,
            jnp.dot(left, weight_ref[:, start:stop], preferred_element_type=jnp.float32),
        )


def project_kernel(part_ref, own_ref, got_ref, weight_ref, out_ref):
    rows = out_ref.shape[0] * out_ref.shape[1]
    half = rows // 2
    quarter = rows // 4
    place = lax.rem(part_ref[0], out_ref.shape[1])
    target = lax.broadcasted_iota(jnp.int32, (rows, half), 0)
    source = lax.broadcasted_iota(jnp.int32, (rows, half), 1)
    row = (source % quarter) * 4
    column = 2 * (source // quarter)
    own_order = jnp.where(target == row + (place ^ column), 1.0, 0.0).astype(jnp.bfloat16)
    got_order = jnp.where(target == row + (place ^ (column + 1)), 1.0, 0.0).astype(jnp.bfloat16)
    attended = jnp.dot(own_order, own_ref[...], preferred_element_type=jnp.float32) + jnp.dot(
        got_order, got_ref[...], preferred_element_type=jnp.float32
    )
    product(
        attended.astype(jnp.bfloat16), weight_ref, functools.partial(scatter_rows, out_ref, None)
    )


def tail_of(squares):
    lane = lax.broadcasted_iota(jnp.int32, (squares.shape[0], lanes), 1)
    high, low = split_stat(squares)
    return jnp.where(lane == 0, high, jnp.where(lane == 1, low, 0.0)).astype(jnp.bfloat16)


def half_of(part_ref, count):
    return (part_ref[0] & 1) * (count // 2)


def rows_in_order(part_ref, rows_ref):
    count = rows_ref.shape[0]
    first = half_of(part_ref, count)
    return jnp.concatenate(
        [rows_ref[lax.rem(first + i, count)].astype(jnp.float32) for i in range(count)], axis=0
    )


def half_product(rows, gain_ref, weight_ref, keep_ref, send_ref):
    half = rows.shape[0] // 2
    scaled = (rows * gain_ref[...]).astype(jnp.bfloat16)

    def emit(start, stop, value):
        value = value.astype(jnp.bfloat16)
        keep_ref[:, start:stop] = value[:half]
        send_ref[:, start:stop] = value[half:]

    product(scaled, weight_ref, emit)


def gate_kernel(part_ref, rows_ref, gain_ref, gate_ref, keep_ref, send_ref, stream, sem):
    copy = pltpu.make_async_copy(rows_ref.at[part_ref[0] // rows_ref.shape[1]], stream, sem)
    copy.start()
    rows = rows_in_order(part_ref, rows_ref)
    half = rows.shape[0] // 2
    units = gate_ref.shape[1]
    tail = tail_of(jnp.sum(rows * rows, axis=1, keepdims=True))
    keep_ref[:, units:] = tail[:half]
    send_ref[:, units:] = tail[half:]
    half_product(rows, gain_ref, gate_ref, keep_ref, send_ref)
    copy.wait()


def up_kernel(part_ref, rows_ref, gain_ref, up_ref, keep_ref, send_ref):
    half_product(rows_in_order(part_ref, rows_ref), gain_ref, up_ref, keep_ref, send_ref)


def summed(own_ref, got_ref, start, stop):
    return own_ref[:, start:stop].astype(jnp.float32) + got_ref[:, start:stop].astype(jnp.float32)


def squares_of(own_ref, got_ref):
    start = own_ref.shape[1] - lanes
    tail = summed(own_ref, got_ref, start, start + lanes)
    return tail[:, 0:1] + tail[:, 1:2]


def gate_pair_kernel(own_ref, got_ref, out_ref):
    units = own_ref.shape[1] - lanes
    out_ref[:, :units] = summed(own_ref, got_ref, 0, units).astype(jnp.bfloat16)
    out_ref[:, units:] = tail_of(squares_of(own_ref, got_ref))


def up_pair_kernel(own_ref, got_ref, out_ref):
    out_ref[...] = summed(own_ref, got_ref, 0, own_ref.shape[1]).astype(jnp.bfloat16)


def hidden_kernel(own_gate, got_gate, own_up, got_up, out_ref):
    units = out_ref.shape[1]
    scale = lax.rsqrt(squares_of(own_gate, got_gate) / MODEL_WIDTH + norm_eps)
    gate = summed(own_gate, got_gate, 0, units) * scale
    up = summed(own_up, got_up, 0, units) * scale
    out_ref[...] = (jax.nn.silu(gate) * up).astype(jnp.bfloat16)


def down_kernel(part_ref, own_ref, got_ref, weight_ref, out_ref):
    hidden = jnp.concatenate([own_ref[...], got_ref[...]], axis=0)
    first = half_of(part_ref, out_ref.shape[0])
    product(hidden, weight_ref, functools.partial(scatter_rows, out_ref, first))


def total_kernel(got_ref, out_ref):
    total = got_ref[0].astype(jnp.float32)
    for i in range(1, got_ref.shape[0]):
        total += got_ref[i].astype(jnp.float32)
    out_ref[...] = total.astype(jnp.bfloat16)


def weighed(kernel, shapes, weights, scalar, *operands, copied=None):
    vmem = pl.BlockSpec(memory_space=pltpu.VMEM)
    outs = [jax.ShapeDtypeStruct(shape, jnp.bfloat16) for shape in shapes]
    out_specs, scratch = [vmem] * len(outs), []
    if copied is not None:
        outs.append(jax.ShapeDtypeStruct(copied, jnp.bfloat16))
        out_specs.append(pl.BlockSpec(memory_space=pltpu.HBM))
        scratch.append(pltpu.SemaphoreType.DMA(()))
    return pl.pallas_call(
        kernel,
        in_specs=[pl.BlockSpec(memory_space=pltpu.SMEM)]
        + [vmem] * (len(operands) + len(weights)),
        out_specs=out_specs,
        out_shape=outs,
        scratch_shapes=scratch,
        compiler_params=pltpu.CompilerParams(vmem_limit_bytes=8 << 20),
        cost_estimate=pl.CostEstimate(
            flops=sum(64 * w.size for w in weights),
            bytes_accessed=sum(2 * w.size for w in weights),
            transcendentals=0,
        ),
    )(scalar, *operands, *(pltpu.with_memory_space_constraint(w, pltpu.VMEM) for w in weights))


def per_device_dense(
    query,
    keys,
    values,
    chosen,
    residual,
    output_weight,
    norm_gain,
    gate_weight,
    up_weight,
    down_weight,
):
    _, heads, group, depth = query.shape
    ctx_count = lax.axis_size("ctx")
    mp_count = lax.axis_size("mp")
    own_part = lax.axis_index("ctx") * mp_count + lax.axis_index("mp")
    all_rows = ctx_count * mp_count

    part = jnp.reshape(own_part, (1,))
    chosen = jnp.transpose(chosen, (0, 2, 1))
    copies = small_call(
        copies_kernel, (ctx_count,) + query.shape[1:], query[0], flops=0
    )
    query_own = over_ctx(copies)
    keys, values = keys[0], values[0]
    query_core = swapped(query_own, 1)
    query_x = swapped(query_own, 2)
    keep_a, send_a, keys, values = attend(0, part, query_own, query_core, keys, values, chosen)
    query_x, _ = lax.optimization_barrier((query_x, send_a))
    query_far = swapped(query_x, 1)
    recv_a = swapped(send_a, 1)
    keep_b, send_b = attend(1, part, query_x, query_far, keys, values, chosen)
    recv_b = swapped(send_b, 1)
    on_chip = core_merge(0, keep_a, recv_a, group, depth)
    on_chip = core_merge(1, keep_b, recv_b, group, depth, into=on_chip)
    got = over_ctx(on_chip)
    half_rows = 2 * ctx_count
    width = group * depth
    column = small_call(
        functools.partial(ctx_kernel, group, depth), (half_rows, width + lanes), got
    )
    attended = small_call(
        functools.partial(x_kernel, group, depth), (half_rows, width), column, swapped(column, 2)
    )
    other = swapped(attended, 1)
    width = output_weight.shape[1]
    block = (ctx_count, mp_count, width)
    (projected,) = weighed(
        project_kernel, [block], (output_weight,), part, attended, other
    )
    copies = small_call(stream_kernel, block, over_ctx(projected), residual)
    rows = over_ctx(copies)
    units = gate_weight.shape[1]
    half = all_rows // 2
    gain = norm_gain.reshape(1, -1)
    keep, send, stream = weighed(
        gate_kernel, [(half, units + lanes)] * 2, (gate_weight,), part, rows, gain,
        copied=residual.shape,
    )
    recv = swapped(send, 1)
    keep_up, send_up = weighed(up_kernel, [(half, units)] * 2, (up_weight,), part, rows, gain)
    recv_up = swapped(send_up, 1)
    gate = small_call(gate_pair_kernel, keep.shape, keep, recv)
    got_gate = swapped(gate, 2)
    up = small_call(up_pair_kernel, keep_up.shape, keep_up, recv_up)
    got_up = swapped(up, 2)
    hidden = small_call(hidden_kernel, (half, units), gate, got_gate, up, got_up)
    (update,) = weighed(
        down_kernel, [block], (down_weight,), part, hidden, swapped(hidden, 1)
    )
    update = small_call(total_kernel, residual.shape, over_ctx(update))
    return (stream, update)


def either(*arrays):
    query, mp_count, ctx_count = arrays[0], lax.axis_size("mp"), lax.axis_size("ctx")
    rows, heads, group, depth = query.shape
    dense = (
        rows == 1
        and mp_count == 4
        and heads == ctx_count == group == 8
        and depth == lanes
        and arrays[1].shape[0] == 1
    )
    return (per_device_dense if dense else per_device)(*arrays)


def solution(mesh):
    return jax.shard_map(
        either,
        mesh=mesh,
        in_specs=(
            P(("ctx", "mp"), None, None, None),
            P(("ctx", "mp"), None, None, None),
            P(("ctx", "mp"), None, None, None),
            P(),
            P("ctx", "mp"),
            P("ctx", "mp"),
            P("mp"),
            P("mp", "ctx"),
            P("mp", "ctx"),
            P("ctx", "mp"),
        ),
        out_specs=(P("ctx", "mp"), P("ctx", "mp")),
        check_vma=False,
    )
```

```python
import functools
import math

import jax
import jax.numpy as jnp
from jax import lax
from jax.experimental import pallas as pl
from jax.experimental.pallas import tpu as pltpu
from jax.sharding import PartitionSpec as P

MODEL_WIDTH = 8192
KEPT_PARTITIONS = 16
ROW_DEV = 1


norm_eps = 1e-05
lowest_value = -1e30


def find_slots(listed, target, capacity):
    member = jnp.any(listed == target, axis=2)
    places = jnp.cumsum(member.astype(jnp.int32), axis=1) - 1
    live_count = jnp.sum(member.astype(jnp.int32), axis=1)
    slot_ranks = jnp.arange(capacity, dtype=jnp.int32)
    slot_hits = member[:, :, None] & (places[:, :, None] == slot_ranks[None, None, :])
    row_numbers = jnp.arange(listed.shape[1], dtype=jnp.int32)
    slot_rows = jnp.sum(jnp.where(slot_hits, row_numbers[None, :, None], 0), axis=1)
    slot_valid = slot_ranks[None, :] < live_count[:, None]
    return (slot_rows, slot_valid)


def global_scaling(block_max, block_sum, block_value, slot_rows, slot_valid, all_rows, head_ids):
    kv_heads, capacity, group_size = block_max.shape
    valid_wide = slot_valid[:, :, None]
    max_table = jnp.full((all_rows, kv_heads, group_size), lowest_value, jnp.float32)
    max_table = max_table.at[slot_rows, head_ids[:, None]].max(
        jnp.where(valid_wide, block_max, lowest_value)
    )
    row_top = lax.pmax(max_table.astype(jnp.bfloat16), ("ctx", "mp")).astype(max_table.dtype)
    factor = jnp.where(valid_wide, jnp.exp(block_max - row_top[slot_rows, head_ids[:, None]]), 0.0)
    return (block_value * factor[..., None], block_sum * factor)


def to_owners(array, kv_heads, capacity, per_head, ctx_count):
    shaped = array.reshape(kv_heads, capacity, per_head, -1)
    return jnp.transpose(shaped, (0, 2, 1, 3)).reshape(ctx_count, capacity, -1)


def per_device(
    query,
    keys,
    values,
    chosen,
    residual,
    output_weight,
    norm_gain,
    gate_weight,
    up_weight,
    down_weight,
):
    kv_heads = query.shape[1]
    group_size = query.shape[2]
    head_dim = query.shape[3]
    score_scale = head_dim ** (-0.5)
    ctx_count = lax.axis_size("ctx")
    mp_count = lax.axis_size("mp")
    ctx_place = lax.axis_index("ctx")
    mp_place = lax.axis_index("mp")
    own_part = ctx_place * mp_count + mp_place
    all_queries = lax.all_gather(query, ("ctx", "mp"), axis=0, tiled=True)
    all_rows = all_queries.shape[0]
    capacity = min(4 * ROW_DEV * KEPT_PARTITIONS, all_rows)
    slot_rows, slot_valid = find_slots(chosen, own_part, capacity)
    head_ids = jnp.arange(kv_heads, dtype=jnp.int32)
    picked = all_queries[slot_rows, head_ids[:, None]].reshape(
        kv_heads, capacity * group_size, head_dim
    )

    def attend(inputs):
        query_block, key_block, value_block = inputs
        scores = (
            lax.dot_general(
                query_block, key_block, (((1,), (1,)), ((), ())), preferred_element_type=jnp.float32
            )
            * score_scale
        )
        block_max = jnp.max(scores, axis=1)
        probs = jnp.exp(scores - block_max[:, None])
        block_sum = jnp.sum(probs, axis=1)
        block_value = jnp.dot(
            probs.astype(jnp.bfloat16), value_block, preferred_element_type=jnp.float32
        )
        return (block_max, block_sum, block_value)

    block_max, block_sum, block_value = lax.map(attend, (picked, keys[0], values[0]))
    block_max = block_max.reshape(kv_heads, capacity, group_size)
    block_sum = block_sum.reshape(kv_heads, capacity, group_size)
    block_value = block_value.reshape(kv_heads, capacity, group_size, head_dim)
    per_head = ctx_count // kv_heads
    feat_width = kv_heads * group_size * head_dim // ctx_count
    head_share = kv_heads * group_size // ctx_count
    own_head = ctx_place // per_head
    head_lists = lax.dynamic_index_in_dim(chosen, own_head, 0, keepdims=True)
    sources = jnp.arange(ctx_count, dtype=jnp.int32) * mp_count + mp_place
    source_rows = jax.vmap(lambda source: find_slots(head_lists, source, capacity)[0])(sources)[
        :, 0
    ]
    weighted, scaled_sum = global_scaling(
        block_max, block_sum, block_value, slot_rows, slot_valid, all_rows, head_ids
    )
    send_values = to_owners(weighted, kv_heads, capacity, per_head, ctx_count)
    send_sums = to_owners(scaled_sum, kv_heads, capacity, per_head, ctx_count)
    got_values, got_sums = (
        lax.all_to_all(
            send_values.astype(jnp.bfloat16), "ctx", split_axis=0, concat_axis=0, tiled=True
        ).astype(send_values.dtype),
        lax.all_to_all(
            send_sums.astype(jnp.bfloat16), "ctx", split_axis=0, concat_axis=0, tiled=True
        ).astype(send_sums.dtype),
    )
    numerator = jnp.zeros((all_rows, feat_width), jnp.float32).at[source_rows].add(got_values)
    denominator = jnp.zeros((all_rows, head_share), jnp.float32).at[source_rows].add(got_sums)
    numerator, denominator = (
        lax.psum(numerator.astype(jnp.bfloat16), "mp").astype(jnp.float32),
        lax.psum(denominator.astype(jnp.bfloat16), "mp").astype(jnp.float32),
    )
    attended = (
        (numerator.reshape(all_rows, -1, head_dim) / denominator[:, :, None])
        .reshape(all_rows, -1)
        .astype(jnp.bfloat16)
    )
    rows_here = attended
    projected = lax.psum_scatter(
        jnp.dot(rows_here, output_weight, preferred_element_type=jnp.float32),
        "ctx",
        scatter_dimension=0,
        tiled=True,
    )
    stream = (residual.astype(jnp.float32) + projected).astype(jnp.bfloat16)
    stream_wide = stream.astype(jnp.float32)
    squares = lax.psum(jnp.sum(stream_wide * stream_wide, axis=1), "mp")
    normed = (
        stream_wide * lax.rsqrt(squares / MODEL_WIDTH + norm_eps)[:, None] * norm_gain
    ).astype(jnp.bfloat16)
    row_piece = lax.all_gather(normed, "ctx", axis=0, tiled=True)
    gate_piece = jnp.dot(row_piece, gate_weight, preferred_element_type=jnp.float32)
    up_piece = jnp.dot(row_piece, up_weight, preferred_element_type=jnp.float32)
    gate_up = jnp.stack([gate_piece, up_piece], axis=1)
    gate_up = lax.psum(gate_up.astype(jnp.bfloat16), "mp").astype(jnp.float32)
    hidden = (jax.nn.silu(gate_up[:, 0]) * gate_up[:, 1]).astype(jnp.bfloat16)
    rows_here = hidden
    update = lax.psum_scatter(
        jnp.dot(rows_here, down_weight, preferred_element_type=jnp.float32),
        "ctx",
        scatter_dimension=0,
        tiled=True,
    ).astype(jnp.bfloat16)
    return (stream, update)


lanes = 128
chunk = 512
ahead = 3
columns_at_once = 256
ahead = 3
log2_e = math.log2(math.e)


def swapped(array, bit):
    count = lax.axis_size("mp")
    return lax.ppermute(array, "mp", [(i, i ^ bit) for i in range(count)])


def over_ctx(array):
    return lax.all_to_all(array, "ctx", split_axis=0, concat_axis=0, tiled=True)


def copies_kernel(in_ref, out_ref):
    for i in range(out_ref.shape[0]):
        out_ref[i] = in_ref[...]


def split_stat(value):
    high = value.astype(jnp.bfloat16).astype(jnp.float32)
    return high, value - high


def attend_kernel(pair, part_ref, query_a, query_b, keys, values, chosen, *refs):
    if pair == 0:
        keep_ref, send_ref, key_ref, value_ref = refs[:4]
    else:
        keep_ref, send_ref = refs[:2]
        key_ref, value_ref = keys, values
    score_s, top_s, out_s, lse_s, chosen_ref, sems, chosen_sem = refs[-7:]
    rows, heads, group, depth = query_a.shape
    count = key_ref.shape[1]
    scale = depth ** (-0.5)
    lane = lax.broadcasted_iota(jnp.int32, (rows, lanes), 1)
    listed = chosen_ref.shape[2]
    row_lane = lax.broadcasted_iota(jnp.int32, (rows, listed), 1)
    row_place = lax.broadcasted_iota(jnp.int32, (rows, listed), 0) * (listed // rows)
    chosen_copy = pltpu.make_async_copy(chosen, chosen_ref, chosen_sem)

    def key_copy(h):
        return pltpu.make_async_copy(keys.at[h], key_ref.at[h], sems.at[0, h])

    def value_copy(h):
        return pltpu.make_async_copy(values.at[h], value_ref.at[h], sems.at[1, h])

    def send(copy_of, h):
        if pair == 0:
            if isinstance(h, int):
                copy_of(h).start()
            else:

                @pl.when(h < heads)
                def _():
                    copy_of(h).start()

    def wait(copy_of, h):
        if pair == 0:
            copy_of(h).wait()

    def query_of(h):
        return jnp.concatenate(
            [
                q[:, h].astype(jnp.float32).reshape(rows * group, depth)
                for q in (query_a, query_b)
            ],
            axis=0,
        ).astype(jnp.bfloat16)

    def score(query, h, slot, i, top):
        window = slice(i * chunk, (i + 1) * chunk)
        scores = lax.dot_general(
            query, key_ref[h, window, :], (((1,), (1,)), ((), ())),
            preferred_element_type=jnp.float32,
        )
        score_s[slot, :, window] = scores
        for j in range(chunk // lanes):
            part = scores[:, j * lanes : (j + 1) * lanes]
            top = part if top is None else jnp.maximum(top, part)
        return top

    def spent(h, slot, i, top, mixed):
        window = slice(i * chunk, (i + 1) * chunk)
        probs = jnp.exp2((score_s[slot, :, window] - top) * (scale * log2_e))
        ones = jnp.ones((chunk, lanes), jnp.bfloat16)
        part = jnp.dot(
            probs.astype(jnp.bfloat16),
            jnp.concatenate([value_ref[h, window, :], ones], axis=1),
            preferred_element_type=jnp.float32,
        )
        return part if mixed is None else mixed + part

    def finish(h, slot, top, mixed):
        total = mixed[:, depth:]
        out_s[slot] = mixed[:, :depth] * (1.0 / total)
        lse_s[slot] = top * scale + jnp.log(total)
        member = jnp.where(chosen_ref[h] == part_ref[0], 1.0, 0.0)
        member = jnp.max(member, axis=0, keepdims=True)
        for part, ref in enumerate((keep_ref, send_ref)):
            row = row_place + (lax.rem(part_ref[0], listed // rows) ^ (2 * pair + part))
            held = jnp.where(row_lane == row, member, 0.0)
            bias = jnp.where(jnp.max(held, axis=1, keepdims=True) > 0.5, 0.0, lowest_value)
            stats = jnp.zeros((rows, lanes), jnp.float32)
            for g in range(group):
                window = pl.ds(part * rows * group + g, rows, stride=group)
                ref[h, :, g * depth : (g + 1) * depth] = out_s[slot, window, :].astype(jnp.bfloat16)
                high, low = split_stat(lse_s[slot, window, :] + bias)
                stats = jnp.where(lane == g, high, jnp.where(lane == group + g, low, stats))
            ref[h, :, group * depth :] = stats.astype(jnp.bfloat16)

    def both(h, slot, following, after):
        top = jnp.max(top_s[slot], axis=1, keepdims=True)
        query = None if following is None else query_of(following)
        mixed = later = None
        for i in range(count // chunk):
            mixed = spent(h, slot, i, top, mixed)
            if query is not None:
                later = score(query, following, after, i, later)
        if query is not None:
            top_s[after] = later
        finish(h, slot, top, mixed)

    send(key_copy, 0)
    for h in range(ahead):
        send(value_copy, h)
        send(key_copy, h + 1)
    chosen_copy.start()
    wait(key_copy, 0)
    query, top = query_of(0), None
    for i in range(count // chunk):
        top = score(query, 0, 0, i, top)
    top_s[0] = top
    chosen_copy.wait()

    def turn(h, slot):
        wait(value_copy, h)
        wait(key_copy, h + 1)
        send(value_copy, h + ahead)
        send(key_copy, h + ahead + 1)
        both(h, slot, h + 1, 1 - slot)

    @pl.loop(0, heads // 2 - 1)
    def _(step):
        turn(2 * step, 0)
        turn(2 * step + 1, 1)

    wait(value_copy, heads - 2)
    wait(key_copy, heads - 1)
    both(heads - 2, 0, heads - 1, 1)
    wait(value_copy, heads - 1)
    both(heads - 1, 1, None, 0)


def attend(pair, part, query_a, query_b, keys, values, chosen):
    rows, heads, group, depth = query_a.shape
    count = keys.shape[1]
    width = group * depth + lanes
    shape = jax.ShapeDtypeStruct((heads, rows, width), jnp.bfloat16)
    held = [pltpu.VMEM(a.shape, a.dtype) for a in (keys, values)]
    vmem, hbm = pl.BlockSpec(memory_space=pltpu.VMEM), pl.BlockSpec(memory_space=pltpu.HBM)
    space = pltpu.VMEM if pair else pltpu.HBM
    return pl.pallas_call(
        functools.partial(attend_kernel, pair),
        in_specs=[pl.BlockSpec(memory_space=pltpu.SMEM)]
        + [vmem] * 2
        + [vmem if pair else hbm] * 2
        + [hbm],
        out_specs=[vmem] * (2 if pair else 4),
        out_shape=[shape, shape] + ([] if pair else held),
        scratch_shapes=[
            pltpu.VMEM((2, 2 * rows * group, count), jnp.float32),
            pltpu.VMEM((2, 2 * rows * group, lanes), jnp.float32),
            pltpu.VMEM((2, 2 * rows * group, depth), jnp.float32),
            pltpu.VMEM((2, 2 * rows * group, lanes), jnp.float32),
            pltpu.VMEM(chosen.shape, chosen.dtype),
            pltpu.SemaphoreType.DMA((2, heads)),
            pltpu.SemaphoreType.DMA(()),
        ],
        compiler_params=pltpu.CompilerParams(vmem_limit_bytes=10 << 20),
        cost_estimate=pl.CostEstimate(
            flops=(1 + 4 * pair) * 8 * heads * rows * group * depth * count,
            bytes_accessed=4 * heads * count * depth,
            transcendentals=2 * heads * rows * group * count,
        ),
    )(
        part,
        query_a,
        query_b,
        pltpu.with_memory_space_constraint(keys, space),
        pltpu.with_memory_space_constraint(values, space),
        pltpu.with_memory_space_constraint(chosen, pltpu.HBM),
    )


def merged(parts, group, depth):
    stats = [part[:, group * depth :] for part in parts]
    lses = [s + pltpu.roll(s, lanes - group, 1) for s in stats]
    top = functools.reduce(jnp.maximum, lses)
    weights = [jnp.exp(lse - top) for lse in lses]
    total = functools.reduce(jnp.add, weights)
    inverse = 1.0 / total
    weights = [w * inverse for w in weights]
    values = []
    for g in range(group):
        values.append(
            functools.reduce(
                jnp.add,
                [
                    w[:, g : g + 1] * part[:, g * depth : (g + 1) * depth]
                    for w, part in zip(weights, parts)
                ],
            )
        )
    return values, top + jnp.log(total)


def packed_stat(lse, group):
    lane = lax.broadcasted_iota(jnp.int32, lse.shape, 1)
    high, low = split_stat(lse)
    low = pltpu.roll(low, group, 1)
    return jnp.where(lane < group, high, jnp.where(lane < 2 * group, low, 0.0))


def core_kernel(group, depth, part, keep_ref, recv_ref, *refs):
    out_ref = refs[-1]
    heads, rows, _ = keep_ref.shape
    where = slice(part * rows, (part + 1) * rows)

    for h in range(heads):
        values, lse = merged(
            [keep_ref[h].astype(jnp.float32), recv_ref[h].astype(jnp.float32)], group, depth
        )
        for g in range(group):
            out_ref[h, where, g * depth : (g + 1) * depth] = values[g].astype(jnp.bfloat16)
        out_ref[h, where, group * depth :] = packed_stat(lse, group).astype(jnp.bfloat16)


def core_merge(part, keep, recv, group, depth, into=None):
    heads, rows, width = keep.shape
    more = [] if into is None else [into]
    vmem = pl.BlockSpec(memory_space=pltpu.VMEM)
    return pl.pallas_call(
        functools.partial(core_kernel, group, depth, part),
        in_specs=[vmem] * (2 + len(more)),
        out_specs=vmem,
        out_shape=jax.ShapeDtypeStruct((heads, 2 * rows, width), jnp.bfloat16),
        input_output_aliases={2: 0} if more else {},
        compiler_params=pltpu.CompilerParams(vmem_limit_bytes=8 << 20),
    )(keep, recv, *more)


def ctx_kernel(group, depth, got_ref, out_ref):
    values, lse = merged(
        [got_ref[s].astype(jnp.float32) for s in range(got_ref.shape[0])], group, depth
    )
    for g in range(group):
        out_ref[:, g * depth : (g + 1) * depth] = values[g].astype(jnp.bfloat16)
    out_ref[:, group * depth :] = packed_stat(lse, group).astype(jnp.bfloat16)


def x_kernel(group, depth, own_ref, got_ref, out_ref):
    half = own_ref.shape[0] // 2
    own = own_ref[...].astype(jnp.float32)
    got = got_ref[...].astype(jnp.float32)
    got = jnp.concatenate([got[half:], got[:half]], axis=0)
    values, _ = merged([own, got], group, depth)
    for g in range(group):
        out_ref[:, g * depth : (g + 1) * depth] = values[g].astype(jnp.bfloat16)


def small_call(kernel, shapes, *operands, flops=0):
    return pl.pallas_call(
        kernel,
        out_shape=jax.tree.map(
            lambda shape: jax.ShapeDtypeStruct(shape, jnp.bfloat16),
            shapes,
            is_leaf=lambda x: isinstance(x, tuple),
        ),
        compiler_params=pltpu.CompilerParams(vmem_limit_bytes=8 << 20),
        cost_estimate=pl.CostEstimate(flops=flops, bytes_accessed=1 << 19, transcendentals=0),
    )(*operands)


def scatter_rows(out_ref, first, start, stop, value):
    count, step, _ = out_ref.shape
    for i in range(count):
        where = i if first is None else lax.rem(first + i, count)
        out_ref[where, :, start:stop] = value[i * step : (i + 1) * step].astype(out_ref.dtype)


def stream_kernel(got_ref, residual_ref, copies_ref):
    total = residual_ref[...].astype(jnp.float32)
    partial = got_ref[0].astype(jnp.float32)
    for i in range(1, got_ref.shape[0]):
        partial += got_ref[i].astype(jnp.float32)
    stream = (total + partial).astype(jnp.bfloat16)
    for i in range(copies_ref.shape[0]):
        copies_ref[i] = stream


def product(left, weight_ref, emit):
    width = weight_ref.shape[1]
    for start in range(0, width, columns_at_once):
        stop = min(start + columns_at_once, width)
        emit(
            start,
            stop,
            jnp.dot(left, weight_ref[:, start:stop], preferred_element_type=jnp.float32),
        )


def project_kernel(part_ref, own_ref, got_ref, weight_ref, out_ref):
    rows = out_ref.shape[0] * out_ref.shape[1]
    half = rows // 2
    quarter = rows // 4
    place = lax.rem(part_ref[0], out_ref.shape[1])
    target = lax.broadcasted_iota(jnp.int32, (rows, half), 0)
    source = lax.broadcasted_iota(jnp.int32, (rows, half), 1)
    row = (source % quarter) * 4
    column = 2 * (source // quarter)
    own_order = jnp.where(target == row + (place ^ column), 1.0, 0.0).astype(jnp.bfloat16)
    got_order = jnp.where(target == row + (place ^ (column + 1)), 1.0, 0.0).astype(jnp.bfloat16)
    attended = jnp.dot(own_order, own_ref[...], preferred_element_type=jnp.float32) + jnp.dot(
        got_order, got_ref[...], preferred_element_type=jnp.float32
    )
    product(
        attended.astype(jnp.bfloat16), weight_ref, functools.partial(scatter_rows, out_ref, None)
    )


def tail_of(squares):
    lane = lax.broadcasted_iota(jnp.int32, (squares.shape[0], lanes), 1)
    high, low = split_stat(squares)
    return jnp.where(lane == 0, high, jnp.where(lane == 1, low, 0.0)).astype(jnp.bfloat16)


def half_of(part_ref, count):
    return (part_ref[0] & 1) * (count // 2)


def rows_in_order(part_ref, rows_ref):
    count = rows_ref.shape[0]
    first = half_of(part_ref, count)
    return jnp.concatenate(
        [rows_ref[lax.rem(first + i, count)].astype(jnp.float32) for i in range(count)], axis=0
    )


def half_product(rows, gain_ref, weight_ref, keep_ref, send_ref):
    half = rows.shape[0] // 2
    scaled = (rows * gain_ref[...]).astype(jnp.bfloat16)

    def emit(start, stop, value):
        value = value.astype(jnp.bfloat16)
        keep_ref[:, start:stop] = value[:half]
        send_ref[:, start:stop] = value[half:]

    product(scaled, weight_ref, emit)


def gate_kernel(part_ref, rows_ref, gain_ref, gate_ref, keep_ref, send_ref, stream, sem):
    copy = pltpu.make_async_copy(rows_ref.at[part_ref[0] // rows_ref.shape[1]], stream, sem)
    copy.start()
    rows = rows_in_order(part_ref, rows_ref)
    half = rows.shape[0] // 2
    units = gate_ref.shape[1]
    tail = tail_of(jnp.sum(rows * rows, axis=1, keepdims=True))
    keep_ref[:, units:] = tail[:half]
    send_ref[:, units:] = tail[half:]
    half_product(rows, gain_ref, gate_ref, keep_ref, send_ref)
    copy.wait()


def up_kernel(part_ref, rows_ref, gain_ref, up_ref, keep_ref, send_ref):
    half_product(rows_in_order(part_ref, rows_ref), gain_ref, up_ref, keep_ref, send_ref)


def summed(own_ref, got_ref, start, stop):
    return own_ref[:, start:stop].astype(jnp.float32) + got_ref[:, start:stop].astype(jnp.float32)


def squares_of(own_ref, got_ref):
    start = own_ref.shape[1] - lanes
    tail = summed(own_ref, got_ref, start, start + lanes)
    return tail[:, 0:1] + tail[:, 1:2]


def gate_pair_kernel(own_ref, got_ref, out_ref):
    units = own_ref.shape[1] - lanes
    out_ref[:, :units] = summed(own_ref, got_ref, 0, units).astype(jnp.bfloat16)
    out_ref[:, units:] = tail_of(squares_of(own_ref, got_ref))


def up_pair_kernel(own_ref, got_ref, out_ref):
    out_ref[...] = summed(own_ref, got_ref, 0, own_ref.shape[1]).astype(jnp.bfloat16)


def hidden_kernel(own_gate, got_gate, own_up, got_up, out_ref):
    units = out_ref.shape[1]
    scale = lax.rsqrt(squares_of(own_gate, got_gate) / MODEL_WIDTH + norm_eps)
    gate = summed(own_gate, got_gate, 0, units) * scale
    up = summed(own_up, got_up, 0, units) * scale
    out_ref[...] = (jax.nn.silu(gate) * up).astype(jnp.bfloat16)


def down_kernel(part_ref, own_ref, got_ref, weight_ref, out_ref):
    hidden = jnp.concatenate([own_ref[...], got_ref[...]], axis=0)
    first = half_of(part_ref, out_ref.shape[0])
    product(hidden, weight_ref, functools.partial(scatter_rows, out_ref, first))


def total_kernel(got_ref, out_ref):
    total = got_ref[0].astype(jnp.float32)
    for i in range(1, got_ref.shape[0]):
        total += got_ref[i].astype(jnp.float32)
    out_ref[...] = total.astype(jnp.bfloat16)


def weighed(kernel, shapes, weights, scalar, *operands, copied=None):
    vmem = pl.BlockSpec(memory_space=pltpu.VMEM)
    outs = [jax.ShapeDtypeStruct(shape, jnp.bfloat16) for shape in shapes]
    out_specs, scratch = [vmem] * len(outs), []
    if copied is not None:
        outs.append(jax.ShapeDtypeStruct(copied, jnp.bfloat16))
        out_specs.append(pl.BlockSpec(memory_space=pltpu.HBM))
        scratch.append(pltpu.SemaphoreType.DMA(()))
    return pl.pallas_call(
        kernel,
        in_specs=[pl.BlockSpec(memory_space=pltpu.SMEM)]
        + [vmem] * (len(operands) + len(weights)),
        out_specs=out_specs,
        out_shape=outs,
        scratch_shapes=scratch,
        compiler_params=pltpu.CompilerParams(vmem_limit_bytes=8 << 20),
        cost_estimate=pl.CostEstimate(
            flops=sum(64 * w.size for w in weights),
            bytes_accessed=sum(2 * w.size for w in weights),
            transcendentals=0,
        ),
    )(scalar, *operands, *(pltpu.with_memory_space_constraint(w, pltpu.VMEM) for w in weights))


def per_device_dense(
    query,
    keys,
    values,
    chosen,
    residual,
    output_weight,
    norm_gain,
    gate_weight,
    up_weight,
    down_weight,
):
    _, heads, group, depth = query.shape
    ctx_count = lax.axis_size("ctx")
    mp_count = lax.axis_size("mp")
    own_part = lax.axis_index("ctx") * mp_count + lax.axis_index("mp")
    all_rows = ctx_count * mp_count

    part = jnp.reshape(own_part, (1,))
    chosen = jnp.transpose(chosen, (0, 2, 1))
    copies = small_call(
        copies_kernel, (ctx_count,) + query.shape[1:], query[0], flops=0
    )
    query_own = over_ctx(copies)
    keys, values = keys[0], values[0]
    query_core = swapped(query_own, 1)
    query_x = swapped(query_own, 2)
    keep_a, send_a, keys, values = attend(0, part, query_own, query_core, keys, values, chosen)
    query_x, _ = lax.optimization_barrier((query_x, send_a))
    query_far = swapped(query_x, 1)
    recv_a = swapped(send_a, 1)
    keep_b, send_b = attend(1, part, query_x, query_far, keys, values, chosen)
    recv_b = swapped(send_b, 1)
    on_chip = core_merge(0, keep_a, recv_a, group, depth)
    on_chip = core_merge(1, keep_b, recv_b, group, depth, into=on_chip)
    got = over_ctx(on_chip)
    half_rows = 2 * ctx_count
    width = group * depth
    column = small_call(
        functools.partial(ctx_kernel, group, depth), (half_rows, width + lanes), got
    )
    attended = small_call(
        functools.partial(x_kernel, group, depth), (half_rows, width), column, swapped(column, 2)
    )
    other = swapped(attended, 1)
    width = output_weight.shape[1]
    block = (ctx_count, mp_count, width)
    (projected,) = weighed(
        project_kernel, [block], (output_weight,), part, attended, other
    )
    copies = small_call(stream_kernel, block, over_ctx(projected), residual)
    rows = over_ctx(copies)
    units = gate_weight.shape[1]
    half = all_rows // 2
    gain = norm_gain.reshape(1, -1)
    keep, send, stream = weighed(
        gate_kernel, [(half, units + lanes)] * 2, (gate_weight,), part, rows, gain,
        copied=residual.shape,
    )
    recv = swapped(send, 1)
    keep_up, send_up = weighed(up_kernel, [(half, units)] * 2, (up_weight,), part, rows, gain)
    recv_up = swapped(send_up, 1)
    gate = small_call(gate_pair_kernel, keep.shape, keep, recv)
    got_gate = swapped(gate, 2)
    up = small_call(up_pair_kernel, keep_up.shape, keep_up, recv_up)
    got_up = swapped(up, 2)
    hidden = small_call(hidden_kernel, (half, units), gate, got_gate, up, got_up)
    (update,) = weighed(
        down_kernel, [block], (down_weight,), part, hidden, swapped(hidden, 1)
    )
    update = small_call(total_kernel, residual.shape, over_ctx(update))
    return (stream, update)


def either(*arrays):
    query, mp_count, ctx_count = arrays[0], lax.axis_size("mp"), lax.axis_size("ctx")
    rows, heads, group, depth = query.shape
    dense = (
        rows == 1
        and mp_count == 4
        and heads == ctx_count == group == 8
        and depth == lanes
        and arrays[1].shape[0] == 1
    )
    return (per_device_dense if dense else per_device)(*arrays)


def solution(mesh):
    return jax.shard_map(
        either,
        mesh=mesh,
        in_specs=(
            P(("ctx", "mp"), None, None, None),
            P(("ctx", "mp"), None, None, None),
            P(("ctx", "mp"), None, None, None),
            P(),
            P("ctx", "mp"),
            P("ctx", "mp"),
            P("mp"),
            P("mp", "ctx"),
            P("mp", "ctx"),
            P("ctx", "mp"),
        ),
        out_specs=(P("ctx", "mp"), P("ctx", "mp")),
        check_vma=False,
    )
```

```python
import functools
import math

import jax
import jax.numpy as jnp
from jax import lax
from jax.experimental import pallas as pl
from jax.experimental.pallas import tpu as pltpu
from jax.sharding import PartitionSpec as P

MODEL_WIDTH = 8192
KEPT_PARTITIONS = 16
ROW_DEV = 1


norm_eps = 1e-05
lowest_value = -1e30


def find_slots(listed, target, capacity):
    member = jnp.any(listed == target, axis=2)
    places = jnp.cumsum(member.astype(jnp.int32), axis=1) - 1
    live_count = jnp.sum(member.astype(jnp.int32), axis=1)
    slot_ranks = jnp.arange(capacity, dtype=jnp.int32)
    slot_hits = member[:, :, None] & (places[:, :, None] == slot_ranks[None, None, :])
    row_numbers = jnp.arange(listed.shape[1], dtype=jnp.int32)
    slot_rows = jnp.sum(jnp.where(slot_hits, row_numbers[None, :, None], 0), axis=1)
    slot_valid = slot_ranks[None, :] < live_count[:, None]
    return (slot_rows, slot_valid)


def global_scaling(block_max, block_sum, block_value, slot_rows, slot_valid, all_rows, head_ids):
    kv_heads, capacity, group_size = block_max.shape
    valid_wide = slot_valid[:, :, None]
    max_table = jnp.full((all_rows, kv_heads, group_size), lowest_value, jnp.float32)
    max_table = max_table.at[slot_rows, head_ids[:, None]].max(
        jnp.where(valid_wide, block_max, lowest_value)
    )
    row_top = lax.pmax(max_table.astype(jnp.bfloat16), ("ctx", "mp")).astype(max_table.dtype)
    factor = jnp.where(valid_wide, jnp.exp(block_max - row_top[slot_rows, head_ids[:, None]]), 0.0)
    return (block_value * factor[..., None], block_sum * factor)


def to_owners(array, kv_heads, capacity, per_head, ctx_count):
    shaped = array.reshape(kv_heads, capacity, per_head, -1)
    return jnp.transpose(shaped, (0, 2, 1, 3)).reshape(ctx_count, capacity, -1)


def per_device(
    query,
    keys,
    values,
    chosen,
    residual,
    output_weight,
    norm_gain,
    gate_weight,
    up_weight,
    down_weight,
):
    kv_heads = query.shape[1]
    group_size = query.shape[2]
    head_dim = query.shape[3]
    score_scale = head_dim ** (-0.5)
    ctx_count = lax.axis_size("ctx")
    mp_count = lax.axis_size("mp")
    ctx_place = lax.axis_index("ctx")
    mp_place = lax.axis_index("mp")
    own_part = ctx_place * mp_count + mp_place
    all_queries = lax.all_gather(query, ("ctx", "mp"), axis=0, tiled=True)
    all_rows = all_queries.shape[0]
    capacity = min(4 * ROW_DEV * KEPT_PARTITIONS, all_rows)
    slot_rows, slot_valid = find_slots(chosen, own_part, capacity)
    head_ids = jnp.arange(kv_heads, dtype=jnp.int32)
    picked = all_queries[slot_rows, head_ids[:, None]].reshape(
        kv_heads, capacity * group_size, head_dim
    )

    def attend(inputs):
        query_block, key_block, value_block = inputs
        scores = (
            lax.dot_general(
                query_block, key_block, (((1,), (1,)), ((), ())), preferred_element_type=jnp.float32
            )
            * score_scale
        )
        block_max = jnp.max(scores, axis=1)
        probs = jnp.exp(scores - block_max[:, None])
        block_sum = jnp.sum(probs, axis=1)
        block_value = jnp.dot(
            probs.astype(jnp.bfloat16), value_block, preferred_element_type=jnp.float32
        )
        return (block_max, block_sum, block_value)

    block_max, block_sum, block_value = lax.map(attend, (picked, keys[0], values[0]))
    block_max = block_max.reshape(kv_heads, capacity, group_size)
    block_sum = block_sum.reshape(kv_heads, capacity, group_size)
    block_value = block_value.reshape(kv_heads, capacity, group_size, head_dim)
    per_head = ctx_count // kv_heads
    feat_width = kv_heads * group_size * head_dim // ctx_count
    head_share = kv_heads * group_size // ctx_count
    own_head = ctx_place // per_head
    head_lists = lax.dynamic_index_in_dim(chosen, own_head, 0, keepdims=True)
    sources = jnp.arange(ctx_count, dtype=jnp.int32) * mp_count + mp_place
    source_rows = jax.vmap(lambda source: find_slots(head_lists, source, capacity)[0])(sources)[
        :, 0
    ]
    weighted, scaled_sum = global_scaling(
        block_max, block_sum, block_value, slot_rows, slot_valid, all_rows, head_ids
    )
    send_values = to_owners(weighted, kv_heads, capacity, per_head, ctx_count)
    send_sums = to_owners(scaled_sum, kv_heads, capacity, per_head, ctx_count)
    got_values, got_sums = (
        lax.all_to_all(
            send_values.astype(jnp.bfloat16), "ctx", split_axis=0, concat_axis=0, tiled=True
        ).astype(send_values.dtype),
        lax.all_to_all(
            send_sums.astype(jnp.bfloat16), "ctx", split_axis=0, concat_axis=0, tiled=True
        ).astype(send_sums.dtype),
    )
    numerator = jnp.zeros((all_rows, feat_width), jnp.float32).at[source_rows].add(got_values)
    denominator = jnp.zeros((all_rows, head_share), jnp.float32).at[source_rows].add(got_sums)
    numerator, denominator = (
        lax.psum(numerator.astype(jnp.bfloat16), "mp").astype(jnp.float32),
        lax.psum(denominator.astype(jnp.bfloat16), "mp").astype(jnp.float32),
    )
    attended = (
        (numerator.reshape(all_rows, -1, head_dim) / denominator[:, :, None])
        .reshape(all_rows, -1)
        .astype(jnp.bfloat16)
    )
    rows_here = attended
    projected = lax.psum_scatter(
        jnp.dot(rows_here, output_weight, preferred_element_type=jnp.float32),
        "ctx",
        scatter_dimension=0,
        tiled=True,
    )
    stream = (residual.astype(jnp.float32) + projected).astype(jnp.bfloat16)
    stream_wide = stream.astype(jnp.float32)
    squares = lax.psum(jnp.sum(stream_wide * stream_wide, axis=1), "mp")
    normed = (
        stream_wide * lax.rsqrt(squares / MODEL_WIDTH + norm_eps)[:, None] * norm_gain
    ).astype(jnp.bfloat16)
    row_piece = lax.all_gather(normed, "ctx", axis=0, tiled=True)
    gate_piece = jnp.dot(row_piece, gate_weight, preferred_element_type=jnp.float32)
    up_piece = jnp.dot(row_piece, up_weight, preferred_element_type=jnp.float32)
    gate_up = jnp.stack([gate_piece, up_piece], axis=1)
    gate_up = lax.psum(gate_up.astype(jnp.bfloat16), "mp").astype(jnp.float32)
    hidden = (jax.nn.silu(gate_up[:, 0]) * gate_up[:, 1]).astype(jnp.bfloat16)
    rows_here = hidden
    update = lax.psum_scatter(
        jnp.dot(rows_here, down_weight, preferred_element_type=jnp.float32),
        "ctx",
        scatter_dimension=0,
        tiled=True,
    ).astype(jnp.bfloat16)
    return (stream, update)


lanes = 128
chunk = 512
ahead = 3
columns_at_once = 256
ahead = 3
log2_e = math.log2(math.e)


def swapped(array, bit):
    count = lax.axis_size("mp")
    return lax.ppermute(array, "mp", [(i, i ^ bit) for i in range(count)])


def over_ctx(array):
    return lax.all_to_all(array, "ctx", split_axis=0, concat_axis=0, tiled=True)


def copies_kernel(in_ref, out_ref):
    for i in range(out_ref.shape[0]):
        out_ref[i] = in_ref[...]


def split_stat(value):
    high = value.astype(jnp.bfloat16).astype(jnp.float32)
    return high, value - high


def attend_kernel(pair, part_ref, query_a, query_b, keys, values, chosen, *refs):
    if pair == 0:
        keep_ref, send_ref, key_ref, value_ref = refs[:4]
    else:
        keep_ref, send_ref = refs[:2]
        key_ref, value_ref = keys, values
    score_s, top_s, out_s, lse_s, chosen_ref, sems, chosen_sem = refs[-7:]
    rows, heads, group, depth = query_a.shape
    count = key_ref.shape[1]
    scale = depth ** (-0.5)
    lane = lax.broadcasted_iota(jnp.int32, (rows, lanes), 1)
    listed = chosen_ref.shape[2]
    row_lane = lax.broadcasted_iota(jnp.int32, (rows, listed), 1)
    row_place = lax.broadcasted_iota(jnp.int32, (rows, listed), 0) * (listed // rows)
    chosen_copy = pltpu.make_async_copy(chosen, chosen_ref, chosen_sem)

    def key_copy(h):
        return pltpu.make_async_copy(keys.at[h], key_ref.at[h], sems.at[0, h])

    def value_copy(h):
        return pltpu.make_async_copy(values.at[h], value_ref.at[h], sems.at[1, h])

    def send(copy_of, h):
        if pair == 0:
            if isinstance(h, int):
                copy_of(h).start()
            else:

                @pl.when(h < heads)
                def _():
                    copy_of(h).start()

    def wait(copy_of, h):
        if pair == 0:
            copy_of(h).wait()

    def query_of(h):
        return jnp.concatenate(
            [
                q[:, h].astype(jnp.float32).reshape(rows * group, depth)
                for q in (query_a, query_b)
            ],
            axis=0,
        ).astype(jnp.bfloat16)

    def score(query, h, slot, i, top):
        window = slice(i * chunk, (i + 1) * chunk)
        scores = lax.dot_general(
            query, key_ref[h, window, :], (((1,), (1,)), ((), ())),
            preferred_element_type=jnp.float32,
        )
        score_s[slot, :, window] = scores
        for j in range(chunk // lanes):
            part = scores[:, j * lanes : (j + 1) * lanes]
            top = part if top is None else jnp.maximum(top, part)
        return top

    def spent(h, slot, i, top, mixed):
        window = slice(i * chunk, (i + 1) * chunk)
        probs = jnp.exp2((score_s[slot, :, window] - top) * (scale * log2_e))
        ones = jnp.ones((chunk, lanes), jnp.bfloat16)
        part = jnp.dot(
            probs.astype(jnp.bfloat16),
            jnp.concatenate([value_ref[h, window, :], ones], axis=1),
            preferred_element_type=jnp.float32,
        )
        return part if mixed is None else mixed + part

    def finish(h, slot, top, mixed):
        total = mixed[:, depth:]
        out_s[slot] = mixed[:, :depth] * (1.0 / total)
        lse_s[slot] = top * scale + jnp.log(total)
        member = jnp.where(chosen_ref[h] == part_ref[0], 1.0, 0.0)
        member = jnp.max(member, axis=0, keepdims=True)
        for part, ref in enumerate((keep_ref, send_ref)):
            row = row_place + (lax.rem(part_ref[0], listed // rows) ^ (2 * pair + part))
            held = jnp.where(row_lane == row, member, 0.0)
            bias = jnp.where(jnp.max(held, axis=1, keepdims=True) > 0.5, 0.0, lowest_value)
            stats = jnp.zeros((rows, lanes), jnp.float32)
            for g in range(group):
                window = pl.ds(part * rows * group + g, rows, stride=group)
                ref[h, :, g * depth : (g + 1) * depth] = out_s[slot, window, :].astype(jnp.bfloat16)
                high, low = split_stat(lse_s[slot, window, :] + bias)
                stats = jnp.where(lane == g, high, jnp.where(lane == group + g, low, stats))
            ref[h, :, group * depth :] = stats.astype(jnp.bfloat16)

    def both(h, slot, following, after):
        top = jnp.max(top_s[slot], axis=1, keepdims=True)
        query = None if following is None else query_of(following)
        mixed = later = None
        for i in range(count // chunk):
            mixed = spent(h, slot, i, top, mixed)
            if query is not None:
                later = score(query, following, after, i, later)
        if query is not None:
            top_s[after] = later
        finish(h, slot, top, mixed)

    send(key_copy, 0)
    for h in range(ahead):
        send(value_copy, h)
        send(key_copy, h + 1)
    chosen_copy.start()
    wait(key_copy, 0)
    query, top = query_of(0), None
    for i in range(count // chunk):
        top = score(query, 0, 0, i, top)
    top_s[0] = top
    chosen_copy.wait()

    def turn(h, slot):
        wait(value_copy, h)
        wait(key_copy, h + 1)
        send(value_copy, h + ahead)
        send(key_copy, h + ahead + 1)
        both(h, slot, h + 1, 1 - slot)

    @pl.loop(0, heads // 2 - 1)
    def _(step):
        turn(2 * step, 0)
        turn(2 * step + 1, 1)

    wait(value_copy, heads - 2)
    wait(key_copy, heads - 1)
    both(heads - 2, 0, heads - 1, 1)
    wait(value_copy, heads - 1)
    both(heads - 1, 1, None, 0)


def attend(pair, part, query_a, query_b, keys, values, chosen):
    rows, heads, group, depth = query_a.shape
    count = keys.shape[1]
    width = group * depth + lanes
    shape = jax.ShapeDtypeStruct((heads, rows, width), jnp.bfloat16)
    held = [pltpu.VMEM(a.shape, a.dtype) for a in (keys, values)]
    vmem, hbm = pl.BlockSpec(memory_space=pltpu.VMEM), pl.BlockSpec(memory_space=pltpu.HBM)
    space = pltpu.VMEM if pair else pltpu.HBM
    return pl.pallas_call(
        functools.partial(attend_kernel, pair),
        in_specs=[pl.BlockSpec(memory_space=pltpu.SMEM)]
        + [vmem] * 2
        + [vmem if pair else hbm] * 2
        + [hbm],
        out_specs=[vmem] * (2 if pair else 4),
        out_shape=[shape, shape] + ([] if pair else held),
        scratch_shapes=[
            pltpu.VMEM((2, 2 * rows * group, count), jnp.float32),
            pltpu.VMEM((2, 2 * rows * group, lanes), jnp.float32),
            pltpu.VMEM((2, 2 * rows * group, depth), jnp.float32),
            pltpu.VMEM((2, 2 * rows * group, lanes), jnp.float32),
            pltpu.VMEM(chosen.shape, chosen.dtype),
            pltpu.SemaphoreType.DMA((2, heads)),
            pltpu.SemaphoreType.DMA(()),
        ],
        compiler_params=pltpu.CompilerParams(vmem_limit_bytes=10 << 20),
        cost_estimate=pl.CostEstimate(
            flops=(1 + 4 * pair) * 8 * heads * rows * group * depth * count,
            bytes_accessed=4 * heads * count * depth,
            transcendentals=2 * heads * rows * group * count,
        ),
    )(
        part,
        query_a,
        query_b,
        pltpu.with_memory_space_constraint(keys, space),
        pltpu.with_memory_space_constraint(values, space),
        pltpu.with_memory_space_constraint(chosen, pltpu.HBM),
    )


def merged(parts, group, depth):
    stats = [part[:, group * depth :] for part in parts]
    lses = [s + pltpu.roll(s, lanes - group, 1) for s in stats]
    top = functools.reduce(jnp.maximum, lses)
    weights = [jnp.exp(lse - top) for lse in lses]
    total = functools.reduce(jnp.add, weights)
    inverse = 1.0 / total
    weights = [w * inverse for w in weights]
    if len(parts) == 2:
        weight, (first, second) = weights[0], parts
        values = []
        for g in range(group):
            window = slice(g * depth, (g + 1) * depth)
            values.append(
                second[:, window] + weight[:, g : g + 1] * (first[:, window] - second[:, window])
            )
        return values, top + jnp.log(total)
    values = []
    for g in range(group):
        values.append(
            functools.reduce(
                jnp.add,
                [
                    w[:, g : g + 1] * part[:, g * depth : (g + 1) * depth]
                    for w, part in zip(weights, parts)
                ],
            )
        )
    return values, top + jnp.log(total)


def packed_stat(lse, group):
    lane = lax.broadcasted_iota(jnp.int32, lse.shape, 1)
    high, low = split_stat(lse)
    low = pltpu.roll(low, group, 1)
    return jnp.where(lane < group, high, jnp.where(lane < 2 * group, low, 0.0))


def core_kernel(group, depth, part, keep_ref, recv_ref, *refs):
    out_ref = refs[-1]
    heads, rows, _ = keep_ref.shape
    where = slice(part * rows, (part + 1) * rows)

    for h in range(heads):
        values, lse = merged(
            [keep_ref[h].astype(jnp.float32), recv_ref[h].astype(jnp.float32)], group, depth
        )
        for g in range(group):
            out_ref[h, where, g * depth : (g + 1) * depth] = values[g].astype(jnp.bfloat16)
        out_ref[h, where, group * depth :] = packed_stat(lse, group).astype(jnp.bfloat16)


def core_merge(part, keep, recv, group, depth, into=None):
    heads, rows, width = keep.shape
    more = [] if into is None else [into]
    vmem = pl.BlockSpec(memory_space=pltpu.VMEM)
    return pl.pallas_call(
        functools.partial(core_kernel, group, depth, part),
        in_specs=[vmem] * (2 + len(more)),
        out_specs=vmem,
        out_shape=jax.ShapeDtypeStruct((heads, 2 * rows, width), jnp.bfloat16),
        input_output_aliases={2: 0} if more else {},
        compiler_params=pltpu.CompilerParams(vmem_limit_bytes=8 << 20),
    )(keep, recv, *more)


def ctx_kernel(group, depth, got_ref, out_ref):
    values, lse = merged(
        [got_ref[s].astype(jnp.float32) for s in range(got_ref.shape[0])], group, depth
    )
    for g in range(group):
        out_ref[:, g * depth : (g + 1) * depth] = values[g].astype(jnp.bfloat16)
    out_ref[:, group * depth :] = packed_stat(lse, group).astype(jnp.bfloat16)


def x_kernel(group, depth, own_ref, got_ref, out_ref):
    half = own_ref.shape[0] // 2
    own = own_ref[...].astype(jnp.float32)
    got = got_ref[...].astype(jnp.float32)
    got = jnp.concatenate([got[half:], got[:half]], axis=0)
    values, _ = merged([own, got], group, depth)
    for g in range(group):
        out_ref[:, g * depth : (g + 1) * depth] = values[g].astype(jnp.bfloat16)


def small_call(kernel, shapes, *operands, flops=0):
    return pl.pallas_call(
        kernel,
        out_shape=jax.tree.map(
            lambda shape: jax.ShapeDtypeStruct(shape, jnp.bfloat16),
            shapes,
            is_leaf=lambda x: isinstance(x, tuple),
        ),
        compiler_params=pltpu.CompilerParams(vmem_limit_bytes=8 << 20),
        cost_estimate=pl.CostEstimate(flops=flops, bytes_accessed=1 << 19, transcendentals=0),
    )(*operands)


def scatter_rows(out_ref, first, start, stop, value):
    count, step, _ = out_ref.shape
    for i in range(count):
        where = i if first is None else lax.rem(first + i, count)
        out_ref[where, :, start:stop] = value[i * step : (i + 1) * step].astype(out_ref.dtype)


def stream_kernel(got_ref, residual_ref, copies_ref):
    total = residual_ref[...].astype(jnp.float32)
    partial = got_ref[0].astype(jnp.float32)
    for i in range(1, got_ref.shape[0]):
        partial += got_ref[i].astype(jnp.float32)
    stream = (total + partial).astype(jnp.bfloat16)
    for i in range(copies_ref.shape[0]):
        copies_ref[i] = stream


def product(left, weight_ref, emit):
    width = weight_ref.shape[1]
    for start in range(0, width, columns_at_once):
        stop = min(start + columns_at_once, width)
        emit(
            start,
            stop,
            jnp.dot(left, weight_ref[:, start:stop], preferred_element_type=jnp.float32),
        )


def project_kernel(part_ref, own_ref, got_ref, weight_ref, out_ref):
    rows = out_ref.shape[0] * out_ref.shape[1]
    half = rows // 2
    quarter = rows // 4
    place = lax.rem(part_ref[0], out_ref.shape[1])
    target = lax.broadcasted_iota(jnp.int32, (rows, half), 0)
    source = lax.broadcasted_iota(jnp.int32, (rows, half), 1)
    row = (source % quarter) * 4
    column = 2 * (source // quarter)
    own_order = jnp.where(target == row + (place ^ column), 1.0, 0.0).astype(jnp.bfloat16)
    got_order = jnp.where(target == row + (place ^ (column + 1)), 1.0, 0.0).astype(jnp.bfloat16)
    attended = jnp.dot(own_order, own_ref[...], preferred_element_type=jnp.float32) + jnp.dot(
        got_order, got_ref[...], preferred_element_type=jnp.float32
    )
    product(
        attended.astype(jnp.bfloat16), weight_ref, functools.partial(scatter_rows, out_ref, None)
    )


def tail_of(squares):
    lane = lax.broadcasted_iota(jnp.int32, (squares.shape[0], lanes), 1)
    high, low = split_stat(squares)
    return jnp.where(lane == 0, high, jnp.where(lane == 1, low, 0.0)).astype(jnp.bfloat16)


def half_of(part_ref, count):
    return (part_ref[0] & 1) * (count // 2)


def rows_in_order(part_ref, rows_ref):
    count = rows_ref.shape[0]
    first = half_of(part_ref, count)
    return jnp.concatenate(
        [rows_ref[lax.rem(first + i, count)].astype(jnp.float32) for i in range(count)], axis=0
    )


def half_product(rows, gain_ref, weight_ref, keep_ref, send_ref):
    half = rows.shape[0] // 2
    scaled = (rows * gain_ref[...]).astype(jnp.bfloat16)

    def emit(start, stop, value):
        value = value.astype(jnp.bfloat16)
        keep_ref[:, start:stop] = value[:half]
        send_ref[:, start:stop] = value[half:]

    product(scaled, weight_ref, emit)


def gate_kernel(part_ref, rows_ref, gain_ref, gate_ref, keep_ref, send_ref, stream, sem):
    copy = pltpu.make_async_copy(rows_ref.at[part_ref[0] // rows_ref.shape[1]], stream, sem)
    copy.start()
    rows = rows_in_order(part_ref, rows_ref)
    half = rows.shape[0] // 2
    units = gate_ref.shape[1]
    tail = tail_of(jnp.sum(rows * rows, axis=1, keepdims=True))
    keep_ref[:, units:] = tail[:half]
    send_ref[:, units:] = tail[half:]
    half_product(rows, gain_ref, gate_ref, keep_ref, send_ref)
    copy.wait()


def up_kernel(part_ref, rows_ref, gain_ref, up_ref, keep_ref, send_ref):
    half_product(rows_in_order(part_ref, rows_ref), gain_ref, up_ref, keep_ref, send_ref)


def summed(own_ref, got_ref, start, stop):
    return own_ref[:, start:stop].astype(jnp.float32) + got_ref[:, start:stop].astype(jnp.float32)


def squares_of(own_ref, got_ref):
    start = own_ref.shape[1] - lanes
    tail = summed(own_ref, got_ref, start, start + lanes)
    return tail[:, 0:1] + tail[:, 1:2]


def gate_pair_kernel(own_ref, got_ref, out_ref):
    units = own_ref.shape[1] - lanes
    out_ref[:, :units] = summed(own_ref, got_ref, 0, units).astype(jnp.bfloat16)
    out_ref[:, units:] = tail_of(squares_of(own_ref, got_ref))


def up_pair_kernel(own_ref, got_ref, out_ref):
    out_ref[...] = summed(own_ref, got_ref, 0, own_ref.shape[1]).astype(jnp.bfloat16)


def hidden_kernel(own_gate, got_gate, own_up, got_up, out_ref):
    units = out_ref.shape[1]
    scale = lax.rsqrt(squares_of(own_gate, got_gate) / MODEL_WIDTH + norm_eps)
    gate = summed(own_gate, got_gate, 0, units) * scale
    up = summed(own_up, got_up, 0, units) * scale
    out_ref[...] = (jax.nn.silu(gate) * up).astype(jnp.bfloat16)


def down_kernel(part_ref, own_ref, got_ref, weight_ref, out_ref):
    hidden = jnp.concatenate([own_ref[...], got_ref[...]], axis=0)
    first = half_of(part_ref, out_ref.shape[0])
    product(hidden, weight_ref, functools.partial(scatter_rows, out_ref, first))


def total_kernel(got_ref, out_ref):
    total = got_ref[0].astype(jnp.float32)
    for i in range(1, got_ref.shape[0]):
        total += got_ref[i].astype(jnp.float32)
    out_ref[...] = total.astype(jnp.bfloat16)


def weighed(kernel, shapes, weights, scalar, *operands, copied=None):
    vmem = pl.BlockSpec(memory_space=pltpu.VMEM)
    outs = [jax.ShapeDtypeStruct(shape, jnp.bfloat16) for shape in shapes]
    out_specs, scratch = [vmem] * len(outs), []
    if copied is not None:
        outs.append(jax.ShapeDtypeStruct(copied, jnp.bfloat16))
        out_specs.append(pl.BlockSpec(memory_space=pltpu.HBM))
        scratch.append(pltpu.SemaphoreType.DMA(()))
    return pl.pallas_call(
        kernel,
        in_specs=[pl.BlockSpec(memory_space=pltpu.SMEM)]
        + [vmem] * (len(operands) + len(weights)),
        out_specs=out_specs,
        out_shape=outs,
        scratch_shapes=scratch,
        compiler_params=pltpu.CompilerParams(vmem_limit_bytes=8 << 20),
        cost_estimate=pl.CostEstimate(
            flops=sum(64 * w.size for w in weights),
            bytes_accessed=sum(2 * w.size for w in weights),
            transcendentals=0,
        ),
    )(scalar, *operands, *(pltpu.with_memory_space_constraint(w, pltpu.VMEM) for w in weights))


def per_device_dense(
    query,
    keys,
    values,
    chosen,
    residual,
    output_weight,
    norm_gain,
    gate_weight,
    up_weight,
    down_weight,
):
    _, heads, group, depth = query.shape
    ctx_count = lax.axis_size("ctx")
    mp_count = lax.axis_size("mp")
    own_part = lax.axis_index("ctx") * mp_count + lax.axis_index("mp")
    all_rows = ctx_count * mp_count

    part = jnp.reshape(own_part, (1,))
    chosen = jnp.transpose(chosen, (0, 2, 1))
    copies = small_call(
        copies_kernel, (ctx_count,) + query.shape[1:], query[0], flops=0
    )
    query_own = over_ctx(copies)
    keys, values = keys[0], values[0]
    query_core = swapped(query_own, 1)
    query_x = swapped(query_own, 2)
    keep_a, send_a, keys, values = attend(0, part, query_own, query_core, keys, values, chosen)
    query_x, _ = lax.optimization_barrier((query_x, send_a))
    query_far = swapped(query_x, 1)
    recv_a = swapped(send_a, 1)
    keep_b, send_b = attend(1, part, query_x, query_far, keys, values, chosen)
    recv_b = swapped(send_b, 1)
    on_chip = core_merge(0, keep_a, recv_a, group, depth)
    on_chip = core_merge(1, keep_b, recv_b, group, depth, into=on_chip)
    got = over_ctx(on_chip)
    half_rows = 2 * ctx_count
    width = group * depth
    column = small_call(
        functools.partial(ctx_kernel, group, depth), (half_rows, width + lanes), got
    )
    attended = small_call(
        functools.partial(x_kernel, group, depth), (half_rows, width), column, swapped(column, 2)
    )
    other = swapped(attended, 1)
    width = output_weight.shape[1]
    block = (ctx_count, mp_count, width)
    (projected,) = weighed(
        project_kernel, [block], (output_weight,), part, attended, other
    )
    copies = small_call(stream_kernel, block, over_ctx(projected), residual)
    rows = over_ctx(copies)
    units = gate_weight.shape[1]
    half = all_rows // 2
    gain = norm_gain.reshape(1, -1)
    keep, send, stream = weighed(
        gate_kernel, [(half, units + lanes)] * 2, (gate_weight,), part, rows, gain,
        copied=residual.shape,
    )
    recv = swapped(send, 1)
    keep_up, send_up = weighed(up_kernel, [(half, units)] * 2, (up_weight,), part, rows, gain)
    recv_up = swapped(send_up, 1)
    gate = small_call(gate_pair_kernel, keep.shape, keep, recv)
    got_gate = swapped(gate, 2)
    up = small_call(up_pair_kernel, keep_up.shape, keep_up, recv_up)
    got_up = swapped(up, 2)
    hidden = small_call(hidden_kernel, (half, units), gate, got_gate, up, got_up)
    (update,) = weighed(
        down_kernel, [block], (down_weight,), part, hidden, swapped(hidden, 1)
    )
    update = small_call(total_kernel, residual.shape, over_ctx(update))
    return (stream, update)


def either(*arrays):
    query, mp_count, ctx_count = arrays[0], lax.axis_size("mp"), lax.axis_size("ctx")
    rows, heads, group, depth = query.shape
    dense = (
        rows == 1
        and mp_count == 4
        and heads == ctx_count == group == 8
        and depth == lanes
        and arrays[1].shape[0] == 1
    )
    return (per_device_dense if dense else per_device)(*arrays)


def solution(mesh):
    return jax.shard_map(
        either,
        mesh=mesh,
        in_specs=(
            P(("ctx", "mp"), None, None, None),
            P(("ctx", "mp"), None, None, None),
            P(("ctx", "mp"), None, None, None),
            P(),
            P("ctx", "mp"),
            P("ctx", "mp"),
            P("mp"),
            P("mp", "ctx"),
            P("mp", "ctx"),
            P("ctx", "mp"),
        ),
        out_specs=(P("ctx", "mp"), P("ctx", "mp")),
        check_vma=False,
    )
```
